32 devices in a mesh: seg: 8 (over z, core), bond: 4 (over y, x).
Axes of the slice: x: 2, y: 2, z: 4, core: 2. Of those that a mesh axis runs over, the one named last changes fastest.
Arguments:
- left_env: bfloat16 [8, 1024, 6, 1024], P('seg', 'bond'), may hold values from -0.1875 to 0.1875
- prev_left: bfloat16 [8, 1024, 1024], P('seg'), may hold values from -0.25 to 1.25
- cur_site: bfloat16 [8, 1024, 4, 1024], P('seg', 'bond'), may hold values from -6 to 6
- prev_site: bfloat16 [8, 1024, 4, 1024], P('seg', None, None, 'bond'), may hold values from -6 to 6
- hamiltonian: bfloat16 [8, 6, 6, 4, 4], P('seg'), may hold values from -1.25 to 1.25
- right_env: bfloat16 [8, 1024, 6, 1024], P('seg', 'bond'), may hold values from -0.078125 to 0.078125
- prev_right: bfloat16 [8, 1024, 1024], P('seg'), may hold values from -0.25 to 1.25
Outputs:
- new_site: bfloat16 [8, 1024, 4, 1024], P('seg', 'bond')
- center: float32 [8, 1024, 1024], P('seg', 'bond')
The draws below stay inside these ranges and needn't reach their ends.
All inputs are finite; a program needn't handle non-finite values.
Results may differ from the reference program's by a relative error of at most 0.0054.
Values may be sent and summed in bfloat16 or wider, within the bound.
A program may use at most 128 MiB of HBM per device.

```python
import math
import jax
import jax.numpy as jnp
from jax import lax

CHI = 1024
PHYS = 4
MPOB = 6
SEGMENTS = 8


def dominant_square(key):
    noise = jax.random.normal(key, (SEGMENTS, CHI, CHI), jnp.float32)
    noise = jnp.clip(noise * (0.5 / math.sqrt(CHI)), -0.25, 0.25)
    return noise + jnp.eye(CHI, dtype=jnp.float32)[None]


def draw_prev_left(key, part):
    return dominant_square(jax.random.fold_in(key, 11)).astype(jnp.bfloat16)


def draw_prev_right(key, part):
    return dominant_square(jax.random.fold_in(key, 23)).astype(jnp.bfloat16)


def draw_prev_site(key, part):
    first = jax.random.fold_in(key, 37)
    base = jax.random.normal(first, (SEGMENTS, CHI, PHYS, CHI), jnp.float32)
    return jnp.clip(base, -6.0, 6.0).astype(jnp.bfloat16)


def block_levels(rng, extent, cuts, low, top_value):
    level, own = 1.0, jax.random.fold_in(rng, 6)
    for position, parts in cuts:
        heights = jnp.exp(jax.random.uniform(jax.random.fold_in(own, position), (parts,), jnp.float32, low / len(cuts), top_value / len(cuts)))
        level = level * jnp.repeat(heights, extent[position] // parts).reshape([-1 if axis == position else 1 for axis in range(len(extent))])
    return level


def gaussian(stream_key, dims, deviation, most, split=(), kind=jnp.bfloat16):
    values = jax.random.normal(stream_key, dims, jnp.float32) * deviation
    if len(split) > 0:
        values = block_levels(stream_key, dims, split, -0.22, 0.18) * values
    return jnp.clip(values, min=-most, max=most).astype(kind)


def setup_inputs(seed: int = 0) -> dict:
    streams_of = jax.random.split(jax.random.key(seed), 8)
    return {
        "left_env": gaussian(streams_of[0], (SEGMENTS, CHI, MPOB, CHI), CHI ** -0.5, 0.1875, ((0, 8), (1, 4))),
        "prev_left": draw_prev_left(jax.random.fold_in(streams_of[7], 71), 0),
        "cur_site": gaussian(streams_of[2], (SEGMENTS, CHI, PHYS, CHI), 1.0, 6.0, ((0, 8), (1, 4))),
        "prev_site": draw_prev_site(jax.random.fold_in(streams_of[7], 71), 0),
        "hamiltonian": gaussian(streams_of[4], (SEGMENTS, MPOB, MPOB, PHYS, PHYS), (MPOB * PHYS) ** -0.5, 1.25, ((0, 8),)),
        "right_env": gaussian(streams_of[5], (SEGMENTS, CHI, MPOB, CHI), (MPOB * CHI) ** -0.5, 0.078125, ((0, 8), (1, 4))),
        "prev_right": draw_prev_right(jax.random.fold_in(streams_of[7], 71), 0),
    }


def segment_step(pieces):
    left_now, prev_now, current, previous, hamiltonian, right_block, prev_block = pieces
    projected = jnp.dot(left_now.reshape(CHI * MPOB, CHI).astype(jnp.float32), current.reshape(CHI, PHYS * CHI).astype(jnp.float32), preferred_element_type=jnp.float32).reshape(CHI, MPOB, PHYS, CHI)
    mixture = jnp.einsum('autc,uvst->asvc', projected, hamiltonian.astype(jnp.float32), precision=lax.Precision.HIGHEST).astype(jnp.bfloat16)
    right_flat = jnp.transpose(right_block, (1, 0, 2)).reshape(MPOB * CHI, CHI)
    applied = jnp.dot(mixture.reshape(CHI * PHYS, MPOB * CHI).astype(jnp.float32), right_flat.astype(jnp.float32), preferred_element_type=jnp.float32)
    partial_value = jnp.dot(prev_now.astype(jnp.float32), previous.reshape(CHI, PHYS * CHI).astype(jnp.float32), preferred_element_type=jnp.float32).astype(jnp.bfloat16)
    second = jnp.dot(partial_value.reshape(CHI * PHYS, CHI).astype(jnp.float32), prev_block.astype(jnp.float32), preferred_element_type=jnp.float32)
    target = 2.0 * applied - second
    correlation = jnp.dot(target.T.astype(jnp.float32), target.astype(jnp.float32), precision=lax.Precision.HIGHEST, preferred_element_type=jnp.float32)
    triangle = jnp.linalg.cholesky(correlation)
    solved = jax.scipy.linalg.solve_triangular(triangle, target.T, lower=True)
    norming = math.sqrt(CHI * PHYS)
    new_site = (solved.T * norming).astype(jnp.bfloat16).reshape(CHI, PHYS, CHI)
    center = triangle.T / norming
    return (new_site, center)

def reference(left_env, prev_left, cur_site, prev_site, hamiltonian, right_env, prev_right):
    left_now = jnp.roll(left_env, 1, axis=0)
    prev_now = jnp.roll(prev_left, 1, axis=0)
    new_site, center = lax.map(segment_step, (left_now, prev_now, cur_site, prev_site, hamiltonian, right_env, prev_right))
    return (new_site, center)
```

```python
import functools
import math

import jax
import jax.numpy as jnp
from jax import lax
from jax.experimental import pallas as pl
from jax.experimental.pallas import tpu as pltpu
from jax.sharding import PartitionSpec as P

PHYS = 4
MPOB = 6
BLOCK = 128
STRIP = 256
GROUP = 4
ROWS = 8
WAVES = 2
CHUNKS = 4


def halves(x):
    high = x.astype(jnp.bfloat16)
    return high, (x - high.astype(jnp.float32)).astype(jnp.bfloat16)


def product(a, b, dims):
    a_high, a_low = halves(a)
    b_high, b_low = halves(b)

    def dot(x, y):
        return lax.dot_general(x, y, (dims, ((), ())), preferred_element_type=jnp.float32)

    return dot(a_high, b_high) + (dot(a_high, b_low) + dot(a_low, b_high))


def reduce_kernel(n, own_ref, out_ref, parts, total, send_sem, recv_sem, send_back, recv_back):
    me = lax.axis_index("bond")
    barrier = pltpu.get_barrier_semaphore()
    peers = [lax.rem(me + d, n) for d in range(1, n)]
    for peer in peers:
        pl.semaphore_signal(barrier, inc=1, device_id={"bond": peer})
    pl.semaphore_wait(barrier, n - 1)
    width = own_ref.shape[2] // WAVES
    waves = [pl.ds(w * width, width) for w in range(WAVES)]
    outward, back = [], []
    for w, lanes in enumerate(waves):
        outward.append([
            pltpu.make_async_remote_copy(
                src_ref=own_ref.at[peer, :, lanes],
                dst_ref=parts.at[d, :, lanes],
                send_sem=send_sem.at[w, d],
                recv_sem=recv_sem.at[w, d],
                device_id={"bond": peer},
            )
            for d, peer in enumerate(peers)
        ])
        for copy in outward[w]:
            copy.start()
    for w, lanes in enumerate(waves):
        for copy in outward[w]:
            copy.wait_recv()
        value = own_ref[me, :, lanes]
        for d in range(n - 1):
            value = value + parts[d, :, lanes]
        total[me, :, lanes] = value
        back.append([
            pltpu.make_async_remote_copy(
                src_ref=total.at[me, :, lanes],
                dst_ref=total.at[me, :, lanes],
                send_sem=send_back.at[w, d],
                recv_sem=recv_back.at[w, d],
                device_id={"bond": peer},
            )
            for d, peer in enumerate(peers)
        ])
        for copy in back[w]:
            copy.start()
    for w, lanes in enumerate(waves):
        for copy in back[w]:
            copy.wait_recv()
        out_ref[:, :, lanes] = total[:, :, lanes]
    for copies in outward + back:
        for copy in copies:
            copy.wait_send()


def summed(packed):
    n = lax.axis_size("bond")
    rows, width = packed.shape
    shape = (n, rows // n, width)
    return pl.pallas_call(
        functools.partial(reduce_kernel, n),
        out_shape=jax.ShapeDtypeStruct(shape, jnp.float32),
        in_specs=[pl.BlockSpec(memory_space=pltpu.VMEM)],
        out_specs=pl.BlockSpec(memory_space=pltpu.VMEM),
        scratch_shapes=[
            pltpu.VMEM((n - 1,) + shape[1:], jnp.float32),
            pltpu.VMEM(shape, jnp.float32),
        ]
        + [pltpu.SemaphoreType.DMA((WAVES, n - 1))] * 4,
        compiler_params=pltpu.CompilerParams(
            collective_id=0, has_side_effects=True, vmem_limit_bytes=24 * 2**20
        ),
        name="summed",
    )(packed.reshape(shape)).reshape(rows, width)


def eliminate(block, rows_ref):
    size = block.shape[0]
    lane = lax.broadcasted_iota(jnp.int32, (1, size), 1)
    rest = block
    top = 0
    for first in range(0, size, GROUP):
        start = first // 8 * 8
        rest, top = rest[start - top :], start
        at = first - top
        rows = [rest[at + q : at + q + 1, :] for q in range(GROUP)]
        columns = [
            jnp.broadcast_to(rest[:, first + q : first + q + 1], rest.shape) for q in range(GROUP)
        ]
        small = [[columns[r][at + p : at + p + 1, :] for r in range(GROUP)] for p in range(GROUP)]
        change = None
        for q in range(GROUP):
            rows_ref[pl.ds(first + q, 1), :] = rows[q]
            inverse = 1.0 / small[q][q]
            lead = jnp.where(lane == first + q, 1.0, rows[q])
            for p in range(q + 1, GROUP):
                factor = small[q][p] * inverse
                for r in range(p, GROUP):
                    small[p][r] = small[p][r] - factor * small[q][r]
                rows[p] = jnp.where(lane == first + q, 0.0, rows[p]) - factor * lead
                columns[p] = columns[p] - factor * columns[q]
            if first + GROUP < size:
                lead = jnp.where((lane > first + q) & (lane < first + GROUP), 0.0, lead)
                term = columns[q] * (inverse * lead)
                change = term if change is None else change + term
        if first + GROUP < size:
            rest = jnp.where((lane >= first) & (lane < first + GROUP), 0.0, rest) - change


def factor_kernel(packed_ref, upper_ref, inverse_ref, work, panel, rows_ref):
    size = work.shape[0]
    blocks = size // BLOCK
    offset = 0
    for start in range(0, size, STRIP):
        width = size - start
        work[start : start + STRIP, start:] = packed_ref[:, offset : offset + width]
        if start > 0:
            work[start : start + STRIP, :start] = jnp.zeros((STRIP, start), jnp.float32)
        offset += width
    row = lax.broadcasted_iota(jnp.int32, (BLOCK, BLOCK), 0)
    column = lax.broadcasted_iota(jnp.int32, (BLOCK, BLOCK), 1)
    full_column = lax.broadcasted_iota(jnp.int32, (BLOCK, size), 1)

    def step(k, carry):
        own = pl.ds(pl.multiple_of(k * BLOCK, BLOCK), BLOCK)
        eliminate(work[own, own], rows_ref)
        done = rows_ref[...]
        pivots = jnp.sum(jnp.where(row == column, done, 0.0), axis=1, keepdims=True)
        scale = lax.rsqrt(pivots)
        scaled = done * scale
        upper = jnp.where(row <= column, scaled, 0.0)
        inverse = jnp.where(row > column, scaled, jnp.where(row == column, scale, 0.0))
        panel[...] = product(inverse, work[own, :], ((1,), (0,)))
        whole = panel[...]
        upper_ref[own, :] = jnp.where(full_column >= (k + 1) * BLOCK, whole, 0.0)
        inverse_ref[own, :] = jnp.where(full_column < k * BLOCK, whole, 0.0)
        upper_ref[own, own] = upper
        inverse_ref[own, own] = inverse
        panel[:, own] = inverse
        right = panel[...]

        def update(i, carry):
            other = pl.ds(pl.multiple_of(i * BLOCK, BLOCK), BLOCK)
            work[other, own] = jnp.zeros((BLOCK, BLOCK), jnp.float32)
            work[other, :] -= product(panel[:, other], right, ((0,), (0,)))
            return carry

        lax.fori_loop(k + 1, blocks, update, 0)
        return carry

    lax.fori_loop(0, blocks, step, 0)


def factorize(packed, size):
    whole = jax.ShapeDtypeStruct((size, size), jnp.float32)
    return pl.pallas_call(
        factor_kernel,
        out_shape=(whole, whole),
        in_specs=[pl.BlockSpec(memory_space=pltpu.VMEM)],
        out_specs=[pl.BlockSpec(memory_space=pltpu.VMEM)] * 2,
        scratch_shapes=[
            pltpu.VMEM((size, size), jnp.float32),
            pltpu.VMEM((BLOCK, size), jnp.float32),
            pltpu.VMEM((BLOCK, BLOCK), jnp.float32),
        ],
        compiler_params=pltpu.CompilerParams(vmem_limit_bytes=40 * 2**20),
        name="factorize",
    )(packed)


def mix_kernel(parts, spread_ref, projected_ref, mixture_ref):
    width = projected_ref.shape[2] // PHYS
    spread = spread_ref[...]
    results = []
    for first in range(0, 2 * ROWS, ROWS):
        stack = jnp.concatenate(
            [
                projected_ref[u, first : first + ROWS, t * width : (t + 1) * width]
                for u in range(MPOB)
                for t in range(PHYS)
            ],
            axis=0,
        )
        results.append(
            jnp.dot(spread, stack.astype(jnp.bfloat16), preferred_element_type=jnp.float32)
        )
    for v in range(MPOB):
        for s in range(PHYS):
            at = (v * PHYS + s) * ROWS
            both = jnp.concatenate([one[at : at + ROWS, :] for one in results], axis=0)
            both = both.astype(jnp.bfloat16)
            part = width // parts
            for p in range(parts):
                start = (p * MPOB + v) * part
                mixture_ref[s, :, start : start + part] = both[:, p * part : (p + 1) * part]


def mixed(projected, coupling, parts):
    own_rows, width = projected.shape[1], projected.shape[2] // PHYS
    side = MPOB * PHYS * ROWS
    diagonal = jnp.eye(ROWS, dtype=coupling.dtype)
    turned = jnp.transpose(coupling, (1, 2, 0, 3))
    spread = turned[:, :, None, :, :, None] * diagonal[None, None, :, None, None, :]
    return pl.pallas_call(
        functools.partial(mix_kernel, parts),
        grid=(own_rows // (2 * ROWS),),
        out_shape=jax.ShapeDtypeStruct((PHYS, own_rows, MPOB * width), jnp.bfloat16),
        in_specs=[
            pl.BlockSpec((side, side), lambda i: (0, 0)),
            pl.BlockSpec((MPOB, 2 * ROWS, PHYS * width), lambda i: (0, i, 0)),
        ],
        out_specs=pl.BlockSpec((PHYS, 2 * ROWS, MPOB * width), lambda i: (0, i, 0)),
        compiler_params=pltpu.CompilerParams(vmem_limit_bytes=40 * 2**20),
        cost_estimate=pl.CostEstimate(
            flops=2 * side * MPOB * PHYS * own_rows * width,
            bytes_accessed=6 * MPOB * PHYS * own_rows * width,
            transcendentals=0,
        ),
        name="mixed",
    )(spread.reshape(side, side), projected)


def minor_size(n):
    return max(d for d in range(1, n + 1) if n % d == 0 and d * d <= n)


def sent(block, hop, major, minor):
    segments, n = lax.axis_size("seg"), lax.axis_size("bond")
    q = minor_size(n)
    p = n // q
    route = []
    for k in range(segments):
        for m in range(p):
            for r in range(q):
                source = (k - hop) % segments * n + (m + major) % p * q + (r + minor) % q
                route.append((source, k * n + m * q + r))
    return lax.ppermute(block, ("seg", "bond"), route)


def blocks_of(array, indices, size, axis):
    pieces = [lax.dynamic_slice_in_dim(array, j * size, size, axis) for j in indices]
    return pieces[0] if len(pieces) == 1 else jnp.concatenate(pieces, axis=axis)


def shards(left_env, prev_left, cur_site, prev_site, hamiltonian, right_env, prev_right):
    n = lax.axis_size("bond")
    q = minor_size(n)
    p = n // q
    index = lax.axis_index("bond")
    major, minor = index // q, index % q
    own = left_env.shape[1]
    bond = left_env.shape[3]
    wide, tall = q * own, p * own

    def at(m, r):
        return lax.rem(m, p) * q + lax.rem(r, q)

    current = jnp.zeros((bond, PHYS * wide), jnp.bfloat16)
    for dm in range(p):
        for dr in range(q):
            m, r = major + p - dm, minor + q - dr
            columns = [at(m, r + d) for d in range(q)]
            block = blocks_of(cur_site[0], columns, own, 2).reshape(own, PHYS * wide)
            if dm or dr:
                block = sent(block, 0, dm, dr)
            current = lax.dynamic_update_slice_in_dim(
                current, block, at(major + dm, minor + dr) * own, 0
            )
    left_own = jnp.transpose(left_env[0], (1, 0, 2))
    left = jnp.concatenate([sent(left_own, 1, d, 0) for d in range(p)], axis=1)
    prev_now = sent(prev_left[0], 1, 0, 0)
    right_own = jnp.transpose(right_env[0], (1, 0, 2))
    right = [right_own] + [sent(right_own, 0, 0, d) for d in range(1, q)]
    parts = q if own % 128 == 0 else 1
    right = jnp.concatenate(right, axis=0 if parts == q else 1)

    partial_value = jnp.einsum(
        "ab,bsc->sac", prev_now, prev_site[0], preferred_element_type=jnp.float32
    ).astype(jnp.bfloat16)
    pieces = []
    for d in range(q):
        rows = [at(major + e, minor + q - d) for e in range(p)]
        piece = blocks_of(partial_value, rows, own, 1)
        pieces.append(sent(piece, 0, 0, d) if d else piece)
    partial_value = jnp.concatenate(pieces, axis=2).reshape(PHYS * tall, wide)
    prev_rows = blocks_of(prev_right[0], [at(major, minor + d) for d in range(q)], own, 0)

    projected = jnp.dot(
        left.reshape(MPOB * tall, bond), current, preferred_element_type=jnp.float32
    ).reshape(MPOB, tall, PHYS * wide)
    mixture = mixed(projected, hamiltonian[0], parts).reshape(PHYS * tall, MPOB * wide)
    right = right.reshape(MPOB * wide, bond)
    columns = bond // CHUNKS
    target = []
    for j in range(CHUNKS):
        lanes = slice(j * columns, (j + 1) * columns)
        applied = jnp.dot(mixture, right[:, lanes], preferred_element_type=jnp.float32)
        second = jnp.dot(partial_value, prev_rows[:, lanes], preferred_element_type=jnp.float32)
        both = (2.0 * applied - second).reshape(PHYS, p, own, columns)
        total = both[:, 0]
        for d in range(1, p):
            other = both[:, d].astype(jnp.bfloat16)
            total = total + sent(other, 0, p - d, 0).astype(jnp.float32)
        target.append(total.reshape(PHYS * own, columns))
    target = jnp.concatenate(target, axis=1)
    own_rows, bond_width = own, bond
    strips = [
        jnp.dot(
            target[:, start : start + STRIP].T,
            target[:, start:],
            precision=lax.Precision.HIGH,
            preferred_element_type=jnp.float32,
        )
        for start in range(0, bond_width, STRIP)
    ]
    packed = summed(jnp.concatenate(strips, axis=1))
    upper, inverse = factorize(packed, bond_width)
    norming = math.sqrt(bond_width * PHYS)
    solved = lax.dot_general(
        target,
        inverse,
        (((1,), (1,)), ((), ())),
        precision=lax.Precision.HIGH,
        preferred_element_type=jnp.float32,
    )
    new_site = (solved * norming).astype(jnp.bfloat16).reshape(PHYS, own_rows, bond_width)
    new_site = jnp.transpose(new_site, (1, 0, 2))[None]
    offset = lax.axis_index("bond") * own_rows
    center = lax.dynamic_slice_in_dim(upper, offset, own_rows, 0) / norming
    return (new_site, center[None])


def solution(mesh):
    return jax.shard_map(
        shards,
        mesh=mesh,
        in_specs=(
            P("seg", "bond", None, None),
            P("seg", None, None),
            P("seg", "bond", None, None),
            P("seg", None, None, "bond"),
            P("seg", None, None, None, None),
            P("seg", "bond", None, None),
            P("seg", None, None),
        ),
        out_specs=(P("seg", "bond", None, None), P("seg", "bond", None)),
        check_vma=False,
    )
```

```python
import functools
import math

import jax
import jax.numpy as jnp
from jax import lax
from jax.experimental import pallas as pl
from jax.experimental.pallas import tpu as pltpu
from jax.sharding import PartitionSpec as P

PHYS = 4
MPOB = 6
BLOCK = 128
STRIP = 256
GROUP = 4
ROWS = 8
WAVES = 2
EDGES = 4
LEFT_ROWS = 64


def halves(x):
    high = x.astype(jnp.bfloat16)
    return high, (x - high.astype(jnp.float32)).astype(jnp.bfloat16)


def product(a, b, dims):
    a_high, a_low = halves(a)
    b_high, b_low = halves(b)

    def dot(x, y):
        return lax.dot_general(x, y, (dims, ((), ())), preferred_element_type=jnp.float32)

    return dot(a_high, b_high) + (dot(a_high, b_low) + dot(a_low, b_high))


def reduce_kernel(n, own_ref, out_ref, parts, total, send_sem, recv_sem, send_back, recv_back):
    me = lax.axis_index("bond")
    barrier = pltpu.get_barrier_semaphore()
    peers = [lax.rem(me + d, n) for d in range(1, n)]
    for peer in peers:
        pl.semaphore_signal(barrier, inc=1, device_id={"bond": peer})
    pl.semaphore_wait(barrier, n - 1)
    width = own_ref.shape[2] // WAVES
    waves = [pl.ds(w * width, width) for w in range(WAVES)]
    outward, back = [], []
    for w, lanes in enumerate(waves):
        outward.append([
            pltpu.make_async_remote_copy(
                src_ref=own_ref.at[peer, :, lanes],
                dst_ref=parts.at[d, :, lanes],
                send_sem=send_sem.at[w, d],
                recv_sem=recv_sem.at[w, d],
                device_id={"bond": peer},
            )
            for d, peer in enumerate(peers)
        ])
        for copy in outward[w]:
            copy.start()
    for w, lanes in enumerate(waves):
        for copy in outward[w]:
            copy.wait_recv()
        value = own_ref[me, :, lanes]
        for d in range(n - 1):
            value = value + parts[d, :, lanes]
        total[me, :, lanes] = value
        back.append([
            pltpu.make_async_remote_copy(
                src_ref=total.at[me, :, lanes],
                dst_ref=total.at[me, :, lanes],
                send_sem=send_back.at[w, d],
                recv_sem=recv_back.at[w, d],
                device_id={"bond": peer},
            )
            for d, peer in enumerate(peers)
        ])
        for copy in back[w]:
            copy.start()
    for w, lanes in enumerate(waves):
        for copy in back[w]:
            copy.wait_recv()
        out_ref[:, :, lanes] = total[:, :, lanes]
    for copies in outward + back:
        for copy in copies:
            copy.wait_send()


def summed(packed):
    n = lax.axis_size("bond")
    rows, width = packed.shape
    shape = (n, rows // n, width)
    return pl.pallas_call(
        functools.partial(reduce_kernel, n),
        out_shape=jax.ShapeDtypeStruct(shape, jnp.float32),
        in_specs=[pl.BlockSpec(memory_space=pltpu.VMEM)],
        out_specs=pl.BlockSpec(memory_space=pltpu.VMEM),
        scratch_shapes=[
            pltpu.VMEM((n - 1,) + shape[1:], jnp.float32),
            pltpu.VMEM(shape, jnp.float32),
        ]
        + [pltpu.SemaphoreType.DMA((WAVES, n - 1))] * 4,
        compiler_params=pltpu.CompilerParams(
            collective_id=0, has_side_effects=True, vmem_limit_bytes=24 * 2**20
        ),
        name="summed",
    )(packed.reshape(shape)).reshape(rows, width)


def eliminate(block, rows_ref):
    size = block.shape[0]
    lane = lax.broadcasted_iota(jnp.int32, (1, size), 1)
    rest = block
    top = 0
    for first in range(0, size, GROUP):
        start = first // 8 * 8
        rest, top = rest[start - top :], start
        at = first - top
        rows = [rest[at + q : at + q + 1, :] for q in range(GROUP)]
        columns = [
            jnp.broadcast_to(rest[:, first + q : first + q + 1], rest.shape) for q in range(GROUP)
        ]
        small = [[columns[r][at + p : at + p + 1, :] for r in range(GROUP)] for p in range(GROUP)]
        change = None
        for q in range(GROUP):
            rows_ref[pl.ds(first + q, 1), :] = rows[q]
            inverse = 1.0 / small[q][q]
            lead = jnp.where(lane == first + q, 1.0, rows[q])
            for p in range(q + 1, GROUP):
                factor = small[q][p] * inverse
                for r in range(p, GROUP):
                    small[p][r] = small[p][r] - factor * small[q][r]
                rows[p] = jnp.where(lane == first + q, 0.0, rows[p]) - factor * lead
                columns[p] = columns[p] - factor * columns[q]
            if first + GROUP < size:
                lead = jnp.where((lane > first + q) & (lane < first + GROUP), 0.0, lead)
                term = columns[q] * (inverse * lead)
                change = term if change is None else change + term
        if first + GROUP < size:
            rest = jnp.where((lane >= first) & (lane < first + GROUP), 0.0, rest) - change


def factor_kernel(packed_ref, upper_ref, inverse_ref, work, panel, rows_ref):
    size = work.shape[0]
    blocks = size // BLOCK
    offset = 0
    for start in range(0, size, STRIP):
        width = size - start
        work[start : start + STRIP, start:] = packed_ref[:, offset : offset + width]
        if start > 0:
            work[start : start + STRIP, :start] = jnp.zeros((STRIP, start), jnp.float32)
        offset += width
    row = lax.broadcasted_iota(jnp.int32, (BLOCK, BLOCK), 0)
    column = lax.broadcasted_iota(jnp.int32, (BLOCK, BLOCK), 1)
    full_column = lax.broadcasted_iota(jnp.int32, (BLOCK, size), 1)

    def step(k, carry):
        own = pl.ds(pl.multiple_of(k * BLOCK, BLOCK), BLOCK)
        eliminate(work[own, own], rows_ref)
        done = rows_ref[...]
        pivots = jnp.sum(jnp.where(row == column, done, 0.0), axis=1, keepdims=True)
        scale = lax.rsqrt(pivots)
        scaled = done * scale
        upper = jnp.where(row <= column, scaled, 0.0)
        inverse = jnp.where(row > column, scaled, jnp.where(row == column, scale, 0.0))
        panel[...] = product(inverse, work[own, :], ((1,), (0,)))
        whole = panel[...]
        upper_ref[own, :] = jnp.where(full_column >= (k + 1) * BLOCK, whole, 0.0)
        inverse_ref[own, :] = jnp.where(full_column < k * BLOCK, whole, 0.0)
        upper_ref[own, own] = upper
        inverse_ref[own, own] = inverse
        panel[:, own] = inverse
        right = panel[...]

        def update(i, carry):
            other = pl.ds(pl.multiple_of(i * BLOCK, BLOCK), BLOCK)
            work[other, own] = jnp.zeros((BLOCK, BLOCK), jnp.float32)
            work[other, :] -= product(panel[:, other], right, ((0,), (0,)))
            return carry

        lax.fori_loop(k + 1, blocks, update, 0)
        return carry

    lax.fori_loop(0, blocks, step, 0)


def factorize(packed, size):
    whole = jax.ShapeDtypeStruct((size, size), jnp.float32)
    return pl.pallas_call(
        factor_kernel,
        out_shape=(whole, whole),
        in_specs=[pl.BlockSpec(memory_space=pltpu.VMEM)],
        out_specs=[pl.BlockSpec(memory_space=pltpu.VMEM)] * 2,
        scratch_shapes=[
            pltpu.VMEM((size, size), jnp.float32),
            pltpu.VMEM((BLOCK, size), jnp.float32),
            pltpu.VMEM((BLOCK, BLOCK), jnp.float32),
        ],
        compiler_params=pltpu.CompilerParams(vmem_limit_bytes=40 * 2**20),
        name="factorize",
    )(packed)


def minor_size(n):
    return max(d for d in range(1, n + 1) if n % d == 0 and d * d <= n)


def edge_spans(width):
    unit = width // EDGES
    return [(j * unit, unit) for j in range(EDGES)]


def front_kernel(
    segments, n, left_ref, prev_left_ref, current_ref, right_ref,
    prev_site_ref, prev_right_ref, spread_ref, target_ref,
    left, current, right, prev_left, partial_out, partial_in, projected, mixture, outgoing, incoming,
    left_send, left_recv, prev_send, prev_recv, major_send, major_recv, minor_send, minor_recv,
    relay_send, relay_recv, right_send, right_recv, partial_send, partial_recv,
    target_send, target_recv, local_sem,
):
    q = minor_size(n)
    p = n // q
    seg, index = lax.axis_index("seg"), lax.axis_index("bond")
    major, minor = index // q, lax.rem(index, q)
    own, bond = left_ref.shape[1], left_ref.shape[2]
    wide, tall = q * own, p * own
    half = own // 2
    rows = projected.shape[1] // MPOB
    chunks = own // rows
    spans = edge_spans(bond)

    def device(hop, dm, dr):
        m, r = lax.rem(major + dm, p), lax.rem(minor + dr, q)
        return {"seg": lax.rem(seg + hop, segments), "bond": m * q + r}

    def copy(src, dst, send, recv, to):
        return pltpu.make_async_remote_copy(
            src_ref=src, dst_ref=dst, send_sem=send, recv_sem=recv, device_id=to
        )

    def slot(d):
        return lax.rem(major + d, p)

    def place(dm, dr):
        return (lax.rem(major + dm, p) * q + lax.rem(minor + dr, q)) * own

    barrier = pltpu.get_barrier_semaphore()
    peers = [device(0, d, 0) for d in range(1, p)] + [device(0, 0, d) for d in range(1, q)]
    peers += [device(hop, d, 0) for d in range(p) for hop in (1, segments - 1)]
    for peer in peers:
        pl.semaphore_signal(barrier, inc=1, device_id=peer)
    pl.semaphore_wait(barrier, len(peers))

    def left_flow(d, j, slot_index, back):
        span = pl.ds(pl.multiple_of(j * rows, rows), rows)
        return copy(
            left_ref.at[:, span, :],
            left.at[slot_index, :, span, :],
            left_send.at[d, j],
            left_recv.at[back, j],
            device(1, d, 0),
        )

    def left_out(d, j):
        return left_flow(d, j, major, (p - d) % p)

    def left_in(d, j):
        return left_flow(d, j, slot(d), d)

    def current_rows(dm, dr, h):
        return pl.ds(pl.multiple_of(place(dm, dr) + h * half, half), half)

    def source_columns(dm):
        return pl.ds(pl.multiple_of(slot(dm) * wide, wide), wide)

    prev_flow = copy(prev_left_ref, prev_left, prev_send.at[0], prev_recv.at[0], device(1, 0, 0))
    prev_flow.start()
    sends = [prev_flow]
    for h in range(2):
        source = pl.ds(h * half, half)
        for d in range(1, p):
            flow = copy(
                current_ref.at[:, source, source_columns(d)],
                current.at[:, current_rows(0, 0, h), :],
                major_send.at[d, h],
                major_recv.at[p - d, h],
                device(0, d, 0),
            )
            flow.start()
            sends.append(flow)
        for d in range(1, q):
            flow = copy(
                current_ref.at[:, source, source_columns(0)],
                current.at[:, current_rows(0, 0, h), :],
                minor_send.at[d, h],
                minor_recv.at[q - d, h],
                device(0, 0, d),
            )
            flow.start()
            sends.append(flow)
    for j in range(chunks):
        for d in range(p):
            flow = left_out(d, j)
            flow.start()
            sends.append(flow)
    locals_ = [
        pltpu.make_async_copy(
            current_ref.at[:, :, source_columns(0)],
            current.at[:, pl.ds(pl.multiple_of(place(0, 0), own), own), :],
            local_sem.at[0],
        ),
        pltpu.make_async_copy(
            right_ref, right.at[:, pl.ds(pl.multiple_of(minor * own, own), own), :], local_sem.at[1]
        ),
    ]
    for one in locals_:
        one.start()

    for h in range(2):
        for dm in range(1, p):
            landed = current.at[:, current_rows(dm, 0, h), :]
            copy(
                landed, landed, major_send.at[dm, h], major_recv.at[dm, h], device(0, dm, 0)
            ).wait_recv()
            for d in range(1, q):
                flow = copy(
                    landed, landed, relay_send.at[dm, d, h], relay_recv.at[dm, q - d, h],
                    device(0, 0, d),
                )
                flow.start()
                sends.append(flow)

    prev_flow.wait_recv()

    def contract(d, out):
        def body(step, carry):
            m, s = step // PHYS, lax.rem(step, PHYS)
            top = (m * q + lax.rem(minor + d, q)) * own
            value = jnp.dot(
                prev_left[pl.ds(pl.multiple_of(top, own), own), :],
                prev_site_ref[s],
                preferred_element_type=jnp.float32,
            )
            out[s, pl.ds(pl.multiple_of(m * own, own), own), :] = value.astype(jnp.bfloat16)
            return carry

        lax.fori_loop(0, p * PHYS, body, 0)

    for d in range(1, q):
        contract(d, partial_out.at[d - 1])
        flow = copy(
            partial_out.at[d - 1], partial_in.at[minor], partial_send.at[d],
            partial_recv.at[q - d], device(0, 0, d),
        )
        flow.start()
        sends.append(flow)

    def right_flow(d, j, row, back):
        first, width = spans[j]
        lanes = pl.ds(first, width)
        return copy(
            right_ref.at[:, :, lanes],
            right.at[:, pl.ds(pl.multiple_of(row * own, own), own), lanes],
            right_send.at[d, j],
            right_recv.at[back, j],
            device(0, 0, d),
        )

    for j in range(len(spans)):
        for d in range(1, q):
            flow = right_flow(d, j, minor, q - d)
            flow.start()
            sends.append(flow)
    contract(0, partial_in.at[minor])

    for h in range(2):
        for d in range(1, q):
            landed = current.at[:, current_rows(0, d, h), :]
            copy(
                landed, landed, minor_send.at[d, h], minor_recv.at[d, h], device(0, 0, d)
            ).wait_recv()
            for dm in range(1, p):
                landed = current.at[:, current_rows(dm, d, h), :]
                copy(
                    landed, landed, relay_send.at[dm, d, h], relay_recv.at[dm, d, h],
                    device(0, 0, d),
                ).wait_recv()
    for one in locals_:
        one.wait()

    def mix(step, carry):
        j, order = step // p, lax.rem(step, p)
        where = lax.rem(major + order, p)
        left_in(order, j).wait_recv()
        span = pl.ds(pl.multiple_of(j * rows, rows), rows)
        block = left[where, :, span, :].reshape(MPOB * rows, bond)

        def project(t, carry):
            projected[t] = jnp.dot(block, current[t], preferred_element_type=jnp.float32)
            return carry

        lax.fori_loop(0, PHYS, project, 0)

        def spread(g, carry):
            results = []
            for first in range(2):
                at = g * 2 * ROWS + first * ROWS
                stack = jnp.concatenate(
                    [
                        projected[t, pl.ds(pl.multiple_of(u * rows + at, ROWS), ROWS), :]
                        for u in range(MPOB)
                        for t in range(PHYS)
                    ],
                    axis=0,
                )
                results.append(
                    jnp.dot(
                        spread_ref[...],
                        stack.astype(jnp.bfloat16),
                        preferred_element_type=jnp.float32,
                    )
                )
            top = pl.multiple_of(where * own + j * rows + g * 2 * ROWS, 2 * ROWS)
            for v in range(MPOB):
                for s in range(PHYS):
                    first = (v * PHYS + s) * ROWS
                    both = jnp.concatenate([one[first : first + ROWS] for one in results], axis=0)
                    mixture[s, pl.ds(top, 2 * ROWS), v * wide : (v + 1) * wide] = both.astype(
                        jnp.bfloat16
                    )
            return carry

        lax.fori_loop(0, rows // (2 * ROWS), spread, 0)
        return carry

    lax.fori_loop(0, chunks * p, mix, 0)

    for d in range(1, q):
        landed = partial_in.at[lax.rem(minor + d, q)]
        copy(
            landed, landed, partial_send.at[d], partial_recv.at[d], device(0, 0, d)
        ).wait_recv()

    def products(d, j, write):
        first, width = spans[j]

        def body(s, carry):
            top = pl.ds(pl.multiple_of(slot(d) * own, own), own)
            lanes = slice(first, first + width)
            value = 2.0 * jnp.dot(
                mixture[s, top, :],
                right[:, :, lanes].reshape(MPOB * wide, width),
                preferred_element_type=jnp.float32,
            )
            for r in range(q):
                prev_rows = pl.ds(pl.multiple_of(major * wide + r * own, own), own)
                value = value - jnp.dot(
                    partial_in[r, s, top, :],
                    prev_right_ref[prev_rows, lanes],
                    preferred_element_type=jnp.float32,
                )
            write(s, lanes, value)
            return carry

        lax.fori_loop(0, PHYS, body, 0)

    def target_flow(d, j, back):
        first, width = spans[j]
        lanes = pl.ds(first, width)
        return copy(
            outgoing.at[d - 1, :, :, lanes], incoming.at[back - 1, :, :, lanes],
            target_send.at[d, j], target_recv.at[back, j], device(0, d, 0),
        )

    for j in range(len(spans)):
        for d in range(1, q):
            right_flow(d, j, lax.rem(minor + d, q), d).wait_recv()
        for d in range(1, p):

            def keep(s, lanes, value):
                outgoing[d - 1, s, :, lanes] = value.astype(jnp.bfloat16)

            products(d, j, keep)
            flow = target_flow(d, j, p - d)
            flow.start()
            sends.append(flow)

        def own_part(s, lanes, value):
            target_ref[s, :, lanes] = value

        products(0, j, own_part)
    for j, (first, width) in enumerate(spans):
        for d in range(1, p):
            target_flow(d, j, d).wait_recv()
            lanes = slice(first, first + width)

            def add(s, carry):
                target_ref[s, :, lanes] += incoming[d - 1, s, :, lanes].astype(jnp.float32)
                return carry

            lax.fori_loop(0, PHYS, add, 0)
    for flow in sends:
        flow.wait_send()


def front(left, prev_left, current, right, prev_site, prev_right, coupling):
    n, segments = lax.axis_size("bond"), lax.axis_size("seg")
    q = minor_size(n)
    p = n // q
    own, bond = left.shape[1], left.shape[2]
    wide, tall = q * own, p * own
    rows = min(LEFT_ROWS, own)
    edges = len(edge_spans(bond))
    side = MPOB * PHYS * ROWS
    diagonal = jnp.eye(ROWS, dtype=coupling.dtype)
    turned = jnp.transpose(coupling, (1, 2, 0, 3))
    spread = turned[:, :, None, :, :, None] * diagonal[None, None, :, None, None, :]
    low, full = jnp.bfloat16, jnp.float32
    whole = pl.BlockSpec(memory_space=pltpu.VMEM)
    there = pl.BlockSpec(memory_space=pl.ANY)

    def pairs(*shape):
        return [pltpu.SemaphoreType.DMA(shape)] * 2

    return pl.pallas_call(
        functools.partial(front_kernel, segments, n),
        out_shape=jax.ShapeDtypeStruct((PHYS, own, bond), full),
        in_specs=[there] * 4 + [whole] * 3,
        out_specs=whole,
        scratch_shapes=[
            pltpu.VMEM((p, MPOB, own, bond), low),
            pltpu.VMEM((PHYS, bond, wide), low),
            pltpu.VMEM((MPOB, wide, bond), low),
            pltpu.VMEM((bond, bond), low),
            pltpu.VMEM((max(q - 1, 1), PHYS, tall, own), low),
            pltpu.VMEM((q, PHYS, tall, own), low),
            pltpu.VMEM((PHYS, MPOB * rows, wide), full),
            pltpu.VMEM((PHYS, tall, MPOB * wide), low),
            pltpu.VMEM((max(p - 1, 1), PHYS, own, bond), low),
            pltpu.VMEM((max(p - 1, 1), PHYS, own, bond), low),
        ]
        + pairs(p, own // rows)
        + pairs(1)
        + pairs(p, 2)
        + pairs(q, 2)
        + pairs(p, q, 2)
        + pairs(q, edges)
        + pairs(q)
        + pairs(p, edges)
        + [pltpu.SemaphoreType.DMA((2,))],
        compiler_params=pltpu.CompilerParams(
            collective_id=1, has_side_effects=True, vmem_limit_bytes=56 * 2**20
        ),
        name="front",
    )(left, prev_left, current, right, prev_site, prev_right, spread.reshape(side, side))


def shards(left_env, prev_left, cur_site, prev_site, hamiltonian, right_env, prev_right):
    own_rows, bond_width = left_env.shape[1], left_env.shape[3]
    target = front(
        jnp.transpose(left_env[0], (1, 0, 2)),
        prev_left[0],
        jnp.transpose(cur_site[0], (1, 0, 2)),
        jnp.transpose(right_env[0], (1, 0, 2)),
        jnp.transpose(prev_site[0], (1, 0, 2)),
        prev_right[0],
        hamiltonian[0],
    ).reshape(PHYS * own_rows, bond_width)
    strips = [
        jnp.dot(
            target[:, start : start + STRIP].T,
            target[:, start:],
            precision=lax.Precision.HIGH,
            preferred_element_type=jnp.float32,
        )
        for start in range(0, bond_width, STRIP)
    ]
    packed = summed(jnp.concatenate(strips, axis=1))
    upper, inverse = factorize(packed, bond_width)
    norming = math.sqrt(bond_width * PHYS)
    solved = lax.dot_general(
        target,
        inverse,
        (((1,), (1,)), ((), ())),
        precision=lax.Precision.HIGH,
        preferred_element_type=jnp.float32,
    )
    new_site = (solved * norming).astype(jnp.bfloat16).reshape(PHYS, own_rows, bond_width)
    new_site = jnp.transpose(new_site, (1, 0, 2))[None]
    offset = lax.axis_index("bond") * own_rows
    center = lax.dynamic_slice_in_dim(upper, offset, own_rows, 0) / norming
    return (new_site, center[None])


def solution(mesh):
    return jax.shard_map(
        shards,
        mesh=mesh,
        in_specs=(
            P("seg", "bond", None, None),
            P("seg", None, None),
            P("seg", "bond", None, None),
            P("seg", None, None, "bond"),
            P("seg", None, None, None, None),
            P("seg", "bond", None, None),
            P("seg", None, None),
        ),
        out_specs=(P("seg", "bond", None, None), P("seg", "bond", None)),
        check_vma=False,
    )
```

```python
import functools
import math

import jax
import jax.numpy as jnp
from jax import lax
from jax.experimental import pallas as pl
from jax.experimental.pallas import tpu as pltpu
from jax.sharding import PartitionSpec as P

PHYS = 4
MPOB = 6
BLOCK = 128
STRIP = 256
GROUP = 4
ROWS = 8
AHEAD = 2
EDGES = 4
LEFT_ROWS = 64


def halves(x):
    high = x.astype(jnp.bfloat16)
    return high, (x - high.astype(jnp.float32)).astype(jnp.bfloat16)


def split_dot(a, b, dims):
    def dot(x, y):
        return lax.dot_general(x, y, (dims, ((), ())), preferred_element_type=jnp.float32)

    return dot(a[0], b[0]) + (dot(a[0], b[1]) + dot(a[1], b[0]))


def eliminate(block, rows_ref):
    size = block.shape[0]
    lane = lax.broadcasted_iota(jnp.int32, (1, size), 1)
    rest = block
    top = 0
    for first in range(0, size, GROUP):
        start = first // 8 * 8
        rest, top = rest[start - top :], start
        at = first - top
        rows = [rest[at + q : at + q + 1, :] for q in range(GROUP)]
        columns = [
            jnp.broadcast_to(rest[:, first + q : first + q + 1], rest.shape) for q in range(GROUP)
        ]
        small = [[columns[r][at + p : at + p + 1, :] for r in range(GROUP)] for p in range(GROUP)]
        change = None
        for q in range(GROUP):
            rows_ref[pl.ds(first + q, 1), :] = rows[q]
            inverse = 1.0 / small[q][q]
            lead = jnp.where(lane == first + q, 1.0, rows[q])
            for p in range(q + 1, GROUP):
                factor = small[q][p] * inverse
                for r in range(p, GROUP):
                    small[p][r] = small[p][r] - factor * small[q][r]
                rows[p] = jnp.where(lane == first + q, 0.0, rows[p]) - factor * lead
                columns[p] = columns[p] - factor * columns[q]
            if first + GROUP < size:
                lead = jnp.where((lane > first + q) & (lane < first + GROUP), 0.0, lead)
                term = columns[q] * (inverse * lead)
                change = term if change is None else change + term
        if first + GROUP < size:
            rest = jnp.where((lane >= first) & (lane < first + GROUP), 0.0, rest) - change


def back_kernel(
    n, norming, target_ref, site_ref, center_ref,
    high, low, turned_high, turned_low, mine, theirs, work, whole_high, whole_low,
    upper, panel, rows_ref,
    out_send, out_recv, back_send, back_recv,
):
    me = lax.axis_index("bond")
    height, size = target_ref.shape
    blocks = size // BLOCK
    share = BLOCK // n
    peers = [lax.rem(me + d, n) for d in range(n)]
    barrier = pltpu.get_barrier_semaphore()
    for peer in peers[1:]:
        pl.semaphore_signal(barrier, inc=1, device_id={"bond": peer})
    pl.semaphore_wait(barrier, n - 1)

    def lanes_of(s):
        return pl.ds(s * BLOCK, size - s * BLOCK)

    def rows_of(s, peer):
        return pl.ds(pl.multiple_of(s * BLOCK + peer * share, share), share)

    def outward(s, d):
        return pltpu.make_async_remote_copy(
            src_ref=mine.at[s, peers[d], :, lanes_of(s)],
            dst_ref=theirs.at[n - d - 1, s, :, lanes_of(s)],
            send_sem=out_send.at[s, d],
            recv_sem=out_recv.at[s, n - d],
            device_id={"bond": peers[d]},
        )

    def arriving(s, d):
        return pltpu.make_async_remote_copy(
            src_ref=mine.at[s, peers[d], :, lanes_of(s)],
            dst_ref=theirs.at[d - 1, s, :, lanes_of(s)],
            send_sem=out_send.at[s, d],
            recv_sem=out_recv.at[s, d],
            device_id={"bond": peers[d]},
        )

    def shared(s, d):
        here = work.at[rows_of(s, me), lanes_of(s)]
        return pltpu.make_async_remote_copy(
            src_ref=here,
            dst_ref=here,
            send_sem=back_send.at[s, d],
            recv_sem=back_recv.at[s, n - d],
            device_id={"bond": peers[d]},
        )

    def returning(s, d):
        there = work.at[rows_of(s, peers[d]), lanes_of(s)]
        return pltpu.make_async_remote_copy(
            src_ref=there,
            dst_ref=there,
            send_sem=back_send.at[s, d],
            recv_sem=back_recv.at[s, d],
            device_id={"bond": peers[d]},
        )

    def send_out(s):
        for d in range(1, n):
            outward(s, d).start()

    def reduce(s):
        first = s * BLOCK
        for d in range(1, n):
            arriving(s, d).wait_recv()
        value = mine[s, me, :, first:]
        for d in range(1, n):
            value = value + theirs[d - 1, s, :, first:]
        work[rows_of(s, me), first:] = value
        for d in range(1, n):
            shared(s, d).start()

    def collect(s):
        for d in range(1, n):
            returning(s, d).wait_recv()

    slab = min(STRIP, height)

    def split(i, carry):
        span = pl.ds(pl.multiple_of(i * slab, slab), slab)
        high[span, :], low[span, :] = halves(target_ref[span, :])
        return carry

    lax.fori_loop(0, height // slab, split, 0)
    whole_high[...] = jnp.zeros_like(whole_high)
    whole_low[...] = jnp.zeros_like(whole_low)
    per = STRIP // BLOCK
    for g in range(size // STRIP):
        turned_high[...], turned_low[...] = halves(target_ref[:, g * STRIP : (g + 1) * STRIP].T)

        def correlate(c, carry):
            lanes = pl.ds(pl.multiple_of(c * STRIP, STRIP), STRIP)
            value = split_dot(
                (turned_high[...], turned_low[...]), (high[:, lanes], low[:, lanes]), ((1,), (0,))
            )
            for b in range(per):
                part = value[b * BLOCK : (b + 1) * BLOCK, :]
                for i in range(n):
                    mine[g * per + b, i, :, lanes] = part[i * share : (i + 1) * share, :]
            return carry

        lax.fori_loop(g, size // STRIP, correlate, 0)
        if g == 0:
            for s in range(AHEAD):
                send_out(s)
    for s in range(AHEAD):
        reduce(s)
        send_out(s + AHEAD)

    row = lax.broadcasted_iota(jnp.int32, (BLOCK, BLOCK), 0)
    column = lax.broadcasted_iota(jnp.int32, (BLOCK, BLOCK), 1)
    full_column = lax.broadcasted_iota(jnp.int32, (BLOCK, size), 1)

    def step(k, carry):
        for s in range(blocks):

            @pl.when(k == s)
            def _():
                collect(s)

        own = pl.ds(pl.multiple_of(k * BLOCK, BLOCK), BLOCK)
        panel[...] = jnp.where(full_column < k * BLOCK, 0.0, work[own, :])

        def update(c, carry):
            span = pl.ds(pl.multiple_of(c * STRIP, STRIP), STRIP)
            panel[...] -= split_dot(
                (whole_high[span, own], whole_low[span, own]),
                (whole_high[span, :], whole_low[span, :]),
                ((0,), (0,)),
            )
            return carry

        lax.fori_loop(0, (k + per - 1) // per, update, 0)
        eliminate(panel[:, own], rows_ref)
        done = rows_ref[...]
        pivots = jnp.sum(jnp.where(row == column, done, 0.0), axis=1, keepdims=True)
        scale = lax.rsqrt(pivots)
        scaled = done * scale
        top = jnp.where(row <= column, scaled, 0.0)
        inverse = jnp.where(row > column, scaled, jnp.where(row == column, scale, 0.0))
        whole = split_dot(halves(inverse), halves(panel[...]), ((1,), (0,)))
        upper[own, :] = jnp.where(full_column >= (k + 1) * BLOCK, whole, 0.0)
        upper[own, own] = top
        whole_high[:, own] = jnp.zeros((size, BLOCK), jnp.bfloat16)
        whole_low[:, own] = jnp.zeros((size, BLOCK), jnp.bfloat16)
        whole_high[own, :], whole_low[own, :] = halves(whole)
        whole_high[own, own], whole_low[own, own] = halves(inverse)
        for s in range(AHEAD, blocks):

            @pl.when(k == s - AHEAD)
            def _():
                reduce(s)
                if s + AHEAD < blocks:
                    send_out(s + AHEAD)

        return carry

    lax.fori_loop(0, blocks, step, 0)
    own_rows = center_ref.shape[0]
    center_ref[...] = upper[pl.ds(pl.multiple_of(me * own_rows, own_rows), own_rows), :] / norming
    for g in range(size // STRIP):
        lanes = slice(g * STRIP, (g + 1) * STRIP)
        depth = (g + 1) * STRIP

        def solve(i, carry):
            span = pl.ds(pl.multiple_of(i * slab, slab), slab)
            value = split_dot(
                (high[span, :depth], low[span, :depth]),
                (whole_high[lanes, :depth], whole_low[lanes, :depth]),
                ((1,), (1,)),
            )
            site_ref[span, lanes] = (value * norming).astype(jnp.bfloat16)
            return carry

        lax.fori_loop(0, height // slab, solve, 0)
    for s in range(blocks):
        for d in range(1, n):
            outward(s, d).wait_send()
            shared(s, d).wait_send()


def back(target):
    n = lax.axis_size("bond")
    height, size = target.shape
    blocks, share = size // BLOCK, BLOCK // n
    norming = math.sqrt(size * PHYS)
    half, full = jnp.bfloat16, jnp.float32
    whole = pl.BlockSpec(memory_space=pltpu.VMEM)
    return pl.pallas_call(
        functools.partial(back_kernel, n, norming),
        out_shape=(
            jax.ShapeDtypeStruct((height, size), half),
            jax.ShapeDtypeStruct((size // n, size), full),
        ),
        in_specs=[whole],
        out_specs=[whole] * 2,
        scratch_shapes=[
            pltpu.VMEM((height, size), half),
            pltpu.VMEM((height, size), half),
            pltpu.VMEM((STRIP, height), half),
            pltpu.VMEM((STRIP, height), half),
            pltpu.VMEM((blocks, n, share, size), full),
            pltpu.VMEM((n - 1, blocks, share, size), full),
            pltpu.VMEM((size, size), full),
            pltpu.VMEM((size, size), half),
            pltpu.VMEM((size, size), half),
            pltpu.VMEM((size, size), full),
            pltpu.VMEM((BLOCK, size), full),
            pltpu.VMEM((BLOCK, BLOCK), full),
        ]
        + [pltpu.SemaphoreType.DMA((blocks, n))] * 4,
        compiler_params=pltpu.CompilerParams(
            collective_id=0, has_side_effects=True, vmem_limit_bytes=56 * 2**20
        ),
        name="back",
    )(target)


def minor_size(n):
    return max(d for d in range(1, n + 1) if n % d == 0 and d * d <= n)


def edge_spans(width):
    unit = width // EDGES
    return [(j * unit, unit) for j in range(EDGES)]


def front_kernel(
    segments, n, left_ref, prev_left_ref, current_ref, right_ref,
    prev_site_ref, prev_right_ref, spread_ref, target_ref,
    left, current, right, prev_left, partial_out, partial_in, projected, mixture, outgoing, incoming,
    left_send, left_recv, prev_send, prev_recv, major_send, major_recv, minor_send, minor_recv,
    relay_send, relay_recv, right_send, right_recv, partial_send, partial_recv,
    target_send, target_recv, local_sem,
):
    q = minor_size(n)
    p = n // q
    seg, index = lax.axis_index("seg"), lax.axis_index("bond")
    major, minor = index // q, lax.rem(index, q)
    own, bond = left_ref.shape[1], left_ref.shape[2]
    wide, tall = q * own, p * own
    half = own // 2
    rows = projected.shape[1] // MPOB
    chunks = own // rows
    spans = edge_spans(bond)

    def device(hop, dm, dr):
        m, r = lax.rem(major + dm, p), lax.rem(minor + dr, q)
        return {"seg": lax.rem(seg + hop, segments), "bond": m * q + r}

    def copy(src, dst, send, recv, to):
        return pltpu.make_async_remote_copy(
            src_ref=src, dst_ref=dst, send_sem=send, recv_sem=recv, device_id=to
        )

    def slot(d):
        return lax.rem(major + d, p)

    def place(dm, dr):
        return (lax.rem(major + dm, p) * q + lax.rem(minor + dr, q)) * own

    barrier = pltpu.get_barrier_semaphore()
    peers = [device(0, d, 0) for d in range(1, p)] + [device(0, 0, d) for d in range(1, q)]
    peers += [device(hop, d, 0) for d in range(p) for hop in (1, segments - 1)]
    for peer in peers:
        pl.semaphore_signal(barrier, inc=1, device_id=peer)
    pl.semaphore_wait(barrier, len(peers))

    def left_flow(d, j, slot_index, back):
        span = pl.ds(pl.multiple_of(j * rows, rows), rows)
        return copy(
            left_ref.at[:, span, :],
            left.at[slot_index, :, span, :],
            left_send.at[d, j],
            left_recv.at[back, j],
            device(1, d, 0),
        )

    def left_out(d, j):
        return left_flow(d, j, major, (p - d) % p)

    def left_in(d, j):
        return left_flow(d, j, slot(d), d)

    def current_rows(dm, dr, h):
        return pl.ds(pl.multiple_of(place(dm, dr) + h * half, half), half)

    def source_columns(dm):
        return pl.ds(pl.multiple_of(slot(dm) * wide, wide), wide)

    prev_flow = copy(prev_left_ref, prev_left, prev_send.at[0], prev_recv.at[0], device(1, 0, 0))
    prev_flow.start()
    sends = [prev_flow]
    for h in range(2):
        source = pl.ds(h * half, half)
        for d in range(1, p):
            flow = copy(
                current_ref.at[:, source, source_columns(d)],
                current.at[:, current_rows(0, 0, h), :],
                major_send.at[d, h],
                major_recv.at[p - d, h],
                device(0, d, 0),
            )
            flow.start()
            sends.append(flow)
        for d in range(1, q):
            flow = copy(
                current_ref.at[:, source, source_columns(0)],
                current.at[:, current_rows(0, 0, h), :],
                minor_send.at[d, h],
                minor_recv.at[q - d, h],
                device(0, 0, d),
            )
            flow.start()
            sends.append(flow)
    for j in range(chunks):
        for d in range(p):
            flow = left_out(d, j)
            flow.start()
            sends.append(flow)
    locals_ = [
        pltpu.make_async_copy(
            current_ref.at[:, :, source_columns(0)],
            current.at[:, pl.ds(pl.multiple_of(place(0, 0), own), own), :],
            local_sem.at[0],
        ),
        pltpu.make_async_copy(
            right_ref, right.at[:, pl.ds(pl.multiple_of(minor * own, own), own), :], local_sem.at[1]
        ),
    ]
    for one in locals_:
        one.start()

    for h in range(2):
        for dm in range(1, p):
            landed = current.at[:, current_rows(dm, 0, h), :]
            copy(
                landed, landed, major_send.at[dm, h], major_recv.at[dm, h], device(0, dm, 0)
            ).wait_recv()
            for d in range(1, q):
                flow = copy(
                    landed, landed, relay_send.at[dm, d, h], relay_recv.at[dm, q - d, h],
                    device(0, 0, d),
                )
                flow.start()
                sends.append(flow)

    prev_flow.wait_recv()

    def contract(d, out):
        def body(step, carry):
            m, s = step // PHYS, lax.rem(step, PHYS)
            top = (m * q + lax.rem(minor + d, q)) * own
            value = jnp.dot(
                prev_left[pl.ds(pl.multiple_of(top, own), own), :],
                prev_site_ref[s],
                preferred_element_type=jnp.float32,
            )
            out[s, pl.ds(pl.multiple_of(m * own, own), own), :] = value.astype(jnp.bfloat16)
            return carry

        lax.fori_loop(0, p * PHYS, body, 0)

    for d in range(1, q):
        contract(d, partial_out.at[d - 1])
        flow = copy(
            partial_out.at[d - 1], partial_in.at[minor], partial_send.at[d],
            partial_recv.at[q - d], device(0, 0, d),
        )
        flow.start()
        sends.append(flow)

    def right_flow(d, j, row, back):
        first, width = spans[j]
        lanes = pl.ds(first, width)
        return copy(
            right_ref.at[:, :, lanes],
            right.at[:, pl.ds(pl.multiple_of(row * own, own), own), lanes],
            right_send.at[d, j],
            right_recv.at[back, j],
            device(0, 0, d),
        )

    for j in range(len(spans)):
        for d in range(1, q):
            flow = right_flow(d, j, minor, q - d)
            flow.start()
            sends.append(flow)
    contract(0, partial_in.at[minor])

    for h in range(2):
        for d in range(1, q):
            landed = current.at[:, current_rows(0, d, h), :]
            copy(
                landed, landed, minor_send.at[d, h], minor_recv.at[d, h], device(0, 0, d)
            ).wait_recv()
            for dm in range(1, p):
                landed = current.at[:, current_rows(dm, d, h), :]
                copy(
                    landed, landed, relay_send.at[dm, d, h], relay_recv.at[dm, d, h],
                    device(0, 0, d),
                ).wait_recv()
    for one in locals_:
        one.wait()

    def mix(step, carry):
        j, order = step // p, lax.rem(step, p)
        where = lax.rem(major + order, p)
        left_in(order, j).wait_recv()
        span = pl.ds(pl.multiple_of(j * rows, rows), rows)
        block = left[where, :, span, :].reshape(MPOB * rows, bond)

        def project(t, carry):
            projected[t] = jnp.dot(block, current[t], preferred_element_type=jnp.float32)
            return carry

        lax.fori_loop(0, PHYS, project, 0)

        def spread(g, carry):
            results = []
            for first in range(2):
                at = g * 2 * ROWS + first * ROWS
                stack = jnp.concatenate(
                    [
                        projected[t, pl.ds(pl.multiple_of(u * rows + at, ROWS), ROWS), :]
                        for u in range(MPOB)
                        for t in range(PHYS)
                    ],
                    axis=0,
                )
                results.append(
                    jnp.dot(
                        spread_ref[...],
                        stack.astype(jnp.bfloat16),
                        preferred_element_type=jnp.float32,
                    )
                )
            top = pl.multiple_of(where * own + j * rows + g * 2 * ROWS, 2 * ROWS)
            for v in range(MPOB):
                for s in range(PHYS):
                    first = (v * PHYS + s) * ROWS
                    both = jnp.concatenate([one[first : first + ROWS] for one in results], axis=0)
                    mixture[s, pl.ds(top, 2 * ROWS), v * wide : (v + 1) * wide] = both.astype(
                        jnp.bfloat16
                    )
            return carry

        lax.fori_loop(0, rows // (2 * ROWS), spread, 0)
        return carry

    lax.fori_loop(0, chunks * p, mix, 0)

    for d in range(1, q):
        landed = partial_in.at[lax.rem(minor + d, q)]
        copy(
            landed, landed, partial_send.at[d], partial_recv.at[d], device(0, 0, d)
        ).wait_recv()

    def products(d, j, write):
        first, width = spans[j]

        def body(s, carry):
            top = pl.ds(pl.multiple_of(slot(d) * own, own), own)
            lanes = slice(first, first + width)
            value = 2.0 * jnp.dot(
                mixture[s, top, :],
                right[:, :, lanes].reshape(MPOB * wide, width),
                preferred_element_type=jnp.float32,
            )
            for r in range(q):
                prev_rows = pl.ds(pl.multiple_of(major * wide + r * own, own), own)
                value = value - jnp.dot(
                    partial_in[r, s, top, :],
                    prev_right_ref[prev_rows, lanes],
                    preferred_element_type=jnp.float32,
                )
            write(s, lanes, value)
            return carry

        lax.fori_loop(0, PHYS, body, 0)

    def target_flow(d, j, back):
        first, width = spans[j]
        lanes = pl.ds(first, width)
        return copy(
            outgoing.at[d - 1, :, :, lanes], incoming.at[back - 1, :, :, lanes],
            target_send.at[d, j], target_recv.at[back, j], device(0, d, 0),
        )

    for j in range(len(spans)):
        for d in range(1, q):
            right_flow(d, j, lax.rem(minor + d, q), d).wait_recv()
        for d in range(1, p):

            def keep(s, lanes, value):
                outgoing[d - 1, s, :, lanes] = value.astype(jnp.bfloat16)

            products(d, j, keep)
            flow = target_flow(d, j, p - d)
            flow.start()
            sends.append(flow)

        def own_part(s, lanes, value):
            target_ref[s, :, lanes] = value

        products(0, j, own_part)
    for j, (first, width) in enumerate(spans):
        for d in range(1, p):
            target_flow(d, j, d).wait_recv()
            lanes = slice(first, first + width)

            def add(s, carry):
                target_ref[s, :, lanes] += incoming[d - 1, s, :, lanes].astype(jnp.float32)
                return carry

            lax.fori_loop(0, PHYS, add, 0)
    for flow in sends:
        flow.wait_send()


def front(left, prev_left, current, right, prev_site, prev_right, coupling):
    n, segments = lax.axis_size("bond"), lax.axis_size("seg")
    q = minor_size(n)
    p = n // q
    own, bond = left.shape[1], left.shape[2]
    wide, tall = q * own, p * own
    rows = min(LEFT_ROWS, own)
    edges = len(edge_spans(bond))
    side = MPOB * PHYS * ROWS
    diagonal = jnp.eye(ROWS, dtype=coupling.dtype)
    turned = jnp.transpose(coupling, (1, 2, 0, 3))
    spread = turned[:, :, None, :, :, None] * diagonal[None, None, :, None, None, :]
    low, full = jnp.bfloat16, jnp.float32
    whole = pl.BlockSpec(memory_space=pltpu.VMEM)
    there = pl.BlockSpec(memory_space=pl.ANY)

    def pairs(*shape):
        return [pltpu.SemaphoreType.DMA(shape)] * 2

    return pl.pallas_call(
        functools.partial(front_kernel, segments, n),
        out_shape=jax.ShapeDtypeStruct((PHYS, own, bond), full),
        in_specs=[there] * 4 + [whole] * 3,
        out_specs=whole,
        scratch_shapes=[
            pltpu.VMEM((p, MPOB, own, bond), low),
            pltpu.VMEM((PHYS, bond, wide), low),
            pltpu.VMEM((MPOB, wide, bond), low),
            pltpu.VMEM((bond, bond), low),
            pltpu.VMEM((max(q - 1, 1), PHYS, tall, own), low),
            pltpu.VMEM((q, PHYS, tall, own), low),
            pltpu.VMEM((PHYS, MPOB * rows, wide), full),
            pltpu.VMEM((PHYS, tall, MPOB * wide), low),
            pltpu.VMEM((max(p - 1, 1), PHYS, own, bond), low),
            pltpu.VMEM((max(p - 1, 1), PHYS, own, bond), low),
        ]
        + pairs(p, own // rows)
        + pairs(1)
        + pairs(p, 2)
        + pairs(q, 2)
        + pairs(p, q, 2)
        + pairs(q, edges)
        + pairs(q)
        + pairs(p, edges)
        + [pltpu.SemaphoreType.DMA((2,))],
        compiler_params=pltpu.CompilerParams(
            collective_id=1, has_side_effects=True, vmem_limit_bytes=56 * 2**20
        ),
        name="front",
    )(left, prev_left, current, right, prev_site, prev_right, spread.reshape(side, side))


def shards(left_env, prev_left, cur_site, prev_site, hamiltonian, right_env, prev_right):
    own_rows, bond_width = left_env.shape[1], left_env.shape[3]
    target = front(
        jnp.transpose(left_env[0], (1, 0, 2)),
        prev_left[0],
        jnp.transpose(cur_site[0], (1, 0, 2)),
        jnp.transpose(right_env[0], (1, 0, 2)),
        jnp.transpose(prev_site[0], (1, 0, 2)),
        prev_right[0],
        hamiltonian[0],
    ).reshape(PHYS * own_rows, bond_width)
    site, center = back(target)
    site = jnp.transpose(site.reshape(PHYS, own_rows, bond_width), (1, 0, 2))
    return (site[None], center[None])


def solution(mesh):
    return jax.shard_map(
        shards,
        mesh=mesh,
        in_specs=(
            P("seg", "bond", None, None),
            P("seg", None, None),
            P("seg", "bond", None, None),
            P("seg", None, None, "bond"),
            P("seg", None, None, None, None),
            P("seg", "bond", None, None),
            P("seg", None, None),
        ),
        out_specs=(P("seg", "bond", None, None), P("seg", "bond", None)),
        check_vma=False,
    )
```

```python
import functools
import math

import jax
import jax.numpy as jnp
from jax import lax
from jax.experimental import pallas as pl
from jax.experimental.pallas import tpu as pltpu
from jax.sharding import PartitionSpec as P

PHYS = 4
MPOB = 6
BLOCK = 128
STRIP = 256
GROUP = 4
ROWS = 8
AHEAD = 2
EDGES = 8
LEFT_ROWS = 64


def halves(x):
    high = x.astype(jnp.bfloat16)
    return high, (x - high.astype(jnp.float32)).astype(jnp.bfloat16)


def split_dot(a, b, dims):
    def dot(x, y):
        return lax.dot_general(x, y, (dims, ((), ())), preferred_element_type=jnp.float32)

    return dot(a[0], b[0]) + (dot(a[0], b[1]) + dot(a[1], b[0]))


def eliminate(block, rows_ref):
    size = block.shape[0]
    lane = lax.broadcasted_iota(jnp.int32, (1, size), 1)
    rest = block
    top = 0
    for first in range(0, size, GROUP):
        start = first // 8 * 8
        rest, top = rest[start - top :], start
        at = first - top
        rows = [rest[at + q : at + q + 1, :] for q in range(GROUP)]
        columns = [
            jnp.broadcast_to(rest[:, first + q : first + q + 1], rest.shape) for q in range(GROUP)
        ]
        small = [[columns[r][at + p : at + p + 1, :] for r in range(GROUP)] for p in range(GROUP)]
        change = None
        for q in range(GROUP):
            rows_ref[pl.ds(first + q, 1), :] = rows[q]
            inverse = 1.0 / small[q][q]
            lead = jnp.where(lane == first + q, 1.0, rows[q])
            for p in range(q + 1, GROUP):
                factor = small[q][p] * inverse
                for r in range(p, GROUP):
                    small[p][r] = small[p][r] - factor * small[q][r]
                rows[p] = jnp.where(lane == first + q, 0.0, rows[p]) - factor * lead
                columns[p] = columns[p] - factor * columns[q]
            if first + GROUP < size:
                lead = jnp.where((lane > first + q) & (lane < first + GROUP), 0.0, lead)
                term = columns[q] * (inverse * lead)
                change = term if change is None else change + term
        if first + GROUP < size:
            rest = jnp.where((lane >= first) & (lane < first + GROUP), 0.0, rest) - change


def back_kernel(
    n, norming, target_ref, site_ref, center_ref,
    high, low, turned_high, turned_low, mine, theirs, work, whole_high, whole_low,
    upper, change, panel, rows_ref,
    out_send, out_recv, back_send, back_recv,
):
    me = lax.axis_index("bond")
    height, size = target_ref.shape
    blocks = size // BLOCK
    share = BLOCK // n
    peers = [lax.rem(me + d, n) for d in range(n)]
    barrier = pltpu.get_barrier_semaphore()
    for peer in peers[1:]:
        pl.semaphore_signal(barrier, inc=1, device_id={"bond": peer})
    pl.semaphore_wait(barrier, n - 1)

    def lanes_of(s):
        return pl.ds(s * BLOCK, size - s * BLOCK)

    def rows_of(s, peer):
        return pl.ds(pl.multiple_of(s * BLOCK + peer * share, share), share)

    def outward(s, d):
        return pltpu.make_async_remote_copy(
            src_ref=mine.at[s, peers[d], :, lanes_of(s)],
            dst_ref=theirs.at[n - d - 1, s, :, lanes_of(s)],
            send_sem=out_send.at[s, d],
            recv_sem=out_recv.at[s, n - d],
            device_id={"bond": peers[d]},
        )

    def arriving(s, d):
        return pltpu.make_async_remote_copy(
            src_ref=mine.at[s, peers[d], :, lanes_of(s)],
            dst_ref=theirs.at[d - 1, s, :, lanes_of(s)],
            send_sem=out_send.at[s, d],
            recv_sem=out_recv.at[s, d],
            device_id={"bond": peers[d]},
        )

    def shared(s, d):
        here = work.at[rows_of(s, me), lanes_of(s)]
        return pltpu.make_async_remote_copy(
            src_ref=here,
            dst_ref=here,
            send_sem=back_send.at[s, d],
            recv_sem=back_recv.at[s, n - d],
            device_id={"bond": peers[d]},
        )

    def returning(s, d):
        there = work.at[rows_of(s, peers[d]), lanes_of(s)]
        return pltpu.make_async_remote_copy(
            src_ref=there,
            dst_ref=there,
            send_sem=back_send.at[s, d],
            recv_sem=back_recv.at[s, d],
            device_id={"bond": peers[d]},
        )

    def send_out(s):
        for d in range(1, n):
            outward(s, d).start()

    def reduce(s):
        first = s * BLOCK
        for d in range(1, n):
            arriving(s, d).wait_recv()
        value = mine[s, me, :, first:]
        for d in range(1, n):
            value = value + theirs[d - 1, s, :, first:]
        work[rows_of(s, me), first:] = value
        for d in range(1, n):
            shared(s, d).start()

    def collect(s):
        for d in range(1, n):
            returning(s, d).wait_recv()

    slab = min(STRIP, height)

    def split(i, carry):
        span = pl.ds(pl.multiple_of(i * slab, slab), slab)
        high[span, :], low[span, :] = halves(target_ref[span, :])
        return carry

    lax.fori_loop(0, height // slab, split, 0)
    per = STRIP // BLOCK
    for g in range(size // STRIP):
        turned_high[...], turned_low[...] = halves(target_ref[:, g * STRIP : (g + 1) * STRIP].T)

        def correlate(c, carry):
            lanes = pl.ds(pl.multiple_of(c * STRIP, STRIP), STRIP)
            value = split_dot(
                (turned_high[...], turned_low[...]), (high[:, lanes], low[:, lanes]), ((1,), (0,))
            )
            for b in range(per):
                part = value[b * BLOCK : (b + 1) * BLOCK, :]
                for i in range(n):
                    mine[g * per + b, i, :, lanes] = part[i * share : (i + 1) * share, :]
            return carry

        lax.fori_loop(g, size // STRIP, correlate, 0)
        if g == 0:
            for s in range(AHEAD):
                send_out(s)
            whole_high[...] = jnp.zeros_like(whole_high)
            whole_low[...] = jnp.zeros_like(whole_low)
            change[...] = jnp.zeros_like(change)
    for s in range(AHEAD):
        reduce(s)
        send_out(s + AHEAD)

    row = lax.broadcasted_iota(jnp.int32, (BLOCK, BLOCK), 0)
    column = lax.broadcasted_iota(jnp.int32, (BLOCK, BLOCK), 1)
    full_column = lax.broadcasted_iota(jnp.int32, (BLOCK, size), 1)

    def solve_strip(g):
        lanes = slice(g * STRIP, (g + 1) * STRIP)
        depth = (g + 1) * STRIP

        def solve(i, carry):
            span = pl.ds(pl.multiple_of(i * slab, slab), slab)
            value = split_dot(
                (high[span, :depth], low[span, :depth]),
                (whole_high[lanes, :depth], whole_low[lanes, :depth]),
                ((1,), (1,)),
            )
            site_ref[span, lanes] = (value * norming).astype(jnp.bfloat16)
            return carry

        lax.fori_loop(0, height // slab, solve, 0)

    def step(k, carry):
        for s in range(blocks):

            @pl.when(k == s)
            def _():
                collect(s)

        own = pl.ds(pl.multiple_of(k * BLOCK, BLOCK), BLOCK)
        panel[...] = jnp.where(full_column < k * BLOCK, 0.0, work[own, :]) - change[own, :]
        eliminate(panel[:, own], rows_ref)
        done = rows_ref[...]
        pivots = jnp.sum(jnp.where(row == column, done, 0.0), axis=1, keepdims=True)
        scale = lax.rsqrt(pivots)
        scaled = done * scale
        top = jnp.where(row <= column, scaled, 0.0)
        inverse = jnp.where(row > column, scaled, jnp.where(row == column, scale, 0.0))
        whole = split_dot(halves(inverse), halves(panel[...]), ((1,), (0,)))
        upper[own, :] = jnp.where(full_column >= (k + 1) * BLOCK, whole, 0.0)
        upper[own, own] = top
        whole_high[:, own] = jnp.zeros((size, BLOCK), jnp.bfloat16)
        whole_low[:, own] = jnp.zeros((size, BLOCK), jnp.bfloat16)
        whole_high[own, :], whole_low[own, :] = halves(whole)
        whole_high[own, own], whole_low[own, own] = halves(inverse)
        for s in range(AHEAD, blocks):

            @pl.when(k == s - AHEAD)
            def _():
                reduce(s)
                if s + AHEAD < blocks:
                    send_out(s + AHEAD)

        def update(i, span):
            other = pl.ds(pl.multiple_of(i * BLOCK, BLOCK), BLOCK)
            change[other, span] = jnp.zeros((BLOCK, span.size), jnp.float32)
            change[other, :] += split_dot(
                (whole_high[span, other], whole_low[span, other]),
                (whole_high[span, :], whole_low[span, :]),
                ((0,), (0,)),
            )

        place = lax.rem(k, per)
        for depth in range(1, per):

            @pl.when((place == depth - 1) & (k + 1 < blocks))
            def _():
                first = (k - depth + 1) * BLOCK
                update(k + 1, pl.ds(pl.multiple_of(first, BLOCK), depth * BLOCK))

        @pl.when(place == per - 1)
        def _():
            span = pl.ds(pl.multiple_of((k - per + 1) * BLOCK, STRIP), STRIP)

            def later(i, carry):
                update(i, span)
                return carry

            lax.fori_loop(k + 1, blocks, later, 0)

        for g in range(size // STRIP):

            @pl.when(k == (g + 1) * per - 1)
            def _():
                solve_strip(g)

        return carry

    lax.fori_loop(0, blocks, step, 0)
    own_rows = center_ref.shape[0]
    center_ref[...] = upper[pl.ds(pl.multiple_of(me * own_rows, own_rows), own_rows), :] / norming
    for s in range(blocks):
        for d in range(1, n):
            outward(s, d).wait_send()
            shared(s, d).wait_send()


def back(target):
    n = lax.axis_size("bond")
    height, size = target.shape
    blocks, share = size // BLOCK, BLOCK // n
    norming = math.sqrt(size * PHYS)
    half, full = jnp.bfloat16, jnp.float32
    whole = pl.BlockSpec(memory_space=pltpu.VMEM)
    return pl.pallas_call(
        functools.partial(back_kernel, n, norming),
        out_shape=(
            jax.ShapeDtypeStruct((height, size), half),
            jax.ShapeDtypeStruct((size // n, size), full),
        ),
        in_specs=[whole],
        out_specs=[whole] * 2,
        scratch_shapes=[
            pltpu.VMEM((height, size), half),
            pltpu.VMEM((height, size), half),
            pltpu.VMEM((STRIP, height), half),
            pltpu.VMEM((STRIP, height), half),
            pltpu.VMEM((blocks, n, share, size), full),
            pltpu.VMEM((n - 1, blocks, share, size), full),
            pltpu.VMEM((size, size), full),
            pltpu.VMEM((size, size), half),
            pltpu.VMEM((size, size), half),
            pltpu.VMEM((size, size), full),
            pltpu.VMEM((size, size), full),
            pltpu.VMEM((BLOCK, size), full),
            pltpu.VMEM((BLOCK, BLOCK), full),
        ]
        + [pltpu.SemaphoreType.DMA((blocks, n))] * 4,
        compiler_params=pltpu.CompilerParams(
            collective_id=0, has_side_effects=True, vmem_limit_bytes=56 * 2**20
        ),
        name="back",
    )(target)


def minor_size(n):
    return max(d for d in range(1, n + 1) if n % d == 0 and d * d <= n)


def edge_spans(width):
    unit = width // EDGES
    return [(j * unit, unit) for j in range(EDGES)]


def front_kernel(
    segments, n, left_ref, prev_left_ref, current_ref, right_ref,
    prev_site_ref, prev_right_ref, spread_ref, target_ref,
    left, current, right, prev_left, partial_out, partial_in, projected, mixture, outgoing, incoming,
    left_send, left_recv, prev_send, prev_recv, major_send, major_recv, minor_send, minor_recv,
    relay_send, relay_recv, right_send, right_recv, partial_send, partial_recv,
    target_send, target_recv, local_sem,
):
    q = minor_size(n)
    p = n // q
    seg, index = lax.axis_index("seg"), lax.axis_index("bond")
    major, minor = index // q, lax.rem(index, q)
    own, bond = left_ref.shape[1], left_ref.shape[2]
    wide, tall = q * own, p * own
    half = own // 2
    rows = projected.shape[1] // MPOB
    chunks = own // rows
    spans = edge_spans(bond)

    def device(hop, dm, dr):
        m, r = lax.rem(major + dm, p), lax.rem(minor + dr, q)
        return {"seg": lax.rem(seg + hop, segments), "bond": m * q + r}

    def copy(src, dst, send, recv, to):
        return pltpu.make_async_remote_copy(
            src_ref=src, dst_ref=dst, send_sem=send, recv_sem=recv, device_id=to
        )

    def slot(d):
        return lax.rem(major + d, p)

    def place(dm, dr):
        return (lax.rem(major + dm, p) * q + lax.rem(minor + dr, q)) * own

    barrier = pltpu.get_barrier_semaphore()
    peers = [device(0, d, 0) for d in range(1, p)] + [device(0, 0, d) for d in range(1, q)]
    peers += [device(hop, d, 0) for d in range(p) for hop in (1, segments - 1)]
    for peer in peers:
        pl.semaphore_signal(barrier, inc=1, device_id=peer)
    pl.semaphore_wait(barrier, len(peers))

    def left_flow(d, j, slot_index, back):
        span = pl.ds(pl.multiple_of(j * rows, rows), rows)
        return copy(
            left_ref.at[:, span, :],
            left.at[slot_index, :, span, :],
            left_send.at[d, j],
            left_recv.at[back, j],
            device(1, d, 0),
        )

    def left_out(d, j):
        return left_flow(d, j, major, (p - d) % p)

    def left_in(d, j):
        return left_flow(d, j, slot(d), d)

    def current_rows(dm, dr, h):
        return pl.ds(pl.multiple_of(place(dm, dr) + h * half, half), half)

    def source_columns(dm):
        return pl.ds(pl.multiple_of(slot(dm) * wide, wide), wide)

    prev_flow = copy(prev_left_ref, prev_left, prev_send.at[0], prev_recv.at[0], device(1, 0, 0))
    prev_flow.start()
    sends = [prev_flow]
    for h in range(2):
        source = pl.ds(h * half, half)
        for d in range(1, p):
            flow = copy(
                current_ref.at[:, source, source_columns(d)],
                current.at[:, current_rows(0, 0, h), :],
                major_send.at[d, h],
                major_recv.at[p - d, h],
                device(0, d, 0),
            )
            flow.start()
            sends.append(flow)
        for d in range(1, q):
            flow = copy(
                current_ref.at[:, source, source_columns(0)],
                current.at[:, current_rows(0, 0, h), :],
                minor_send.at[d, h],
                minor_recv.at[q - d, h],
                device(0, 0, d),
            )
            flow.start()
            sends.append(flow)
    for j in range(chunks):
        for d in range(p):
            flow = left_out(d, j)
            flow.start()
            sends.append(flow)
    locals_ = [
        pltpu.make_async_copy(
            current_ref.at[:, :, source_columns(0)],
            current.at[:, pl.ds(pl.multiple_of(place(0, 0), own), own), :],
            local_sem.at[0],
        ),
        pltpu.make_async_copy(
            right_ref, right.at[:, pl.ds(pl.multiple_of(minor * own, own), own), :], local_sem.at[1]
        ),
    ]
    for one in locals_:
        one.start()

    for h in range(2):
        for dm in range(1, p):
            landed = current.at[:, current_rows(dm, 0, h), :]
            copy(
                landed, landed, major_send.at[dm, h], major_recv.at[dm, h], device(0, dm, 0)
            ).wait_recv()
            for d in range(1, q):
                flow = copy(
                    landed, landed, relay_send.at[dm, d, h], relay_recv.at[dm, q - d, h],
                    device(0, 0, d),
                )
                flow.start()
                sends.append(flow)

    prev_flow.wait_recv()

    def contract(d, out):
        def body(step, carry):
            m, s = step // PHYS, lax.rem(step, PHYS)
            top = (m * q + lax.rem(minor + d, q)) * own
            value = jnp.dot(
                prev_left[pl.ds(pl.multiple_of(top, own), own), :],
                prev_site_ref[s],
                preferred_element_type=jnp.float32,
            )
            out[s, pl.ds(pl.multiple_of(m * own, own), own), :] = value.astype(jnp.bfloat16)
            return carry

        lax.fori_loop(0, p * PHYS, body, 0)

    for d in range(1, q):
        contract(d, partial_out.at[d - 1])
        flow = copy(
            partial_out.at[d - 1], partial_in.at[minor], partial_send.at[d],
            partial_recv.at[q - d], device(0, 0, d),
        )
        flow.start()
        sends.append(flow)

    def right_flow(d, j, row, back):
        first, width = spans[j]
        lanes = pl.ds(first, width)
        return copy(
            right_ref.at[:, :, lanes],
            right.at[:, pl.ds(pl.multiple_of(row * own, own), own), lanes],
            right_send.at[d, j],
            right_recv.at[back, j],
            device(0, 0, d),
        )

    for j in range(len(spans)):
        for d in range(1, q):
            flow = right_flow(d, j, minor, q - d)
            flow.start()
            sends.append(flow)
    contract(0, partial_in.at[minor])

    for h in range(2):
        for d in range(1, q):
            landed = current.at[:, current_rows(0, d, h), :]
            copy(
                landed, landed, minor_send.at[d, h], minor_recv.at[d, h], device(0, 0, d)
            ).wait_recv()
            for dm in range(1, p):
                landed = current.at[:, current_rows(dm, d, h), :]
                copy(
                    landed, landed, relay_send.at[dm, d, h], relay_recv.at[dm, d, h],
                    device(0, 0, d),
                ).wait_recv()
    for one in locals_:
        one.wait()

    def mix(step, carry):
        j, order = step // p, lax.rem(step, p)
        where = lax.rem(major + order, p)
        left_in(order, j).wait_recv()
        span = pl.ds(pl.multiple_of(j * rows, rows), rows)
        block = left[where, :, span, :].reshape(MPOB * rows, bond)

        def project(t, carry):
            projected[t] = jnp.dot(block, current[t], preferred_element_type=jnp.float32)
            return carry

        lax.fori_loop(0, PHYS, project, 0)

        def spread(g, carry):
            results = []
            for first in range(2):
                at = g * 2 * ROWS + first * ROWS
                stack = jnp.concatenate(
                    [
                        projected[t, pl.ds(pl.multiple_of(u * rows + at, ROWS), ROWS), :]
                        for u in range(MPOB)
                        for t in range(PHYS)
                    ],
                    axis=0,
                )
                results.append(
                    jnp.dot(
                        spread_ref[...],
                        stack.astype(jnp.bfloat16),
                        preferred_element_type=jnp.float32,
                    )
                )
            top = pl.multiple_of(where * own + j * rows + g * 2 * ROWS, 2 * ROWS)
            for v in range(MPOB):
                for s in range(PHYS):
                    first = (v * PHYS + s) * ROWS
                    both = jnp.concatenate([one[first : first + ROWS] for one in results], axis=0)
                    mixture[s, pl.ds(top, 2 * ROWS), v * wide : (v + 1) * wide] = both.astype(
                        jnp.bfloat16
                    )
            return carry

        lax.fori_loop(0, rows // (2 * ROWS), spread, 0)
        return carry

    lax.fori_loop(0, chunks * p, mix, 0)

    for d in range(1, q):
        landed = partial_in.at[lax.rem(minor + d, q)]
        copy(
            landed, landed, partial_send.at[d], partial_recv.at[d], device(0, 0, d)
        ).wait_recv()

    def products(d, j, write):
        first, width = spans[j]

        def body(s, carry):
            top = pl.ds(pl.multiple_of(slot(d) * own, own), own)
            lanes = slice(first, first + width)
            value = 2.0 * jnp.dot(
                mixture[s, top, :],
                right[:, :, lanes].reshape(MPOB * wide, width),
                preferred_element_type=jnp.float32,
            )
            for r in range(q):
                prev_rows = pl.ds(pl.multiple_of(major * wide + r * own, own), own)
                value = value - jnp.dot(
                    partial_in[r, s, top, :],
                    prev_right_ref[prev_rows, lanes],
                    preferred_element_type=jnp.float32,
                )
            write(s, lanes, value)
            return carry

        lax.fori_loop(0, PHYS, body, 0)

    def target_flow(d, j, back):
        first, width = spans[j]
        lanes = pl.ds(first, width)
        return copy(
            outgoing.at[d - 1, :, :, lanes], incoming.at[back - 1, :, :, lanes],
            target_send.at[d, j], target_recv.at[back, j], device(0, d, 0),
        )

    for j in range(len(spans)):
        for d in range(1, q):
            right_flow(d, j, lax.rem(minor + d, q), d).wait_recv()
        for d in range(1, p):

            def keep(s, lanes, value):
                outgoing[d - 1, s, :, lanes] = value.astype(jnp.bfloat16)

            products(d, j, keep)
            flow = target_flow(d, j, p - d)
            flow.start()
            sends.append(flow)

        def own_part(s, lanes, value):
            target_ref[s, :, lanes] = value

        products(0, j, own_part)
    for j, (first, width) in enumerate(spans):
        for d in range(1, p):
            target_flow(d, j, d).wait_recv()
            lanes = slice(first, first + width)

            def add(s, carry):
                target_ref[s, :, lanes] += incoming[d - 1, s, :, lanes].astype(jnp.float32)
                return carry

            lax.fori_loop(0, PHYS, add, 0)
    for flow in sends:
        flow.wait_send()


def front(left, prev_left, current, right, prev_site, prev_right, coupling):
    n, segments = lax.axis_size("bond"), lax.axis_size("seg")
    q = minor_size(n)
    p = n // q
    own, bond = left.shape[1], left.shape[2]
    wide, tall = q * own, p * own
    rows = min(LEFT_ROWS, own)
    edges = len(edge_spans(bond))
    side = MPOB * PHYS * ROWS
    diagonal = jnp.eye(ROWS, dtype=coupling.dtype)
    turned = jnp.transpose(coupling, (1, 2, 0, 3))
    spread = turned[:, :, None, :, :, None] * diagonal[None, None, :, None, None, :]
    low, full = jnp.bfloat16, jnp.float32
    whole = pl.BlockSpec(memory_space=pltpu.VMEM)
    there = pl.BlockSpec(memory_space=pl.ANY)

    def pairs(*shape):
        return [pltpu.SemaphoreType.DMA(shape)] * 2

    return pl.pallas_call(
        functools.partial(front_kernel, segments, n),
        out_shape=jax.ShapeDtypeStruct((PHYS, own, bond), full),
        in_specs=[there] * 4 + [whole] * 3,
        out_specs=whole,
        scratch_shapes=[
            pltpu.VMEM((p, MPOB, own, bond), low),
            pltpu.VMEM((PHYS, bond, wide), low),
            pltpu.VMEM((MPOB, wide, bond), low),
            pltpu.VMEM((bond, bond), low),
            pltpu.VMEM((max(q - 1, 1), PHYS, tall, own), low),
            pltpu.VMEM((q, PHYS, tall, own), low),
            pltpu.VMEM((PHYS, MPOB * rows, wide), full),
            pltpu.VMEM((PHYS, tall, MPOB * wide), low),
            pltpu.VMEM((max(p - 1, 1), PHYS, own, bond), low),
            pltpu.VMEM((max(p - 1, 1), PHYS, own, bond), low),
        ]
        + pairs(p, own // rows)
        + pairs(1)
        + pairs(p, 2)
        + pairs(q, 2)
        + pairs(p, q, 2)
        + pairs(q, edges)
        + pairs(q)
        + pairs(p, edges)
        + [pltpu.SemaphoreType.DMA((2,))],
        compiler_params=pltpu.CompilerParams(
            collective_id=1, has_side_effects=True, vmem_limit_bytes=56 * 2**20
        ),
        name="front",
    )(left, prev_left, current, right, prev_site, prev_right, spread.reshape(side, side))


def shards(left_env, prev_left, cur_site, prev_site, hamiltonian, right_env, prev_right):
    own_rows, bond_width = left_env.shape[1], left_env.shape[3]
    target = front(
        jnp.transpose(left_env[0], (1, 0, 2)),
        prev_left[0],
        jnp.transpose(cur_site[0], (1, 0, 2)),
        jnp.transpose(right_env[0], (1, 0, 2)),
        jnp.transpose(prev_site[0], (1, 0, 2)),
        prev_right[0],
        hamiltonian[0],
    ).reshape(PHYS * own_rows, bond_width)
    site, center = back(target)
    site = jnp.transpose(site.reshape(PHYS, own_rows, bond_width), (1, 0, 2))
    return (site[None], center[None])


def solution(mesh):
    return jax.shard_map(
        shards,
        mesh=mesh,
        in_specs=(
            P("seg", "bond", None, None),
            P("seg", None, None),
            P("seg", "bond", None, None),
            P("seg", None, None, "bond"),
            P("seg", None, None, None, None),
            P("seg", "bond", None, None),
            P("seg", None, None),
        ),
        out_specs=(P("seg", "bond", None, None), P("seg", "bond", None)),
        check_vma=False,
    )
```

```python
import functools
import math

import jax
import jax.numpy as jnp
from jax import lax
from jax.experimental import pallas as pl
from jax.experimental.pallas import tpu as pltpu
from jax.sharding import PartitionSpec as P

PHYS = 4
MPOB = 6
BLOCK = 128
STRIP = 256
GROUP = 4
ROWS = 8
AHEAD = 3
EDGES = 8
LEFT_ROWS = 64


def halves(x):
    high = x.astype(jnp.bfloat16)
    return high, (x - high.astype(jnp.float32)).astype(jnp.bfloat16)


def split_dot(a, b, dims):
    def dot(x, y):
        return lax.dot_general(x, y, (dims, ((), ())), preferred_element_type=jnp.float32)

    return dot(a[0], b[0]) + (dot(a[0], b[1]) + dot(a[1], b[0]))


def eliminate(block, rows_ref):
    size = block.shape[0]
    lane = lax.broadcasted_iota(jnp.int32, (1, size), 1)
    rest = block
    top = 0
    for first in range(0, size, GROUP):
        start = first // 8 * 8
        rest, top = rest[start - top :], start
        at = first - top
        rows = [rest[at + q : at + q + 1, :] for q in range(GROUP)]
        columns = [
            jnp.broadcast_to(rest[:, first + q : first + q + 1], rest.shape) for q in range(GROUP)
        ]
        small = [[columns[r][at + p : at + p + 1, :] for r in range(GROUP)] for p in range(GROUP)]
        change = None
        for q in range(GROUP):
            rows_ref[pl.ds(first + q, 1), :] = rows[q]
            inverse = 1.0 / small[q][q]
            lead = jnp.where(lane == first + q, 1.0, rows[q])
            for p in range(q + 1, GROUP):
                factor = small[q][p] * inverse
                for r in range(p, GROUP):
                    small[p][r] = small[p][r] - factor * small[q][r]
                rows[p] = jnp.where(lane == first + q, 0.0, rows[p]) - factor * lead
                columns[p] = columns[p] - factor * columns[q]
            if first + GROUP < size:
                lead = jnp.where((lane > first + q) & (lane < first + GROUP), 0.0, lead)
                term = columns[q] * (inverse * lead)
                change = term if change is None else change + term
        if first + GROUP < size:
            rest = jnp.where((lane >= first) & (lane < first + GROUP), 0.0, rest) - change


def back_kernel(
    n, norming, target_ref, site_ref, center_ref,
    high, low, turned_high, turned_low, mine, theirs, work, whole_high, whole_low,
    upper, left, panel, given_high, given_low, rows_ref,
    out_send, out_recv, back_send, back_recv,
):
    me = lax.axis_index("bond")
    height, size = target_ref.shape
    blocks = size // BLOCK
    share = BLOCK // n
    peers = [lax.rem(me + d, n) for d in range(n)]
    barrier = pltpu.get_barrier_semaphore()
    for peer in peers[1:]:
        pl.semaphore_signal(barrier, inc=1, device_id={"bond": peer})
    pl.semaphore_wait(barrier, n - 1)

    def lanes_of(s):
        return pl.ds(0, (s + 1) * BLOCK)

    def rows_of(s, peer):
        return pl.ds(pl.multiple_of(s * BLOCK + peer * share, share), share)

    def outward(s, d):
        return pltpu.make_async_remote_copy(
            src_ref=mine.at[s, peers[d], :, lanes_of(s)],
            dst_ref=theirs.at[n - d - 1, s, :, lanes_of(s)],
            send_sem=out_send.at[s, d],
            recv_sem=out_recv.at[s, n - d],
            device_id={"bond": peers[d]},
        )

    def arriving(s, d):
        return pltpu.make_async_remote_copy(
            src_ref=mine.at[s, peers[d], :, lanes_of(s)],
            dst_ref=theirs.at[d - 1, s, :, lanes_of(s)],
            send_sem=out_send.at[s, d],
            recv_sem=out_recv.at[s, d],
            device_id={"bond": peers[d]},
        )

    def shared(s, d):
        here = work.at[rows_of(s, me), lanes_of(s)]
        return pltpu.make_async_remote_copy(
            src_ref=here,
            dst_ref=here,
            send_sem=back_send.at[s, d],
            recv_sem=back_recv.at[s, n - d],
            device_id={"bond": peers[d]},
        )

    def returning(s, d):
        there = work.at[rows_of(s, peers[d]), lanes_of(s)]
        return pltpu.make_async_remote_copy(
            src_ref=there,
            dst_ref=there,
            send_sem=back_send.at[s, d],
            recv_sem=back_recv.at[s, d],
            device_id={"bond": peers[d]},
        )

    def send_out(s):
        for d in range(1, n):
            outward(s, d).start()

    def reduce(s):
        last = (s + 1) * BLOCK
        for d in range(1, n):
            arriving(s, d).wait_recv()
        value = mine[s, me, :, :last]
        for d in range(1, n):
            value = value + theirs[d - 1, s, :, :last]
        work[rows_of(s, me), :last] = value
        for d in range(1, n):
            shared(s, d).start()

    def collect(s):
        for d in range(1, n):
            returning(s, d).wait_recv()

    slab = min(STRIP, height)

    def split(i, carry):
        span = pl.ds(pl.multiple_of(i * slab, slab), slab)
        high[span, :], low[span, :] = halves(target_ref[span, :])
        return carry

    lax.fori_loop(0, height // slab, split, 0)
    per = STRIP // BLOCK
    for g in range(size // STRIP):
        turned_high[...], turned_low[...] = halves(target_ref[:, g * STRIP : (g + 1) * STRIP].T)

        def correlate(c, carry):
            lanes = pl.ds(pl.multiple_of(c * STRIP, STRIP), STRIP)
            value = split_dot(
                (turned_high[...], turned_low[...]), (high[:, lanes], low[:, lanes]), ((1,), (0,))
            )
            for b in range(per):
                part = value[b * BLOCK : (b + 1) * BLOCK, :]
                for i in range(n):
                    mine[g * per + b, i, :, lanes] = part[i * share : (i + 1) * share, :]
            return carry

        lax.fori_loop(0, g + 1, correlate, 0)
        for s in range(g * per, min((g + 1) * per, AHEAD)):
            send_out(s)
    whole_high[...] = jnp.zeros_like(whole_high)
    whole_low[...] = jnp.zeros_like(whole_low)
    left[...] = jnp.zeros_like(left)
    for s in range(min(AHEAD, blocks)):
        reduce(s)
        if s + AHEAD < blocks:
            send_out(s + AHEAD)

    row = lax.broadcasted_iota(jnp.int32, (BLOCK, BLOCK), 0)
    column = lax.broadcasted_iota(jnp.int32, (BLOCK, BLOCK), 1)
    full_column = lax.broadcasted_iota(jnp.int32, (BLOCK, size), 1)

    def solve_strip(g):
        lanes = slice(g * STRIP, (g + 1) * STRIP)
        depth = (g + 1) * STRIP

        def solve(i, carry):
            span = pl.ds(pl.multiple_of(i * slab, slab), slab)
            value = split_dot(
                (high[span, :depth], low[span, :depth]),
                (whole_high[lanes, :depth], whole_low[lanes, :depth]),
                ((1,), (1,)),
            )
            site_ref[span, lanes] = (value * norming).astype(jnp.bfloat16)
            return carry

        lax.fori_loop(0, height // slab, solve, 0)

    def step(k, carry):
        for s in range(blocks):

            @pl.when(k == s)
            def _():
                collect(s)
                if s + AHEAD < blocks:
                    reduce(s + AHEAD)
                if s + 2 * AHEAD < blocks:
                    send_out(s + 2 * AHEAD)

        own = pl.ds(pl.multiple_of(k * BLOCK, BLOCK), BLOCK)
        given_high[...], given_low[...] = halves(
            jnp.where(full_column < k * BLOCK, work[own, :], 0.0)
        )

        def reach(c, carry):
            span = pl.ds(pl.multiple_of(c * STRIP, STRIP), STRIP)
            left[:, span] = split_dot(
                (given_high[...], given_low[...]),
                (whole_high[span, :], whole_low[span, :]),
                ((1,), (1,)),
            )
            return carry

        chunks = (k + per - 1) // per
        lax.fori_loop(0, chunks, reach, 0)
        given_high[...], given_low[...] = halves(left[...])
        given = (given_high[...], given_low[...])
        eliminate(work[own, own] - split_dot(given, given, ((1,), (1,))), rows_ref)
        panel[...] = jnp.zeros_like(panel)

        def gather(c, carry):
            span = pl.ds(pl.multiple_of(c * STRIP, STRIP), STRIP)
            panel[...] += split_dot(
                (given_high[:, span], given_low[:, span]),
                (whole_high[span, :], whole_low[span, :]),
                ((1,), (0,)),
            )
            return carry

        lax.fori_loop(0, chunks, gather, 0)
        done = rows_ref[...]
        pivots = jnp.sum(jnp.where(row == column, done, 0.0), axis=1, keepdims=True)
        scale = lax.rsqrt(pivots)
        scaled = done * scale
        top = jnp.where(row <= column, scaled, 0.0)
        inverse = jnp.where(row > column, scaled, jnp.where(row == column, scale, 0.0))
        whole = split_dot(halves(-inverse), halves(panel[...]), ((1,), (0,)))
        whole_high[own, :], whole_low[own, :] = halves(whole)
        whole_high[own, own], whole_low[own, own] = halves(inverse)
        upper[:, own] = left[...].T
        upper[own, own] = top
        for g in range(size // STRIP):

            @pl.when(k == (g + 1) * per - 1)
            def _():
                solve_strip(g)

        return carry

    lax.fori_loop(0, blocks, step, 0)
    own_rows = center_ref.shape[0]
    center_ref[...] = upper[pl.ds(pl.multiple_of(me * own_rows, own_rows), own_rows), :] / norming
    for s in range(blocks):
        for d in range(1, n):
            outward(s, d).wait_send()
            shared(s, d).wait_send()


def back(target):
    n = lax.axis_size("bond")
    height, size = target.shape
    blocks, share = size // BLOCK, BLOCK // n
    norming = math.sqrt(size * PHYS)
    half, full = jnp.bfloat16, jnp.float32
    whole = pl.BlockSpec(memory_space=pltpu.VMEM)
    return pl.pallas_call(
        functools.partial(back_kernel, n, norming),
        out_shape=(
            jax.ShapeDtypeStruct((height, size), half),
            jax.ShapeDtypeStruct((size // n, size), full),
        ),
        in_specs=[whole],
        out_specs=[whole] * 2,
        scratch_shapes=[
            pltpu.VMEM((height, size), half),
            pltpu.VMEM((height, size), half),
            pltpu.VMEM((STRIP, height), half),
            pltpu.VMEM((STRIP, height), half),
            pltpu.VMEM((blocks, n, share, size), full),
            pltpu.VMEM((n - 1, blocks, share, size), full),
            pltpu.VMEM((size, size), full),
            pltpu.VMEM((size, size), half),
            pltpu.VMEM((size, size), half),
            pltpu.VMEM((size, size), full),
            pltpu.VMEM((BLOCK, size), full),
            pltpu.VMEM((BLOCK, size), full),
            pltpu.VMEM((BLOCK, size), half),
            pltpu.VMEM((BLOCK, size), half),
            pltpu.VMEM((BLOCK, BLOCK), full),
        ]
        + [pltpu.SemaphoreType.DMA((blocks, n))] * 4,
        compiler_params=pltpu.CompilerParams(
            collective_id=0, has_side_effects=True, vmem_limit_bytes=56 * 2**20
        ),
        name="back",
    )(target)


def minor_size(n):
    return max(d for d in range(1, n + 1) if n % d == 0 and d * d <= n)


def edge_spans(width):
    unit = width // EDGES
    return [(j * unit, unit) for j in range(EDGES)]


def front_kernel(
    segments, n, left_ref, prev_left_ref, current_ref, right_ref,
    prev_site_ref, prev_right_ref, spread_ref, target_ref,
    left, current, right, prev_left, partial_out, partial_in, projected, mixture, outgoing, incoming,
    left_send, left_recv, prev_send, prev_recv, major_send, major_recv, minor_send, minor_recv,
    relay_send, relay_recv, right_send, right_recv, partial_send, partial_recv,
    target_send, target_recv, local_sem,
):
    q = minor_size(n)
    p = n // q
    seg, index = lax.axis_index("seg"), lax.axis_index("bond")
    major, minor = index // q, lax.rem(index, q)
    own, bond = left_ref.shape[1], left_ref.shape[2]
    wide, tall = q * own, p * own
    half = own // 2
    rows = projected.shape[1] // MPOB
    chunks = own // rows
    spans = edge_spans(bond)

    def device(hop, dm, dr):
        m, r = lax.rem(major + dm, p), lax.rem(minor + dr, q)
        return {"seg": lax.rem(seg + hop, segments), "bond": m * q + r}

    def copy(src, dst, send, recv, to):
        return pltpu.make_async_remote_copy(
            src_ref=src, dst_ref=dst, send_sem=send, recv_sem=recv, device_id=to
        )

    def slot(d):
        return lax.rem(major + d, p)

    def place(dm, dr):
        return (lax.rem(major + dm, p) * q + lax.rem(minor + dr, q)) * own

    barrier = pltpu.get_barrier_semaphore()
    peers = [device(0, d, 0) for d in range(1, p)] + [device(0, 0, d) for d in range(1, q)]
    peers += [device(hop, d, 0) for d in range(p) for hop in (1, segments - 1)]
    for peer in peers:
        pl.semaphore_signal(barrier, inc=1, device_id=peer)
    pl.semaphore_wait(barrier, len(peers))

    def left_flow(d, j, slot_index, back):
        span = pl.ds(pl.multiple_of(j * rows, rows), rows)
        return copy(
            left_ref.at[:, span, :],
            left.at[slot_index, :, span, :],
            left_send.at[d, j],
            left_recv.at[back, j],
            device(1, d, 0),
        )

    def left_out(d, j):
        return left_flow(d, j, major, (p - d) % p)

    def left_in(d, j):
        return left_flow(d, j, slot(d), d)

    def current_rows(dm, dr, h):
        return pl.ds(pl.multiple_of(place(dm, dr) + h * half, half), half)

    def source_columns(dm):
        return pl.ds(pl.multiple_of(slot(dm) * wide, wide), wide)

    prev_flow = copy(prev_left_ref, prev_left, prev_send.at[0], prev_recv.at[0], device(1, 0, 0))
    prev_flow.start()
    sends = [prev_flow]
    for h in range(2):
        source = pl.ds(h * half, half)
        for d in range(1, p):
            flow = copy(
                current_ref.at[:, source, source_columns(d)],
                current.at[:, current_rows(0, 0, h), :],
                major_send.at[d, h],
                major_recv.at[p - d, h],
                device(0, d, 0),
            )
            flow.start()
            sends.append(flow)
        for d in range(1, q):
            flow = copy(
                current_ref.at[:, source, source_columns(0)],
                current.at[:, current_rows(0, 0, h), :],
                minor_send.at[d, h],
                minor_recv.at[q - d, h],
                device(0, 0, d),
            )
            flow.start()
            sends.append(flow)
    for j in range(chunks):
        for d in range(p):
            flow = left_out(d, j)
            flow.start()
            sends.append(flow)
    locals_ = [
        pltpu.make_async_copy(
            current_ref.at[:, :, source_columns(0)],
            current.at[:, pl.ds(pl.multiple_of(place(0, 0), own), own), :],
            local_sem.at[0],
        ),
        pltpu.make_async_copy(
            right_ref, right.at[:, pl.ds(pl.multiple_of(minor * own, own), own), :], local_sem.at[1]
        ),
    ]
    for one in locals_:
        one.start()

    for h in range(2):
        for dm in range(1, p):
            landed = current.at[:, current_rows(dm, 0, h), :]
            copy(
                landed, landed, major_send.at[dm, h], major_recv.at[dm, h], device(0, dm, 0)
            ).wait_recv()
            for d in range(1, q):
                flow = copy(
                    landed, landed, relay_send.at[dm, d, h], relay_recv.at[dm, q - d, h],
                    device(0, 0, d),
                )
                flow.start()
                sends.append(flow)

    prev_flow.wait_recv()

    def contract(d, out):
        def body(step, carry):
            m, s = step // PHYS, lax.rem(step, PHYS)
            top = (m * q + lax.rem(minor + d, q)) * own
            value = jnp.dot(
                prev_left[pl.ds(pl.multiple_of(top, own), own), :],
                prev_site_ref[s],
                preferred_element_type=jnp.float32,
            )
            out[s, pl.ds(pl.multiple_of(m * own, own), own), :] = value.astype(jnp.bfloat16)
            return carry

        lax.fori_loop(0, p * PHYS, body, 0)

    for d in range(1, q):
        contract(d, partial_out.at[d - 1])
        flow = copy(
            partial_out.at[d - 1], partial_in.at[minor], partial_send.at[d],
            partial_recv.at[q - d], device(0, 0, d),
        )
        flow.start()
        sends.append(flow)

    def right_flow(d, j, row, back):
        first, width = spans[j]
        lanes = pl.ds(first, width)
        return copy(
            right_ref.at[:, :, lanes],
            right.at[:, pl.ds(pl.multiple_of(row * own, own), own), lanes],
            right_send.at[d, j],
            right_recv.at[back, j],
            device(0, 0, d),
        )

    for j in range(len(spans)):
        for d in range(1, q):
            flow = right_flow(d, j, minor, q - d)
            flow.start()
            sends.append(flow)
    contract(0, partial_in.at[minor])

    for h in range(2):
        for d in range(1, q):
            landed = current.at[:, current_rows(0, d, h), :]
            copy(
                landed, landed, minor_send.at[d, h], minor_recv.at[d, h], device(0, 0, d)
            ).wait_recv()
            for dm in range(1, p):
                landed = current.at[:, current_rows(dm, d, h), :]
                copy(
                    landed, landed, relay_send.at[dm, d, h], relay_recv.at[dm, d, h],
                    device(0, 0, d),
                ).wait_recv()
    for one in locals_:
        one.wait()

    def mix(step, carry):
        j, order = step // p, lax.rem(step, p)
        where = lax.rem(major + order, p)
        left_in(order, j).wait_recv()
        span = pl.ds(pl.multiple_of(j * rows, rows), rows)
        block = left[where, :, span, :].reshape(MPOB * rows, bond)

        def project(t, carry):
            projected[t] = jnp.dot(block, current[t], preferred_element_type=jnp.float32)
            return carry

        lax.fori_loop(0, PHYS, project, 0)

        def spread(g, carry):
            results = []
            for first in range(2):
                at = g * 2 * ROWS + first * ROWS
                stack = jnp.concatenate(
                    [
                        projected[t, pl.ds(pl.multiple_of(u * rows + at, ROWS), ROWS), :]
                        for u in range(MPOB)
                        for t in range(PHYS)
                    ],
                    axis=0,
                )
                results.append(
                    jnp.dot(
                        spread_ref[...],
                        stack.astype(jnp.bfloat16),
                        preferred_element_type=jnp.float32,
                    )
                )
            top = pl.multiple_of(where * own + j * rows + g * 2 * ROWS, 2 * ROWS)
            for v in range(MPOB):
                for s in range(PHYS):
                    first = (v * PHYS + s) * ROWS
                    both = jnp.concatenate([one[first : first + ROWS] for one in results], axis=0)
                    mixture[s, pl.ds(top, 2 * ROWS), v * wide : (v + 1) * wide] = both.astype(
                        jnp.bfloat16
                    )
            return carry

        lax.fori_loop(0, rows // (2 * ROWS), spread, 0)
        return carry

    lax.fori_loop(0, chunks * p, mix, 0)

    for d in range(1, q):
        landed = partial_in.at[lax.rem(minor + d, q)]
        copy(
            landed, landed, partial_send.at[d], partial_recv.at[d], device(0, 0, d)
        ).wait_recv()

    def products(d, j, write):
        first, width = spans[j]

        def body(s, carry):
            top = pl.ds(pl.multiple_of(slot(d) * own, own), own)
            lanes = slice(first, first + width)
            value = 2.0 * jnp.dot(
                mixture[s, top, :],
                right[:, :, lanes].reshape(MPOB * wide, width),
                preferred_element_type=jnp.float32,
            )
            for r in range(q):
                prev_rows = pl.ds(pl.multiple_of(major * wide + r * own, own), own)
                value = value - jnp.dot(
                    partial_in[r, s, top, :],
                    prev_right_ref[prev_rows, lanes],
                    preferred_element_type=jnp.float32,
                )
            write(s, lanes, value)
            return carry

        lax.fori_loop(0, PHYS, body, 0)

    def target_flow(d, j, back):
        first, width = spans[j]
        lanes = pl.ds(first, width)
        return copy(
            outgoing.at[d - 1, :, :, lanes], incoming.at[back - 1, :, :, lanes],
            target_send.at[d, j], target_recv.at[back, j], device(0, d, 0),
        )

    for j in range(len(spans)):
        for d in range(1, q):
            right_flow(d, j, lax.rem(minor + d, q), d).wait_recv()
        for d in range(1, p):

            def keep(s, lanes, value):
                outgoing[d - 1, s, :, lanes] = value.astype(jnp.bfloat16)

            products(d, j, keep)
            flow = target_flow(d, j, p - d)
            flow.start()
            sends.append(flow)

        def own_part(s, lanes, value):
            target_ref[s, :, lanes] = value

        products(0, j, own_part)
    for j, (first, width) in enumerate(spans):
        for d in range(1, p):
            target_flow(d, j, d).wait_recv()
            lanes = slice(first, first + width)

            def add(s, carry):
                target_ref[s, :, lanes] += incoming[d - 1, s, :, lanes].astype(jnp.float32)
                return carry

            lax.fori_loop(0, PHYS, add, 0)
    for flow in sends:
        flow.wait_send()


def front(left, prev_left, current, right, prev_site, prev_right, coupling):
    n, segments = lax.axis_size("bond"), lax.axis_size("seg")
    q = minor_size(n)
    p = n // q
    own, bond = left.shape[1], left.shape[2]
    wide, tall = q * own, p * own
    rows = min(LEFT_ROWS, own)
    edges = len(edge_spans(bond))
    side = MPOB * PHYS * ROWS
    diagonal = jnp.eye(ROWS, dtype=coupling.dtype)
    turned = jnp.transpose(coupling, (1, 2, 0, 3))
    spread = turned[:, :, None, :, :, None] * diagonal[None, None, :, None, None, :]
    low, full = jnp.bfloat16, jnp.float32
    whole = pl.BlockSpec(memory_space=pltpu.VMEM)
    there = pl.BlockSpec(memory_space=pl.ANY)

    def pairs(*shape):
        return [pltpu.SemaphoreType.DMA(shape)] * 2

    return pl.pallas_call(
        functools.partial(front_kernel, segments, n),
        out_shape=jax.ShapeDtypeStruct((PHYS, own, bond), full),
        in_specs=[there] * 4 + [whole] * 3,
        out_specs=whole,
        scratch_shapes=[
            pltpu.VMEM((p, MPOB, own, bond), low),
            pltpu.VMEM((PHYS, bond, wide), low),
            pltpu.VMEM((MPOB, wide, bond), low),
            pltpu.VMEM((bond, bond), low),
            pltpu.VMEM((max(q - 1, 1), PHYS, tall, own), low),
            pltpu.VMEM((q, PHYS, tall, own), low),
            pltpu.VMEM((PHYS, MPOB * rows, wide), full),
            pltpu.VMEM((PHYS, tall, MPOB * wide), low),
            pltpu.VMEM((max(p - 1, 1), PHYS, own, bond), low),
            pltpu.VMEM((max(p - 1, 1), PHYS, own, bond), low),
        ]
        + pairs(p, own // rows)
        + pairs(1)
        + pairs(p, 2)
        + pairs(q, 2)
        + pairs(p, q, 2)
        + pairs(q, edges)
        + pairs(q)
        + pairs(p, edges)
        + [pltpu.SemaphoreType.DMA((2,))],
        compiler_params=pltpu.CompilerParams(
            collective_id=1, has_side_effects=True, vmem_limit_bytes=56 * 2**20
        ),
        name="front",
    )(left, prev_left, current, right, prev_site, prev_right, spread.reshape(side, side))


def shards(left_env, prev_left, cur_site, prev_site, hamiltonian, right_env, prev_right):
    own_rows, bond_width = left_env.shape[1], left_env.shape[3]
    target = front(
        jnp.transpose(left_env[0], (1, 0, 2)),
        prev_left[0],
        jnp.transpose(cur_site[0], (1, 0, 2)),
        jnp.transpose(right_env[0], (1, 0, 2)),
        jnp.transpose(prev_site[0], (1, 0, 2)),
        prev_right[0],
        hamiltonian[0],
    ).reshape(PHYS * own_rows, bond_width)
    site, center = back(target)
    site = jnp.transpose(site.reshape(PHYS, own_rows, bond_width), (1, 0, 2))
    return (site[None], center[None])


def solution(mesh):
    return jax.shard_map(
        shards,
        mesh=mesh,
        in_specs=(
            P("seg", "bond", None, None),
            P("seg", None, None),
            P("seg", "bond", None, None),
            P("seg", None, None, "bond"),
            P("seg", None, None, None, None),
            P("seg", "bond", None, None),
            P("seg", None, None),
        ),
        out_specs=(P("seg", "bond", None, None), P("seg", "bond", None)),
        check_vma=False,
    )
```

```python
import functools
import math

import jax
import jax.numpy as jnp
from jax import lax
from jax.experimental import pallas as pl
from jax.experimental.pallas import tpu as pltpu
from jax.sharding import PartitionSpec as P

PHYS = 4
MPOB = 6
BLOCK = 128
STRIP = 256
GROUP = 4
PIECE = 64
ROWS = 8
AHEAD = 3
EDGES = 8
LEFT_ROWS = 64


def halves(x):
    high = x.astype(jnp.bfloat16)
    return high, (x - high.astype(jnp.float32)).astype(jnp.bfloat16)


def split_dot(a, b, dims):
    def dot(x, y):
        return lax.dot_general(x, y, (dims, ((), ())), preferred_element_type=jnp.float32)

    return dot(a[0], b[0]) + (dot(a[0], b[1]) + dot(a[1], b[0]))


def eliminate(block, base, rows_ref):
    height, size = block.shape
    lane = lax.broadcasted_iota(jnp.int32, (1, size), 1)
    rest = block
    top = 0
    for first in range(0, height, GROUP):
        start = first // 8 * 8
        rest, top = rest[start - top :], start
        at = first - top
        pivot = base + first
        rows = [rest[at + q : at + q + 1, :] for q in range(GROUP)]
        columns = [
            jnp.broadcast_to(rest[:, pivot + q : pivot + q + 1], rest.shape) for q in range(GROUP)
        ]
        small = [[columns[r][at + p : at + p + 1, :] for r in range(GROUP)] for p in range(GROUP)]
        change = None
        for q in range(GROUP):
            rows_ref[pl.ds(pivot + q, 1), :] = rows[q]
            inverse = 1.0 / small[q][q]
            lead = jnp.where(lane == pivot + q, 1.0, rows[q])
            for p in range(q + 1, GROUP):
                factor = small[q][p] * inverse
                for r in range(p, GROUP):
                    small[p][r] = small[p][r] - factor * small[q][r]
                rows[p] = jnp.where(lane == pivot + q, 0.0, rows[p]) - factor * lead
                columns[p] = columns[p] - factor * columns[q]
            if first + GROUP < height:
                lead = jnp.where((lane > pivot + q) & (lane < pivot + GROUP), 0.0, lead)
                term = columns[q] * (inverse * lead)
                change = term if change is None else change + term
        if first + GROUP < height:
            rest = jnp.where((lane >= pivot) & (lane < pivot + GROUP), 0.0, rest) - change


def factor_tile(block, rows_ref):
    size = block.shape[0]
    row = lax.broadcasted_iota(jnp.int32, (PIECE, size), 0)
    column = lax.broadcasted_iota(jnp.int32, (PIECE, size), 1)
    tops, inverses = [], []
    for base in range(0, size, PIECE):
        eliminate(block[:PIECE], base, rows_ref)
        done = rows_ref[base : base + PIECE, :]
        diagonal = column == row + base
        scale = lax.rsqrt(jnp.sum(jnp.where(diagonal, done, 0.0), axis=1, keepdims=True))
        scaled = done * scale
        upper = jnp.where(column >= row + base, scaled, 0.0)
        inverse = jnp.where(column < row + base, scaled, jnp.where(diagonal, scale, 0.0))
        tops.append(upper)
        inverses.append(inverse)
        if base + PIECE < size:
            right = jnp.where(column >= base + PIECE, scaled, inverse)
            change = split_dot(halves(scaled), halves(right), ((0,), (0,)))
            below = block[PIECE:]
            inside = lax.broadcasted_iota(jnp.int32, below.shape, 1)
            inside = (inside >= base) & (inside < base + PIECE)
            block = jnp.where(inside, 0.0, below) - change[base + PIECE :]
    return jnp.concatenate(tops, axis=0), jnp.concatenate(inverses, axis=0)


def back_kernel(
    n, norming, target_ref, site_ref, center_ref,
    turned, mine, theirs, work, whole_high, whole_low,
    upper, left, panel, given_high, given_low, rows_ref,
    out_send, out_recv, back_send, back_recv,
):
    me = lax.axis_index("bond")
    height, size = target_ref.shape
    blocks = size // BLOCK
    share = BLOCK // n
    peers = [lax.rem(me + d, n) for d in range(n)]
    barrier = pltpu.get_barrier_semaphore()
    for peer in peers[1:]:
        pl.semaphore_signal(barrier, inc=1, device_id={"bond": peer})
    pl.semaphore_wait(barrier, n - 1)

    def lanes_of(s):
        return pl.ds(0, (s + 1) * BLOCK)

    def rows_of(s, peer):
        return pl.ds(pl.multiple_of(s * BLOCK + peer * share, share), share)

    def outward(s, d):
        return pltpu.make_async_remote_copy(
            src_ref=mine.at[s, peers[d], :, lanes_of(s)],
            dst_ref=theirs.at[n - d - 1, s, :, lanes_of(s)],
            send_sem=out_send.at[s, d],
            recv_sem=out_recv.at[s, n - d],
            device_id={"bond": peers[d]},
        )

    def arriving(s, d):
        return pltpu.make_async_remote_copy(
            src_ref=mine.at[s, peers[d], :, lanes_of(s)],
            dst_ref=theirs.at[d - 1, s, :, lanes_of(s)],
            send_sem=out_send.at[s, d],
            recv_sem=out_recv.at[s, d],
            device_id={"bond": peers[d]},
        )

    def shared(s, d):
        here = work.at[rows_of(s, me), lanes_of(s)]
        return pltpu.make_async_remote_copy(
            src_ref=here,
            dst_ref=here,
            send_sem=back_send.at[s, d],
            recv_sem=back_recv.at[s, n - d],
            device_id={"bond": peers[d]},
        )

    def returning(s, d):
        there = work.at[rows_of(s, peers[d]), lanes_of(s)]
        return pltpu.make_async_remote_copy(
            src_ref=there,
            dst_ref=there,
            send_sem=back_send.at[s, d],
            recv_sem=back_recv.at[s, d],
            device_id={"bond": peers[d]},
        )

    def send_out(s):
        for d in range(1, n):
            outward(s, d).start()

    def reduce(s):
        last = (s + 1) * BLOCK
        for d in range(1, n):
            arriving(s, d).wait_recv()
        value = mine[s, me, :, :last]
        for d in range(1, n):
            value = value + theirs[d - 1, s, :, :last]
        work[rows_of(s, me), :last] = value
        for d in range(1, n):
            shared(s, d).start()

    def collect(s):
        for d in range(1, n):
            returning(s, d).wait_recv()

    slab = min(STRIP, height)

    per = STRIP // BLOCK
    for g in range(size // STRIP):
        turned[...] = target_ref[:, g * STRIP : (g + 1) * STRIP].T

        def correlate(c, carry):
            lanes = pl.ds(pl.multiple_of(c * STRIP, STRIP), STRIP)
            value = jnp.dot(turned[...], target_ref[:, lanes], preferred_element_type=jnp.float32)
            for b in range(per):
                part = value[b * BLOCK : (b + 1) * BLOCK, :]
                for i in range(n):
                    mine[g * per + b, i, :, lanes] = part[i * share : (i + 1) * share, :]
            return carry

        lax.fori_loop(0, g + 1, correlate, 0)
        for s in range(g * per, min((g + 1) * per, AHEAD)):
            send_out(s)
    whole_high[...] = jnp.zeros_like(whole_high)
    whole_low[...] = jnp.zeros_like(whole_low)
    left[...] = jnp.zeros_like(left)
    for s in range(min(AHEAD, blocks)):
        reduce(s)
        if s + AHEAD < blocks:
            send_out(s + AHEAD)

    full_column = lax.broadcasted_iota(jnp.int32, (BLOCK, size), 1)

    def solve_strip(g):
        lanes = slice(g * STRIP, (g + 1) * STRIP)
        depth = (g + 1) * STRIP

        def solve(i, carry):
            span = pl.ds(pl.multiple_of(i * slab, slab), slab)
            given = target_ref[span, :depth]
            value = lax.dot_general(
                given,
                whole_high[lanes, :depth],
                (((1,), (1,)), ((), ())),
                preferred_element_type=jnp.float32,
            ) + lax.dot_general(
                given,
                whole_low[lanes, :depth],
                (((1,), (1,)), ((), ())),
                preferred_element_type=jnp.float32,
            )
            site_ref[span, lanes] = (value * norming).astype(jnp.bfloat16)
            return carry

        lax.fori_loop(0, height // slab, solve, 0)

    def step(k, carry):
        for s in range(blocks):

            @pl.when(k == s)
            def _():
                collect(s)
                if s + AHEAD < blocks:
                    reduce(s + AHEAD)
                if s + 2 * AHEAD < blocks:
                    send_out(s + 2 * AHEAD)

        own = pl.ds(pl.multiple_of(k * BLOCK, BLOCK), BLOCK)
        given_high[...], given_low[...] = halves(
            jnp.where(full_column < k * BLOCK, work[own, :], 0.0)
        )

        for c in range(size // STRIP):

            @pl.when(c * per < k)
            def _():
                span, depth = slice(c * STRIP, (c + 1) * STRIP), (c + 1) * STRIP
                left[:, span] = split_dot(
                    (given_high[:, :depth], given_low[:, :depth]),
                    (whole_high[span, :depth], whole_low[span, :depth]),
                    ((1,), (1,)),
                )

        given_high[...], given_low[...] = halves(left[...])
        given = (given_high[...], given_low[...])
        panel[...] = jnp.zeros_like(panel)
        for c in range(size // STRIP):

            @pl.when(c * per < k)
            def _():
                span, depth = slice(c * STRIP, (c + 1) * STRIP), (c + 1) * STRIP
                panel[:, :depth] += split_dot(
                    (given_high[:, span], given_low[:, span]),
                    (whole_high[span, :depth], whole_low[span, :depth]),
                    ((1,), (0,)),
                )

        top, inverse = factor_tile(
            work[own, own] - split_dot(given, given, ((1,), (1,))), rows_ref
        )
        whole = split_dot(halves(-inverse), halves(panel[...]), ((1,), (0,)))
        whole_high[own, :], whole_low[own, :] = halves(whole)
        whole_high[own, own], whole_low[own, own] = halves(inverse)
        upper[:, own] = left[...].T
        upper[own, own] = top
        for g in range(size // STRIP):

            @pl.when(k == (g + 1) * per - 1)
            def _():
                solve_strip(g)

        return carry

    lax.fori_loop(0, blocks, step, 0)
    own_rows = center_ref.shape[0]
    center_ref[...] = upper[pl.ds(pl.multiple_of(me * own_rows, own_rows), own_rows), :] / norming
    for s in range(blocks):
        for d in range(1, n):
            outward(s, d).wait_send()
            shared(s, d).wait_send()


def back(target):
    n = lax.axis_size("bond")
    height, size = target.shape
    blocks, share = size // BLOCK, BLOCK // n
    norming = math.sqrt(size * PHYS)
    half, full = jnp.bfloat16, jnp.float32
    whole = pl.BlockSpec(memory_space=pltpu.VMEM)
    return pl.pallas_call(
        functools.partial(back_kernel, n, norming),
        out_shape=(
            jax.ShapeDtypeStruct((height, size), half),
            jax.ShapeDtypeStruct((size // n, size), full),
        ),
        in_specs=[whole],
        out_specs=[whole] * 2,
        scratch_shapes=[
            pltpu.VMEM((STRIP, height), half),
            pltpu.VMEM((blocks, n, share, size), full),
            pltpu.VMEM((n - 1, blocks, share, size), full),
            pltpu.VMEM((size, size), full),
            pltpu.VMEM((size, size), half),
            pltpu.VMEM((size, size), half),
            pltpu.VMEM((size, size), full),
            pltpu.VMEM((BLOCK, size), full),
            pltpu.VMEM((BLOCK, size), full),
            pltpu.VMEM((BLOCK, size), half),
            pltpu.VMEM((BLOCK, size), half),
            pltpu.VMEM((BLOCK, BLOCK), full),
        ]
        + [pltpu.SemaphoreType.DMA((blocks, n))] * 4,
        compiler_params=pltpu.CompilerParams(
            collective_id=0, has_side_effects=True, vmem_limit_bytes=56 * 2**20
        ),
        name="back",
    )(target)


def minor_size(n):
    return max(d for d in range(1, n + 1) if n % d == 0 and d * d <= n)


def edge_spans(width):
    unit = width // EDGES
    return [(j * unit, unit) for j in range(EDGES)]


def front_kernel(
    segments, n, left_ref, prev_left_ref, current_ref, right_ref,
    prev_site_ref, prev_right_ref, spread_ref, target_ref,
    left, current, right, prev_left, partial_out, partial_in, projected, mixture, outgoing, incoming,
    total,
    left_send, left_recv, prev_send, prev_recv, major_send, major_recv, minor_send, minor_recv,
    relay_send, relay_recv, right_send, right_recv, partial_send, partial_recv,
    target_send, target_recv, local_sem,
):
    q = minor_size(n)
    p = n // q
    seg, index = lax.axis_index("seg"), lax.axis_index("bond")
    major, minor = index // q, lax.rem(index, q)
    own, bond = left_ref.shape[1], left_ref.shape[2]
    wide, tall = q * own, p * own
    half = own // 2
    rows = projected.shape[1] // MPOB
    chunks = own // rows
    spans = edge_spans(bond)

    def device(hop, dm, dr):
        m, r = lax.rem(major + dm, p), lax.rem(minor + dr, q)
        return {"seg": lax.rem(seg + hop, segments), "bond": m * q + r}

    def copy(src, dst, send, recv, to):
        return pltpu.make_async_remote_copy(
            src_ref=src, dst_ref=dst, send_sem=send, recv_sem=recv, device_id=to
        )

    def slot(d):
        return lax.rem(major + d, p)

    def place(dm, dr):
        return (lax.rem(major + dm, p) * q + lax.rem(minor + dr, q)) * own

    barrier = pltpu.get_barrier_semaphore()
    peers = [device(0, d, 0) for d in range(1, p)] + [device(0, 0, d) for d in range(1, q)]
    peers += [device(hop, d, 0) for d in range(p) for hop in (1, segments - 1)]
    for peer in peers:
        pl.semaphore_signal(barrier, inc=1, device_id=peer)
    pl.semaphore_wait(barrier, len(peers))

    def left_flow(d, j, slot_index, back):
        span = pl.ds(pl.multiple_of(j * rows, rows), rows)
        return copy(
            left_ref.at[:, span, :],
            left.at[slot_index, :, span, :],
            left_send.at[d, j],
            left_recv.at[back, j],
            device(1, d, 0),
        )

    def left_out(d, j):
        return left_flow(d, j, major, (p - d) % p)

    def left_in(d, j):
        return left_flow(d, j, slot(d), d)

    def current_rows(dm, dr, h):
        return pl.ds(pl.multiple_of(place(dm, dr) + h * half, half), half)

    def source_columns(dm):
        return pl.ds(pl.multiple_of(slot(dm) * wide, wide), wide)

    prev_flow = copy(prev_left_ref, prev_left, prev_send.at[0], prev_recv.at[0], device(1, 0, 0))
    prev_flow.start()
    sends = [prev_flow]
    for h in range(2):
        source = pl.ds(h * half, half)
        for d in range(1, p):
            flow = copy(
                current_ref.at[:, source, source_columns(d)],
                current.at[:, current_rows(0, 0, h), :],
                major_send.at[d, h],
                major_recv.at[p - d, h],
                device(0, d, 0),
            )
            flow.start()
            sends.append(flow)
        for d in range(1, q):
            flow = copy(
                current_ref.at[:, source, source_columns(0)],
                current.at[:, current_rows(0, 0, h), :],
                minor_send.at[d, h],
                minor_recv.at[q - d, h],
                device(0, 0, d),
            )
            flow.start()
            sends.append(flow)
    for j in range(chunks):
        for d in range(p):
            flow = left_out(d, j)
            flow.start()
            sends.append(flow)
    locals_ = [
        pltpu.make_async_copy(
            current_ref.at[:, :, source_columns(0)],
            current.at[:, pl.ds(pl.multiple_of(place(0, 0), own), own), :],
            local_sem.at[0],
        ),
        pltpu.make_async_copy(
            right_ref, right.at[:, pl.ds(pl.multiple_of(minor * own, own), own), :], local_sem.at[1]
        ),
    ]
    for one in locals_:
        one.start()

    for h in range(2):
        for dm in range(1, p):
            landed = current.at[:, current_rows(dm, 0, h), :]
            copy(
                landed, landed, major_send.at[dm, h], major_recv.at[dm, h], device(0, dm, 0)
            ).wait_recv()
            for d in range(1, q):
                flow = copy(
                    landed, landed, relay_send.at[dm, d, h], relay_recv.at[dm, q - d, h],
                    device(0, 0, d),
                )
                flow.start()
                sends.append(flow)

    prev_flow.wait_recv()

    def contract(d, out):
        def body(step, carry):
            m, s = step // PHYS, lax.rem(step, PHYS)
            top = (m * q + lax.rem(minor + d, q)) * own
            value = jnp.dot(
                prev_left[pl.ds(pl.multiple_of(top, own), own), :],
                prev_site_ref[s],
                preferred_element_type=jnp.float32,
            )
            out[s, pl.ds(pl.multiple_of(m * own, own), own), :] = value.astype(jnp.bfloat16)
            return carry

        lax.fori_loop(0, p * PHYS, body, 0)

    for d in range(1, q):
        contract(d, partial_out.at[d - 1])
        flow = copy(
            partial_out.at[d - 1], partial_in.at[minor], partial_send.at[d],
            partial_recv.at[q - d], device(0, 0, d),
        )
        flow.start()
        sends.append(flow)

    def right_flow(d, j, row, back):
        first, width = spans[j]
        lanes = pl.ds(first, width)
        return copy(
            right_ref.at[:, :, lanes],
            right.at[:, pl.ds(pl.multiple_of(row * own, own), own), lanes],
            right_send.at[d, j],
            right_recv.at[back, j],
            device(0, 0, d),
        )

    for j in range(len(spans)):
        for d in range(1, q):
            flow = right_flow(d, j, minor, q - d)
            flow.start()
            sends.append(flow)
    contract(0, partial_in.at[minor])

    for h in range(2):
        for d in range(1, q):
            landed = current.at[:, current_rows(0, d, h), :]
            copy(
                landed, landed, minor_send.at[d, h], minor_recv.at[d, h], device(0, 0, d)
            ).wait_recv()
            for dm in range(1, p):
                landed = current.at[:, current_rows(dm, d, h), :]
                copy(
                    landed, landed, relay_send.at[dm, d, h], relay_recv.at[dm, d, h],
                    device(0, 0, d),
                ).wait_recv()
    for one in locals_:
        one.wait()

    def mix(step, carry):
        j, order = step // p, lax.rem(step, p)
        where = lax.rem(major + order, p)
        left_in(order, j).wait_recv()
        span = pl.ds(pl.multiple_of(j * rows, rows), rows)
        block = left[where, :, span, :].reshape(MPOB * rows, bond)

        def project(t, carry):
            projected[t] = jnp.dot(block, current[t], preferred_element_type=jnp.float32)
            return carry

        lax.fori_loop(0, PHYS, project, 0)

        def spread(g, carry):
            results = []
            for first in range(2):
                at = g * 2 * ROWS + first * ROWS
                stack = jnp.concatenate(
                    [
                        projected[t, pl.ds(pl.multiple_of(u * rows + at, ROWS), ROWS), :]
                        for u in range(MPOB)
                        for t in range(PHYS)
                    ],
                    axis=0,
                )
                results.append(
                    jnp.dot(
                        spread_ref[...],
                        stack.astype(jnp.bfloat16),
                        preferred_element_type=jnp.float32,
                    )
                )
            top = pl.multiple_of(where * own + j * rows + g * 2 * ROWS, 2 * ROWS)
            for v in range(MPOB):
                for s in range(PHYS):
                    first = (v * PHYS + s) * ROWS
                    both = jnp.concatenate([one[first : first + ROWS] for one in results], axis=0)
                    mixture[s, pl.ds(top, 2 * ROWS), v * wide : (v + 1) * wide] = both.astype(
                        jnp.bfloat16
                    )
            return carry

        lax.fori_loop(0, rows // (2 * ROWS), spread, 0)
        return carry

    lax.fori_loop(0, chunks * p, mix, 0)

    for d in range(1, q):
        landed = partial_in.at[lax.rem(minor + d, q)]
        copy(
            landed, landed, partial_send.at[d], partial_recv.at[d], device(0, 0, d)
        ).wait_recv()

    def products(d, j, write):
        first, width = spans[j]

        def body(s, carry):
            top = pl.ds(pl.multiple_of(slot(d) * own, own), own)
            lanes = slice(first, first + width)
            value = 2.0 * jnp.dot(
                mixture[s, top, :],
                right[:, :, lanes].reshape(MPOB * wide, width),
                preferred_element_type=jnp.float32,
            )
            for r in range(q):
                prev_rows = pl.ds(pl.multiple_of(major * wide + r * own, own), own)
                value = value - jnp.dot(
                    partial_in[r, s, top, :],
                    prev_right_ref[prev_rows, lanes],
                    preferred_element_type=jnp.float32,
                )
            write(s, lanes, value)
            return carry

        lax.fori_loop(0, PHYS, body, 0)

    def target_flow(d, j, back):
        first, width = spans[j]
        lanes = pl.ds(first, width)
        return copy(
            outgoing.at[d - 1, :, :, lanes], incoming.at[back - 1, :, :, lanes],
            target_send.at[d, j], target_recv.at[back, j], device(0, d, 0),
        )

    for j in range(len(spans)):
        for d in range(1, q):
            right_flow(d, j, lax.rem(minor + d, q), d).wait_recv()
        for d in range(1, p):

            def keep(s, lanes, value):
                outgoing[d - 1, s, :, lanes] = value.astype(jnp.bfloat16)

            products(d, j, keep)
            flow = target_flow(d, j, p - d)
            flow.start()
            sends.append(flow)

        def own_part(s, lanes, value):
            total[s, :, lanes] = value

        products(0, j, own_part)
    for j, (first, width) in enumerate(spans):
        for d in range(1, p):
            target_flow(d, j, d).wait_recv()
        lanes = slice(first, first + width)

        def add(s, carry):
            value = total[s, :, lanes]
            for d in range(1, p):
                value = value + incoming[d - 1, s, :, lanes].astype(jnp.float32)
            target_ref[s, :, lanes] = value.astype(jnp.bfloat16)
            return carry

        lax.fori_loop(0, PHYS, add, 0)
    for flow in sends:
        flow.wait_send()


def front(left, prev_left, current, right, prev_site, prev_right, coupling):
    n, segments = lax.axis_size("bond"), lax.axis_size("seg")
    q = minor_size(n)
    p = n // q
    own, bond = left.shape[1], left.shape[2]
    wide, tall = q * own, p * own
    rows = min(LEFT_ROWS, own)
    edges = len(edge_spans(bond))
    side = MPOB * PHYS * ROWS
    diagonal = jnp.eye(ROWS, dtype=coupling.dtype)
    turned = jnp.transpose(coupling, (1, 2, 0, 3))
    spread = turned[:, :, None, :, :, None] * diagonal[None, None, :, None, None, :]
    low, full = jnp.bfloat16, jnp.float32
    whole = pl.BlockSpec(memory_space=pltpu.VMEM)
    there = pl.BlockSpec(memory_space=pl.ANY)

    def pairs(*shape):
        return [pltpu.SemaphoreType.DMA(shape)] * 2

    return pl.pallas_call(
        functools.partial(front_kernel, segments, n),
        out_shape=jax.ShapeDtypeStruct((PHYS, own, bond), low),
        in_specs=[there] * 4 + [whole] * 3,
        out_specs=whole,
        scratch_shapes=[
            pltpu.VMEM((p, MPOB, own, bond), low),
            pltpu.VMEM((PHYS, bond, wide), low),
            pltpu.VMEM((MPOB, wide, bond), low),
            pltpu.VMEM((bond, bond), low),
            pltpu.VMEM((max(q - 1, 1), PHYS, tall, own), low),
            pltpu.VMEM((q, PHYS, tall, own), low),
            pltpu.VMEM((PHYS, MPOB * rows, wide), full),
            pltpu.VMEM((PHYS, tall, MPOB * wide), low),
            pltpu.VMEM((max(p - 1, 1), PHYS, own, bond), low),
            pltpu.VMEM((max(p - 1, 1), PHYS, own, bond), low),
            pltpu.VMEM((PHYS, own, bond), full),
        ]
        + pairs(p, own // rows)
        + pairs(1)
        + pairs(p, 2)
        + pairs(q, 2)
        + pairs(p, q, 2)
        + pairs(q, edges)
        + pairs(q)
        + pairs(p, edges)
        + [pltpu.SemaphoreType.DMA((2,))],
        compiler_params=pltpu.CompilerParams(
            collective_id=1, has_side_effects=True, vmem_limit_bytes=56 * 2**20
        ),
        name="front",
    )(left, prev_left, current, right, prev_site, prev_right, spread.reshape(side, side))


def shards(left_env, prev_left, cur_site, prev_site, hamiltonian, right_env, prev_right):
    own_rows, bond_width = left_env.shape[1], left_env.shape[3]
    target = front(
        jnp.transpose(left_env[0], (1, 0, 2)),
        prev_left[0],
        jnp.transpose(cur_site[0], (1, 0, 2)),
        jnp.transpose(right_env[0], (1, 0, 2)),
        jnp.transpose(prev_site[0], (1, 0, 2)),
        prev_right[0],
        hamiltonian[0],
    ).reshape(PHYS * own_rows, bond_width)
    site, center = back(target)
    site = jnp.transpose(site.reshape(PHYS, own_rows, bond_width), (1, 0, 2))
    return (site[None], center[None])


def solution(mesh):
    return jax.shard_map(
        shards,
        mesh=mesh,
        in_specs=(
            P("seg", "bond", None, None),
            P("seg", None, None),
            P("seg", "bond", None, None),
            P("seg", None, None, "bond"),
            P("seg", None, None, None, None),
            P("seg", "bond", None, None),
            P("seg", None, None),
        ),
        out_specs=(P("seg", "bond", None, None), P("seg", "bond", None)),
        check_vma=False,
    )
```

```python
import functools
import math

import jax
import jax.numpy as jnp
from jax import lax
from jax.experimental import pallas as pl
from jax.experimental.pallas import tpu as pltpu
from jax.sharding import PartitionSpec as P

PHYS = 4
MPOB = 6
BLOCK = 128
STRIP = 256
GROUP = 8
PIECE = 64
ROWS = 8
AHEAD = 3
EDGES = 8
LEFT_ROWS = 64


def halves(x):
    high = x.astype(jnp.bfloat16)
    return high, (x - high.astype(jnp.float32)).astype(jnp.bfloat16)


def split_dot(a, b, dims):
    def dot(x, y):
        return lax.dot_general(x, y, (dims, ((), ())), preferred_element_type=jnp.float32)

    return dot(a[0], b[0]) + (dot(a[0], b[1]) + dot(a[1], b[0]))


def eliminate(block, base, rows_ref):
    height, size = block.shape
    lane = lax.broadcasted_iota(jnp.int32, (1, size), 1)
    rest = block
    top = 0
    for first in range(0, height, GROUP):
        start = first // 8 * 8
        rest, top = rest[start - top :], start
        at = first - top
        pivot = base + first
        rows = [rest[at + q : at + q + 1, :] for q in range(GROUP)]
        columns = [
            jnp.broadcast_to(rest[:, pivot + q : pivot + q + 1], rest.shape) for q in range(GROUP)
        ]
        small = [[columns[r][at + p : at + p + 1, :] for r in range(GROUP)] for p in range(GROUP)]
        change = None
        for q in range(GROUP):
            rows_ref[pl.ds(pivot + q, 1), :] = rows[q]
            inverse = 1.0 / small[q][q]
            lead = jnp.where(lane == pivot + q, 1.0, rows[q])
            for p in range(q + 1, GROUP):
                factor = small[q][p] * inverse
                for r in range(p, GROUP):
                    small[p][r] = small[p][r] - factor * small[q][r]
                rows[p] = jnp.where(lane == pivot + q, 0.0, rows[p]) - factor * lead
                columns[p] = columns[p] - factor * columns[q]
            if first + GROUP < height:
                lead = jnp.where((lane > pivot + q) & (lane < pivot + GROUP), 0.0, lead)
                term = columns[q] * (inverse * lead)
                change = term if change is None else change + term
        if first + GROUP < height:
            rest = jnp.where((lane >= pivot) & (lane < pivot + GROUP), 0.0, rest) - change


def factor_tile(block, rows_ref):
    size = block.shape[0]
    row = lax.broadcasted_iota(jnp.int32, (PIECE, size), 0)
    column = lax.broadcasted_iota(jnp.int32, (PIECE, size), 1)
    tops, inverses = [], []
    for base in range(0, size, PIECE):
        eliminate(block[:PIECE], base, rows_ref)
        done = rows_ref[base : base + PIECE, :]
        diagonal = column == row + base
        scale = lax.rsqrt(jnp.sum(jnp.where(diagonal, done, 0.0), axis=1, keepdims=True))
        scaled = done * scale
        upper = jnp.where(column >= row + base, scaled, 0.0)
        inverse = jnp.where(column < row + base, scaled, jnp.where(diagonal, scale, 0.0))
        tops.append(upper)
        inverses.append(inverse)
        if base + PIECE < size:
            right = jnp.where(column >= base + PIECE, scaled, inverse)
            change = split_dot(halves(scaled), halves(right), ((0,), (0,)))
            below = block[PIECE:]
            inside = lax.broadcasted_iota(jnp.int32, below.shape, 1)
            inside = (inside >= base) & (inside < base + PIECE)
            block = jnp.where(inside, 0.0, below) - change[base + PIECE :]
    return jnp.concatenate(tops, axis=0), jnp.concatenate(inverses, axis=0)


def back_kernel(
    n, norming, target_ref, site_ref, center_ref,
    turned, mine, theirs, work, whole_high, whole_low,
    upper, left, panel, given_high, given_low, rows_ref,
    out_send, out_recv, back_send, back_recv,
):
    me = lax.axis_index("bond")
    height, size = target_ref.shape
    blocks = size // BLOCK
    share = BLOCK // n
    peers = [lax.rem(me + d, n) for d in range(n)]
    barrier = pltpu.get_barrier_semaphore()
    for peer in peers[1:]:
        pl.semaphore_signal(barrier, inc=1, device_id={"bond": peer})
    pl.semaphore_wait(barrier, n - 1)

    def lanes_of(s):
        return pl.ds(0, (s + 1) * BLOCK)

    def rows_of(s, peer):
        return pl.ds(pl.multiple_of(s * BLOCK + peer * share, share), share)

    def outward(s, d):
        return pltpu.make_async_remote_copy(
            src_ref=mine.at[s, peers[d], :, lanes_of(s)],
            dst_ref=theirs.at[n - d - 1, s, :, lanes_of(s)],
            send_sem=out_send.at[s, d],
            recv_sem=out_recv.at[s, n - d],
            device_id={"bond": peers[d]},
        )

    def arriving(s, d):
        return pltpu.make_async_remote_copy(
            src_ref=mine.at[s, peers[d], :, lanes_of(s)],
            dst_ref=theirs.at[d - 1, s, :, lanes_of(s)],
            send_sem=out_send.at[s, d],
            recv_sem=out_recv.at[s, d],
            device_id={"bond": peers[d]},
        )

    def shared(s, d):
        here = work.at[rows_of(s, me), lanes_of(s)]
        return pltpu.make_async_remote_copy(
            src_ref=here,
            dst_ref=here,
            send_sem=back_send.at[s, d],
            recv_sem=back_recv.at[s, n - d],
            device_id={"bond": peers[d]},
        )

    def returning(s, d):
        there = work.at[rows_of(s, peers[d]), lanes_of(s)]
        return pltpu.make_async_remote_copy(
            src_ref=there,
            dst_ref=there,
            send_sem=back_send.at[s, d],
            recv_sem=back_recv.at[s, d],
            device_id={"bond": peers[d]},
        )

    def send_out(s):
        for d in range(1, n):
            outward(s, d).start()

    def reduce(s):
        last = (s + 1) * BLOCK
        for d in range(1, n):
            arriving(s, d).wait_recv()
        value = mine[s, me, :, :last]
        for d in range(1, n):
            value = value + theirs[d - 1, s, :, :last]
        work[rows_of(s, me), :last] = value
        for d in range(1, n):
            shared(s, d).start()

    def collect(s):
        for d in range(1, n):
            returning(s, d).wait_recv()

    per = STRIP // BLOCK
    for g in range(size // STRIP):
        turned[...] = target_ref[:, g * STRIP : (g + 1) * STRIP].T

        def correlate(c, carry):
            lanes = pl.ds(pl.multiple_of(c * STRIP, STRIP), STRIP)
            value = jnp.dot(turned[...], target_ref[:, lanes], preferred_element_type=jnp.float32)
            for b in range(per):
                part = value[b * BLOCK : (b + 1) * BLOCK, :]
                for i in range(n):
                    mine[g * per + b, i, :, lanes] = part[i * share : (i + 1) * share, :]
            return carry

        lax.fori_loop(0, g + 1, correlate, 0)
        for s in range(g * per, min((g + 1) * per, AHEAD)):
            send_out(s)
    whole_high[...] = jnp.zeros_like(whole_high)
    whole_low[...] = jnp.zeros_like(whole_low)
    left[...] = jnp.zeros_like(left)
    for s in range(min(AHEAD, blocks)):
        reduce(s)
        if s + AHEAD < blocks:
            send_out(s + AHEAD)

    full_column = lax.broadcasted_iota(jnp.int32, (BLOCK, size), 1)

    def solve_block(k):
        own = pl.ds(pl.multiple_of(k * BLOCK, BLOCK), BLOCK)
        dims = (((1,), (1,)), ((), ()))
        target = target_ref[...]
        value = lax.dot_general(
            target, whole_high[own, :], dims, preferred_element_type=jnp.float32
        ) + lax.dot_general(target, whole_low[own, :], dims, preferred_element_type=jnp.float32)
        site_ref[:, own] = (value * norming).astype(jnp.bfloat16)

    def step(k, carry):
        for s in range(blocks):

            @pl.when(k == s)
            def _():
                collect(s)
                if s + AHEAD < blocks:
                    reduce(s + AHEAD)
                if s + 2 * AHEAD < blocks:
                    send_out(s + 2 * AHEAD)

        own = pl.ds(pl.multiple_of(k * BLOCK, BLOCK), BLOCK)
        given_high[...], given_low[...] = halves(
            jnp.where(full_column < k * BLOCK, work[own, :], 0.0)
        )

        for c in range(size // STRIP):

            @pl.when(c * per < k)
            def _():
                span, depth = slice(c * STRIP, (c + 1) * STRIP), (c + 1) * STRIP
                left[:, span] = split_dot(
                    (given_high[:, :depth], given_low[:, :depth]),
                    (whole_high[span, :depth], whole_low[span, :depth]),
                    ((1,), (1,)),
                )

        given_high[...], given_low[...] = halves(left[...])
        given = (given_high[...], given_low[...])
        panel[...] = split_dot(given, (whole_high[...], whole_low[...]), ((1,), (0,)))
        solve_block(jnp.maximum(k - 1, 0))
        upper[:, own] = left[...].T
        top, inverse = factor_tile(
            work[own, own] - split_dot(given, given, ((1,), (1,))), rows_ref
        )
        whole = split_dot(halves(-inverse), halves(panel[...]), ((1,), (0,)))
        whole_high[own, :], whole_low[own, :] = halves(whole)
        whole_high[own, own], whole_low[own, own] = halves(inverse)
        upper[own, own] = top
        return carry

    lax.fori_loop(0, blocks, step, 0)
    solve_block(blocks - 1)
    own_rows = center_ref.shape[0]
    center_ref[...] = upper[pl.ds(pl.multiple_of(me * own_rows, own_rows), own_rows), :] / norming
    for s in range(blocks):
        for d in range(1, n):
            outward(s, d).wait_send()
            shared(s, d).wait_send()


def back(target):
    n = lax.axis_size("bond")
    height, size = target.shape
    blocks, share = size // BLOCK, BLOCK // n
    norming = math.sqrt(size * PHYS)
    half, full = jnp.bfloat16, jnp.float32
    whole = pl.BlockSpec(memory_space=pltpu.VMEM)
    return pl.pallas_call(
        functools.partial(back_kernel, n, norming),
        out_shape=(
            jax.ShapeDtypeStruct((height, size), half),
            jax.ShapeDtypeStruct((size // n, size), full),
        ),
        in_specs=[whole],
        out_specs=[whole] * 2,
        scratch_shapes=[
            pltpu.VMEM((STRIP, height), half),
            pltpu.VMEM((blocks, n, share, size), full),
            pltpu.VMEM((n - 1, blocks, share, size), full),
            pltpu.VMEM((size, size), full),
            pltpu.VMEM((size, size), half),
            pltpu.VMEM((size, size), half),
            pltpu.VMEM((size, size), full),
            pltpu.VMEM((BLOCK, size), full),
            pltpu.VMEM((BLOCK, size), full),
            pltpu.VMEM((BLOCK, size), half),
            pltpu.VMEM((BLOCK, size), half),
            pltpu.VMEM((BLOCK, BLOCK), full),
        ]
        + [pltpu.SemaphoreType.DMA((blocks, n))] * 4,
        compiler_params=pltpu.CompilerParams(
            collective_id=0, has_side_effects=True, vmem_limit_bytes=36 * 2**20
        ),
        name="back",
    )(target)


def minor_size(n):
    return max(d for d in range(1, n + 1) if n % d == 0 and d * d <= n)


def edge_spans(width):
    unit = width // EDGES
    return [(j * unit, unit) for j in range(EDGES)]


def front_kernel(
    segments, n, left_ref, prev_left_ref, current_ref, right_ref,
    prev_site_ref, prev_right_ref, spread_ref, target_ref,
    left, current, right, prev_left, partial_out, partial_in, projected, mixture, outgoing, incoming,
    total,
    left_send, left_recv, prev_send, prev_recv, major_send, major_recv, minor_send, minor_recv,
    relay_send, relay_recv, right_send, right_recv, partial_send, partial_recv,
    target_send, target_recv, local_sem,
):
    q = minor_size(n)
    p = n // q
    seg, index = lax.axis_index("seg"), lax.axis_index("bond")
    major, minor = index // q, lax.rem(index, q)
    own, bond = left_ref.shape[1], left_ref.shape[2]
    wide, tall = q * own, p * own
    half = own // 2
    rows = projected.shape[1] // MPOB
    chunks = own // rows
    spans = edge_spans(bond)

    def device(hop, dm, dr):
        m, r = lax.rem(major + dm, p), lax.rem(minor + dr, q)
        return {"seg": lax.rem(seg + hop, segments), "bond": m * q + r}

    def copy(src, dst, send, recv, to):
        return pltpu.make_async_remote_copy(
            src_ref=src, dst_ref=dst, send_sem=send, recv_sem=recv, device_id=to
        )

    def slot(d):
        return lax.rem(major + d, p)

    def place(dm, dr):
        return (lax.rem(major + dm, p) * q + lax.rem(minor + dr, q)) * own

    barrier = pltpu.get_barrier_semaphore()
    peers = [device(0, d, 0) for d in range(1, p)] + [device(0, 0, d) for d in range(1, q)]
    peers += [device(hop, d, 0) for d in range(p) for hop in (1, segments - 1)]
    for peer in peers:
        pl.semaphore_signal(barrier, inc=1, device_id=peer)
    pl.semaphore_wait(barrier, len(peers))

    def left_flow(d, j, slot_index, back):
        span = pl.ds(pl.multiple_of(j * rows, rows), rows)
        return copy(
            left_ref.at[:, span, :],
            left.at[slot_index, :, span, :],
            left_send.at[d, j],
            left_recv.at[back, j],
            device(1, d, 0),
        )

    def left_out(d, j):
        return left_flow(d, j, major, (p - d) % p)

    def left_in(d, j):
        return left_flow(d, j, slot(d), d)

    def current_rows(dm, dr, h):
        return pl.ds(pl.multiple_of(place(dm, dr) + h * half, half), half)

    def source_columns(dm):
        return pl.ds(pl.multiple_of(slot(dm) * wide, wide), wide)

    prev_flow = copy(prev_left_ref, prev_left, prev_send.at[0], prev_recv.at[0], device(1, 0, 0))
    prev_flow.start()
    sends = [prev_flow]
    for h in range(2):
        source = pl.ds(h * half, half)
        for d in range(1, p):
            flow = copy(
                current_ref.at[:, source, source_columns(d)],
                current.at[:, current_rows(0, 0, h), :],
                major_send.at[d, h],
                major_recv.at[p - d, h],
                device(0, d, 0),
            )
            flow.start()
            sends.append(flow)
        for d in range(1, q):
            flow = copy(
                current_ref.at[:, source, source_columns(0)],
                current.at[:, current_rows(0, 0, h), :],
                minor_send.at[d, h],
                minor_recv.at[q - d, h],
                device(0, 0, d),
            )
            flow.start()
            sends.append(flow)
    for j in range(chunks):
        for d in range(p):
            flow = left_out(d, j)
            flow.start()
            sends.append(flow)
    locals_ = [
        pltpu.make_async_copy(
            current_ref.at[:, :, source_columns(0)],
            current.at[:, pl.ds(pl.multiple_of(place(0, 0), own), own), :],
            local_sem.at[0],
        ),
        pltpu.make_async_copy(
            right_ref, right.at[:, pl.ds(pl.multiple_of(minor * own, own), own), :], local_sem.at[1]
        ),
    ]
    for one in locals_:
        one.start()

    for h in range(2):
        for dm in range(1, p):
            landed = current.at[:, current_rows(dm, 0, h), :]
            copy(
                landed, landed, major_send.at[dm, h], major_recv.at[dm, h], device(0, dm, 0)
            ).wait_recv()
            for d in range(1, q):
                flow = copy(
                    landed, landed, relay_send.at[dm, d, h], relay_recv.at[dm, q - d, h],
                    device(0, 0, d),
                )
                flow.start()
                sends.append(flow)

    prev_flow.wait_recv()

    def contract(d, out):
        def body(step, carry):
            m, s = step // PHYS, lax.rem(step, PHYS)
            top = (m * q + lax.rem(minor + d, q)) * own
            value = jnp.dot(
                prev_left[pl.ds(pl.multiple_of(top, own), own), :],
                prev_site_ref[s],
                preferred_element_type=jnp.float32,
            )
            out[s, pl.ds(pl.multiple_of(m * own, own), own), :] = value.astype(jnp.bfloat16)
            return carry

        lax.fori_loop(0, p * PHYS, body, 0)

    for d in range(1, q):
        contract(d, partial_out.at[d - 1])
        flow = copy(
            partial_out.at[d - 1], partial_in.at[minor], partial_send.at[d],
            partial_recv.at[q - d], device(0, 0, d),
        )
        flow.start()
        sends.append(flow)

    def right_flow(d, j, row, back):
        first, width = spans[j]
        lanes = pl.ds(first, width)
        return copy(
            right_ref.at[:, :, lanes],
            right.at[:, pl.ds(pl.multiple_of(row * own, own), own), lanes],
            right_send.at[d, j],
            right_recv.at[back, j],
            device(0, 0, d),
        )

    for j in range(len(spans)):
        for d in range(1, q):
            flow = right_flow(d, j, minor, q - d)
            flow.start()
            sends.append(flow)
    contract(0, partial_in.at[minor])

    for h in range(2):
        for d in range(1, q):
            landed = current.at[:, current_rows(0, d, h), :]
            copy(
                landed, landed, minor_send.at[d, h], minor_recv.at[d, h], device(0, 0, d)
            ).wait_recv()
            for dm in range(1, p):
                landed = current.at[:, current_rows(dm, d, h), :]
                copy(
                    landed, landed, relay_send.at[dm, d, h], relay_recv.at[dm, d, h],
                    device(0, 0, d),
                ).wait_recv()
    for one in locals_:
        one.wait()

    def mix(step, carry):
        j, order = step // p, lax.rem(step, p)
        where = lax.rem(major + order, p)
        left_in(order, j).wait_recv()
        span = pl.ds(pl.multiple_of(j * rows, rows), rows)
        block = left[where, :, span, :].reshape(MPOB * rows, bond)

        def project(t, carry):
            projected[t] = jnp.dot(block, current[t], preferred_element_type=jnp.float32)
            return carry

        lax.fori_loop(0, PHYS, project, 0)

        def spread(g, carry):
            results = []
            for first in range(2):
                at = g * 2 * ROWS + first * ROWS
                stack = jnp.concatenate(
                    [
                        projected[t, pl.ds(pl.multiple_of(u * rows + at, ROWS), ROWS), :]
                        for u in range(MPOB)
                        for t in range(PHYS)
                    ],
                    axis=0,
                )
                results.append(
                    jnp.dot(
                        spread_ref[...],
                        stack.astype(jnp.bfloat16),
                        preferred_element_type=jnp.float32,
                    )
                )
            top = pl.multiple_of(where * own + j * rows + g * 2 * ROWS, 2 * ROWS)
            for v in range(MPOB):
                for s in range(PHYS):
                    first = (v * PHYS + s) * ROWS
                    both = jnp.concatenate([one[first : first + ROWS] for one in results], axis=0)
                    mixture[s, pl.ds(top, 2 * ROWS), v * wide : (v + 1) * wide] = both.astype(
                        jnp.bfloat16
                    )
            return carry

        lax.fori_loop(0, rows // (2 * ROWS), spread, 0)
        return carry

    lax.fori_loop(0, chunks * p, mix, 0)

    for d in range(1, q):
        landed = partial_in.at[lax.rem(minor + d, q)]
        copy(
            landed, landed, partial_send.at[d], partial_recv.at[d], device(0, 0, d)
        ).wait_recv()

    def products(d, j, write):
        first, width = spans[j]

        def body(s, carry):
            top = pl.ds(pl.multiple_of(slot(d) * own, own), own)
            lanes = slice(first, first + width)
            value = 2.0 * jnp.dot(
                mixture[s, top, :],
                right[:, :, lanes].reshape(MPOB * wide, width),
                preferred_element_type=jnp.float32,
            )
            for r in range(q):
                prev_rows = pl.ds(pl.multiple_of(major * wide + r * own, own), own)
                value = value - jnp.dot(
                    partial_in[r, s, top, :],
                    prev_right_ref[prev_rows, lanes],
                    preferred_element_type=jnp.float32,
                )
            write(s, lanes, value)
            return carry

        lax.fori_loop(0, PHYS, body, 0)

    def target_flow(d, j, back):
        first, width = spans[j]
        lanes = pl.ds(first, width)
        return copy(
            outgoing.at[d - 1, :, :, lanes], incoming.at[back - 1, :, :, lanes],
            target_send.at[d, j], target_recv.at[back, j], device(0, d, 0),
        )

    for j in range(len(spans)):
        for d in range(1, q):
            right_flow(d, j, lax.rem(minor + d, q), d).wait_recv()
        for d in range(1, p):

            def keep(s, lanes, value):
                outgoing[d - 1, s, :, lanes] = value.astype(jnp.bfloat16)

            products(d, j, keep)
            flow = target_flow(d, j, p - d)
            flow.start()
            sends.append(flow)

        def own_part(s, lanes, value):
            total[s, :, lanes] = value

        products(0, j, own_part)
    for j, (first, width) in enumerate(spans):
        for d in range(1, p):
            target_flow(d, j, d).wait_recv()
        lanes = slice(first, first + width)

        def add(s, carry):
            value = total[s, :, lanes]
            for d in range(1, p):
                value = value + incoming[d - 1, s, :, lanes].astype(jnp.float32)
            target_ref[s, :, lanes] = value.astype(jnp.bfloat16)
            return carry

        lax.fori_loop(0, PHYS, add, 0)
    for flow in sends:
        flow.wait_send()


def front(left, prev_left, current, right, prev_site, prev_right, coupling):
    n, segments = lax.axis_size("bond"), lax.axis_size("seg")
    q = minor_size(n)
    p = n // q
    own, bond = left.shape[1], left.shape[2]
    wide, tall = q * own, p * own
    rows = min(LEFT_ROWS, own)
    edges = len(edge_spans(bond))
    side = MPOB * PHYS * ROWS
    diagonal = jnp.eye(ROWS, dtype=coupling.dtype)
    turned = jnp.transpose(coupling, (1, 2, 0, 3))
    spread = turned[:, :, None, :, :, None] * diagonal[None, None, :, None, None, :]
    low, full = jnp.bfloat16, jnp.float32
    whole = pl.BlockSpec(memory_space=pltpu.VMEM)
    there = pl.BlockSpec(memory_space=pl.ANY)

    def pairs(*shape):
        return [pltpu.SemaphoreType.DMA(shape)] * 2

    return pl.pallas_call(
        functools.partial(front_kernel, segments, n),
        out_shape=jax.ShapeDtypeStruct((PHYS, own, bond), low),
        in_specs=[there] * 4 + [whole] * 3,
        out_specs=whole,
        scratch_shapes=[
            pltpu.VMEM((p, MPOB, own, bond), low),
            pltpu.VMEM((PHYS, bond, wide), low),
            pltpu.VMEM((MPOB, wide, bond), low),
            pltpu.VMEM((bond, bond), low),
            pltpu.VMEM((max(q - 1, 1), PHYS, tall, own), low),
            pltpu.VMEM((q, PHYS, tall, own), low),
            pltpu.VMEM((PHYS, MPOB * rows, wide), full),
            pltpu.VMEM((PHYS, tall, MPOB * wide), low),
            pltpu.VMEM((max(p - 1, 1), PHYS, own, bond), low),
            pltpu.VMEM((max(p - 1, 1), PHYS, own, bond), low),
            pltpu.VMEM((PHYS, own, bond), full),
        ]
        + pairs(p, own // rows)
        + pairs(1)
        + pairs(p, 2)
        + pairs(q, 2)
        + pairs(p, q, 2)
        + pairs(q, edges)
        + pairs(q)
        + pairs(p, edges)
        + [pltpu.SemaphoreType.DMA((2,))],
        compiler_params=pltpu.CompilerParams(
            collective_id=1, has_side_effects=True, vmem_limit_bytes=56 * 2**20
        ),
        name="front",
    )(left, prev_left, current, right, prev_site, prev_right, spread.reshape(side, side))


def shards(left_env, prev_left, cur_site, prev_site, hamiltonian, right_env, prev_right):
    own_rows, bond_width = left_env.shape[1], left_env.shape[3]
    target = front(
        jnp.transpose(left_env[0], (1, 0, 2)),
        prev_left[0],
        jnp.transpose(cur_site[0], (1, 0, 2)),
        jnp.transpose(right_env[0], (1, 0, 2)),
        jnp.transpose(prev_site[0], (1, 0, 2)),
        prev_right[0],
        hamiltonian[0],
    ).reshape(PHYS * own_rows, bond_width)
    site, center = back(target)
    site = jnp.transpose(site.reshape(PHYS, own_rows, bond_width), (1, 0, 2))
    return (site[None], center[None])


def solution(mesh):
    return jax.shard_map(
        shards,
        mesh=mesh,
        in_specs=(
            P("seg", "bond", None, None),
            P("seg", None, None),
            P("seg", "bond", None, None),
            P("seg", None, None, "bond"),
            P("seg", None, None, None, None),
            P("seg", "bond", None, None),
            P("seg", None, None),
        ),
        out_specs=(P("seg", "bond", None, None), P("seg", "bond", None)),
        check_vma=False,
    )
```

```python
import functools
import math

import jax
import jax.numpy as jnp
from jax import lax
from jax.experimental import pallas as pl
from jax.experimental.pallas import tpu as pltpu
from jax.sharding import PartitionSpec as P

PHYS = 4
MPOB = 6
BLOCK = 128
STRIP = 256
GROUP = 8
PIECE = 64
ROWS = 8
AHEAD = 3
EDGES = 8
LEFT_ROWS = 64


def halves(x):
    high = x.astype(jnp.bfloat16)
    return high, (x - high.astype(jnp.float32)).astype(jnp.bfloat16)


def split_dot(a, b, dims):
    def dot(x, y):
        return lax.dot_general(x, y, (dims, ((), ())), preferred_element_type=jnp.float32)

    return dot(a[0], b[0]) + (dot(a[0], b[1]) + dot(a[1], b[0]))


def eliminate(block, base, rows_ref):
    height, size = block.shape
    lane = lax.broadcasted_iota(jnp.int32, (1, size), 1)
    rest = block
    top = 0
    for first in range(0, height, GROUP):
        start = first // 8 * 8
        rest, top = rest[start - top :], start
        at = first - top
        pivot = base + first
        rows = [rest[at + q : at + q + 1, :] for q in range(GROUP)]
        columns = [
            jnp.broadcast_to(rest[:, pivot + q : pivot + q + 1], rest.shape) for q in range(GROUP)
        ]
        small = [[columns[r][at + p : at + p + 1, :] for r in range(GROUP)] for p in range(GROUP)]
        change = None
        for q in range(GROUP):
            rows_ref[pl.ds(pivot + q, 1), :] = rows[q]
            inverse = 1.0 / small[q][q]
            lead = jnp.where(lane == pivot + q, 1.0, rows[q])
            for p in range(q + 1, GROUP):
                factor = small[q][p] * inverse
                for r in range(p, GROUP):
                    small[p][r] = small[p][r] - factor * small[q][r]
                rows[p] = jnp.where(lane == pivot + q, 0.0, rows[p]) - factor * lead
                columns[p] = columns[p] - factor * columns[q]
            if first + GROUP < height:
                lead = jnp.where((lane > pivot + q) & (lane < pivot + GROUP), 0.0, lead)
                term = columns[q] * (inverse * lead)
                change = term if change is None else change + term
        if first + GROUP < height:
            rest = jnp.where((lane >= pivot) & (lane < pivot + GROUP), 0.0, rest) - change


def factor_tile(block, rows_ref):
    size = block.shape[0]
    row = lax.broadcasted_iota(jnp.int32, (PIECE, size), 0)
    column = lax.broadcasted_iota(jnp.int32, (PIECE, size), 1)
    tops, inverses = [], []
    for base in range(0, size, PIECE):
        eliminate(block[:PIECE], base, rows_ref)
        done = rows_ref[base : base + PIECE, :]
        diagonal = column == row + base
        scale = lax.rsqrt(jnp.sum(jnp.where(diagonal, done, 0.0), axis=1, keepdims=True))
        scaled = done * scale
        upper = jnp.where(column >= row + base, scaled, 0.0)
        inverse = jnp.where(column < row + base, scaled, jnp.where(diagonal, scale, 0.0))
        tops.append(upper)
        inverses.append(inverse)
        if base + PIECE < size:
            right = jnp.where(column >= base + PIECE, scaled, inverse)
            change = split_dot(halves(scaled), halves(right), ((0,), (0,)))
            below = block[PIECE:]
            inside = lax.broadcasted_iota(jnp.int32, below.shape, 1)
            inside = (inside >= base) & (inside < base + PIECE)
            block = jnp.where(inside, 0.0, below) - change[base + PIECE :]
    return jnp.concatenate(tops, axis=0), jnp.concatenate(inverses, axis=0)


def back_kernel(
    n, norming, target_ref, site_ref, center_ref,
    turned, mine, theirs, work, whole_high, whole_low,
    upper, left, panel, given_high, given_low, rows_ref,
    out_send, out_recv, back_send, back_recv,
):
    me = lax.axis_index("bond")
    height, size = target_ref.shape
    blocks = size // BLOCK
    share = BLOCK // n
    peers = [lax.rem(me + d, n) for d in range(n)]
    barrier = pltpu.get_barrier_semaphore()
    for peer in peers[1:]:
        pl.semaphore_signal(barrier, inc=1, device_id={"bond": peer})
    pl.semaphore_wait(barrier, n - 1)

    def lanes_of(s):
        return pl.ds(0, (s + 1) * BLOCK)

    def rows_of(s, peer):
        return pl.ds(pl.multiple_of(s * BLOCK + peer * share, share), share)

    def outward(s, d):
        return pltpu.make_async_remote_copy(
            src_ref=mine.at[s, peers[d], :, lanes_of(s)],
            dst_ref=theirs.at[n - d - 1, s, :, lanes_of(s)],
            send_sem=out_send.at[s, d],
            recv_sem=out_recv.at[s, n - d],
            device_id={"bond": peers[d]},
        )

    def arriving(s, d):
        return pltpu.make_async_remote_copy(
            src_ref=mine.at[s, peers[d], :, lanes_of(s)],
            dst_ref=theirs.at[d - 1, s, :, lanes_of(s)],
            send_sem=out_send.at[s, d],
            recv_sem=out_recv.at[s, d],
            device_id={"bond": peers[d]},
        )

    def shared(s, d):
        here = work.at[rows_of(s, me), lanes_of(s)]
        return pltpu.make_async_remote_copy(
            src_ref=here,
            dst_ref=here,
            send_sem=back_send.at[s, d],
            recv_sem=back_recv.at[s, n - d],
            device_id={"bond": peers[d]},
        )

    def returning(s, d):
        there = work.at[rows_of(s, peers[d]), lanes_of(s)]
        return pltpu.make_async_remote_copy(
            src_ref=there,
            dst_ref=there,
            send_sem=back_send.at[s, d],
            recv_sem=back_recv.at[s, d],
            device_id={"bond": peers[d]},
        )

    def send_out(s):
        for d in range(1, n):
            outward(s, d).start()

    def reduce(s):
        last = (s + 1) * BLOCK
        for d in range(1, n):
            arriving(s, d).wait_recv()
        value = mine[s, me, :, :last]
        for d in range(1, n):
            value = value + theirs[d - 1, s, :, :last]
        work[rows_of(s, me), :last] = value
        for d in range(1, n):
            shared(s, d).start()

    def collect(s):
        for d in range(1, n):
            returning(s, d).wait_recv()

    per = STRIP // BLOCK
    for g in range(size // STRIP):
        turned[...] = target_ref[:, g * STRIP : (g + 1) * STRIP].T

        def correlate(c, carry):
            lanes = pl.ds(pl.multiple_of(c * STRIP, STRIP), STRIP)
            value = jnp.dot(turned[...], target_ref[:, lanes], preferred_element_type=jnp.float32)
            for b in range(per):
                part = value[b * BLOCK : (b + 1) * BLOCK, :]
                for i in range(n):
                    mine[g * per + b, i, :, lanes] = part[i * share : (i + 1) * share, :]
            return carry

        lax.fori_loop(0, g + 1, correlate, 0)
        for s in range(g * per, min((g + 1) * per, AHEAD)):
            send_out(s)
    whole_high[...] = jnp.zeros_like(whole_high)
    whole_low[...] = jnp.zeros_like(whole_low)
    left[...] = jnp.zeros_like(left)
    for s in range(min(AHEAD, blocks)):
        reduce(s)
        if s + AHEAD < blocks:
            send_out(s + AHEAD)

    full_column = lax.broadcasted_iota(jnp.int32, (BLOCK, size), 1)

    def solve_block(k):
        own = pl.ds(pl.multiple_of(k * BLOCK, BLOCK), BLOCK)
        dims = (((1,), (1,)), ((), ()))
        target = target_ref[...]
        value = lax.dot_general(
            target, whole_high[own, :], dims, preferred_element_type=jnp.float32
        ) + lax.dot_general(target, whole_low[own, :], dims, preferred_element_type=jnp.float32)
        site_ref[:, own] = (value * norming).astype(jnp.bfloat16)

    def step(k, carry):
        for s in range(blocks):

            @pl.when(k == s)
            def _():
                collect(s)
                if s + AHEAD < blocks:
                    reduce(s + AHEAD)
                if s + 2 * AHEAD < blocks:
                    send_out(s + 2 * AHEAD)

        own = pl.ds(pl.multiple_of(k * BLOCK, BLOCK), BLOCK)
        given_high[...], given_low[...] = halves(
            jnp.where(full_column < k * BLOCK, work[own, :], 0.0)
        )

        for c in range(size // STRIP):

            @pl.when(c * per < k)
            def _():
                span, depth = slice(c * STRIP, (c + 1) * STRIP), (c + 1) * STRIP
                left[:, span] = split_dot(
                    (given_high[:, :depth], given_low[:, :depth]),
                    (whole_high[span, :depth], whole_low[span, :depth]),
                    ((1,), (1,)),
                )

        given_high[...], given_low[...] = halves(left[...])
        given = (given_high[...], given_low[...])
        panel[...] = split_dot(given, (whole_high[...], whole_low[...]), ((1,), (0,)))
        solve_block(jnp.maximum(k - 1, 0))
        upper[:, own] = left[...].T
        top, inverse = factor_tile(
            work[own, own] - split_dot(given, given, ((1,), (1,))), rows_ref
        )
        whole = split_dot(halves(-inverse), halves(panel[...]), ((1,), (0,)))
        whole_high[own, :], whole_low[own, :] = halves(whole)
        whole_high[own, own], whole_low[own, own] = halves(inverse)
        upper[own, own] = top
        return carry

    lax.fori_loop(0, blocks, step, 0)
    solve_block(blocks - 1)
    own_rows = center_ref.shape[0]
    center_ref[...] = upper[pl.ds(pl.multiple_of(me * own_rows, own_rows), own_rows), :] / norming
    for s in range(blocks):
        for d in range(1, n):
            outward(s, d).wait_send()
            shared(s, d).wait_send()


def back(target):
    n = lax.axis_size("bond")
    height, size = target.shape
    blocks, share = size // BLOCK, BLOCK // n
    norming = math.sqrt(size * PHYS)
    half, full = jnp.bfloat16, jnp.float32
    whole = pl.BlockSpec(memory_space=pltpu.VMEM)
    return pl.pallas_call(
        functools.partial(back_kernel, n, norming),
        out_shape=(
            jax.ShapeDtypeStruct((height, size), half),
            jax.ShapeDtypeStruct((size // n, size), full),
        ),
        in_specs=[whole],
        out_specs=[whole] * 2,
        scratch_shapes=[
            pltpu.VMEM((STRIP, height), half),
            pltpu.VMEM((blocks, n, share, size), full),
            pltpu.VMEM((n - 1, blocks, share, size), full),
            pltpu.VMEM((size, size), full),
            pltpu.VMEM((size, size), half),
            pltpu.VMEM((size, size), half),
            pltpu.VMEM((size, size), full),
            pltpu.VMEM((BLOCK, size), full),
            pltpu.VMEM((BLOCK, size), full),
            pltpu.VMEM((BLOCK, size), half),
            pltpu.VMEM((BLOCK, size), half),
            pltpu.VMEM((BLOCK, BLOCK), full),
        ]
        + [pltpu.SemaphoreType.DMA((blocks, n))] * 4,
        compiler_params=pltpu.CompilerParams(
            collective_id=0, has_side_effects=True, vmem_limit_bytes=36 * 2**20
        ),
        name="back",
    )(target)


def minor_size(n):
    return max(d for d in range(1, n + 1) if n % d == 0 and d * d <= n)


def edge_spans(width):
    unit = width // EDGES
    return [(j * unit, unit) for j in range(EDGES)]


def spread_coupling(coupling):
    pair, side = PHYS * ROWS, MPOB * PHYS * ROWS

    def grid(height, width):
        shape = (height, width)
        return [lax.broadcasted_iota(jnp.int32, shape, axis) for axis in range(2)]

    def hot(mask):
        return jnp.where(mask, 1.0, 0.0).astype(jnp.bfloat16)

    total = None
    for u in range(MPOB):
        row, column = grid(side, MPOB * MPOB)
        offset = row - pair * (column - u * MPOB)
        picked = jnp.dot(
            hot((offset >= 0) & (offset < pair)), coupling, preferred_element_type=jnp.float32
        )
        row, column = grid(side, PHYS * PHYS)
        offset = (row & (pair - 1)) * PHYS - ROWS * (column & (PHYS * PHYS - PHYS))
        kept = jnp.where((offset >= 0) & (offset < ROWS * PHYS), picked, 0.0)
        row, column = grid(PHYS * PHYS, side)
        offset = column - u * pair - ROWS * (row & (PHYS - 1))
        term = jnp.dot(
            kept.astype(jnp.bfloat16),
            hot((offset >= 0) & (offset < ROWS)),
            preferred_element_type=jnp.float32,
        )
        total = term if total is None else total + term
    row, column = grid(side, side)
    same = (row & (ROWS - 1)) == (column & (ROWS - 1))
    return jnp.where(same, total, 0.0).astype(jnp.bfloat16)


def front_kernel(
    segments, n, left_ref, prev_left_ref, current_ref, right_ref,
    prev_site_ref, prev_right_ref, coupling_ref, target_ref,
    left, current, right, prev_left, partial_out, partial_in, projected, mixture, outgoing, incoming,
    total, spread_ref,
    left_send, left_recv, prev_send, prev_recv, major_send, major_recv, minor_send, minor_recv,
    relay_send, relay_recv, right_send, right_recv, partial_send, partial_recv,
    target_send, target_recv, local_sem,
):
    q = minor_size(n)
    p = n // q
    seg, index = lax.axis_index("seg"), lax.axis_index("bond")
    major, minor = index // q, lax.rem(index, q)
    own, bond = left_ref.shape[1], left_ref.shape[2]
    wide, tall = q * own, p * own
    half = own // 2
    rows = projected.shape[1] // MPOB
    chunks = own // rows
    spans = edge_spans(bond)

    def device(hop, dm, dr):
        m, r = lax.rem(major + dm, p), lax.rem(minor + dr, q)
        return {"seg": lax.rem(seg + hop, segments), "bond": m * q + r}

    def copy(src, dst, send, recv, to):
        return pltpu.make_async_remote_copy(
            src_ref=src, dst_ref=dst, send_sem=send, recv_sem=recv, device_id=to
        )

    def slot(d):
        return lax.rem(major + d, p)

    def place(dm, dr):
        return (lax.rem(major + dm, p) * q + lax.rem(minor + dr, q)) * own

    barrier = pltpu.get_barrier_semaphore()
    peers = [device(0, d, 0) for d in range(1, p)] + [device(0, 0, d) for d in range(1, q)]
    peers += [device(hop, d, 0) for d in range(p) for hop in (1, segments - 1)]
    for peer in peers:
        pl.semaphore_signal(barrier, inc=1, device_id=peer)
    pl.semaphore_wait(barrier, len(peers))

    def left_flow(d, j, slot_index, back):
        span = pl.ds(pl.multiple_of(j * rows, rows), rows)
        return copy(
            left_ref.at[:, span, :],
            left.at[slot_index, :, span, :],
            left_send.at[d, j],
            left_recv.at[back, j],
            device(1, d, 0),
        )

    def left_out(d, j):
        return left_flow(d, j, major, (p - d) % p)

    def left_in(d, j):
        return left_flow(d, j, slot(d), d)

    def current_rows(dm, dr, h):
        return pl.ds(pl.multiple_of(place(dm, dr) + h * half, half), half)

    def source_columns(dm):
        return pl.ds(pl.multiple_of(slot(dm) * wide, wide), wide)

    prev_flow = copy(prev_left_ref, prev_left, prev_send.at[0], prev_recv.at[0], device(1, 0, 0))
    prev_flow.start()
    sends = [prev_flow]
    for h in range(2):
        source = pl.ds(h * half, half)
        for d in range(1, p):
            flow = copy(
                current_ref.at[:, source, source_columns(d)],
                current.at[:, current_rows(0, 0, h), :],
                major_send.at[d, h],
                major_recv.at[p - d, h],
                device(0, d, 0),
            )
            flow.start()
            sends.append(flow)
        for d in range(1, q):
            flow = copy(
                current_ref.at[:, source, source_columns(0)],
                current.at[:, current_rows(0, 0, h), :],
                minor_send.at[d, h],
                minor_recv.at[q - d, h],
                device(0, 0, d),
            )
            flow.start()
            sends.append(flow)
    for j in range(chunks):
        for d in range(p):
            flow = left_out(d, j)
            flow.start()
            sends.append(flow)
    locals_ = [
        pltpu.make_async_copy(
            current_ref.at[:, :, source_columns(0)],
            current.at[:, pl.ds(pl.multiple_of(place(0, 0), own), own), :],
            local_sem.at[0],
        ),
        pltpu.make_async_copy(
            right_ref, right.at[:, pl.ds(pl.multiple_of(minor * own, own), own), :], local_sem.at[1]
        ),
    ]
    for one in locals_:
        one.start()

    spread_ref[...] = spread_coupling(coupling_ref[...])

    for h in range(2):
        for dm in range(1, p):
            landed = current.at[:, current_rows(dm, 0, h), :]
            copy(
                landed, landed, major_send.at[dm, h], major_recv.at[dm, h], device(0, dm, 0)
            ).wait_recv()
            for d in range(1, q):
                flow = copy(
                    landed, landed, relay_send.at[dm, d, h], relay_recv.at[dm, q - d, h],
                    device(0, 0, d),
                )
                flow.start()
                sends.append(flow)

    prev_flow.wait_recv()

    def contract(d, out):
        def body(step, carry):
            m, s = step // PHYS, lax.rem(step, PHYS)
            top = (m * q + lax.rem(minor + d, q)) * own
            value = jnp.dot(
                prev_left[pl.ds(pl.multiple_of(top, own), own), :],
                prev_site_ref[s],
                preferred_element_type=jnp.float32,
            )
            out[s, pl.ds(pl.multiple_of(m * own, own), own), :] = value.astype(jnp.bfloat16)
            return carry

        lax.fori_loop(0, p * PHYS, body, 0)

    for d in range(1, q):
        contract(d, partial_out.at[d - 1])
        flow = copy(
            partial_out.at[d - 1], partial_in.at[minor], partial_send.at[d],
            partial_recv.at[q - d], device(0, 0, d),
        )
        flow.start()
        sends.append(flow)

    def right_flow(d, j, row, back):
        first, width = spans[j]
        lanes = pl.ds(first, width)
        return copy(
            right_ref.at[:, :, lanes],
            right.at[:, pl.ds(pl.multiple_of(row * own, own), own), lanes],
            right_send.at[d, j],
            right_recv.at[back, j],
            device(0, 0, d),
        )

    for j in range(len(spans)):
        for d in range(1, q):
            flow = right_flow(d, j, minor, q - d)
            flow.start()
            sends.append(flow)
    contract(0, partial_in.at[minor])

    for h in range(2):
        for d in range(1, q):
            landed = current.at[:, current_rows(0, d, h), :]
            copy(
                landed, landed, minor_send.at[d, h], minor_recv.at[d, h], device(0, 0, d)
            ).wait_recv()
            for dm in range(1, p):
                landed = current.at[:, current_rows(dm, d, h), :]
                copy(
                    landed, landed, relay_send.at[dm, d, h], relay_recv.at[dm, d, h],
                    device(0, 0, d),
                ).wait_recv()
    for one in locals_:
        one.wait()

    def mix(step, carry):
        j, order = step // p, lax.rem(step, p)
        where = lax.rem(major + order, p)
        left_in(order, j).wait_recv()
        span = pl.ds(pl.multiple_of(j * rows, rows), rows)
        block = left[where, :, span, :].reshape(MPOB * rows, bond)

        def project(t, carry):
            projected[t] = jnp.dot(block, current[t], preferred_element_type=jnp.float32)
            return carry

        lax.fori_loop(0, PHYS, project, 0)

        def spread(g, carry):
            results = []
            for first in range(2):
                at = g * 2 * ROWS + first * ROWS
                stack = jnp.concatenate(
                    [
                        projected[t, pl.ds(pl.multiple_of(u * rows + at, ROWS), ROWS), :]
                        for u in range(MPOB)
                        for t in range(PHYS)
                    ],
                    axis=0,
                )
                results.append(
                    jnp.dot(
                        spread_ref[...],
                        stack.astype(jnp.bfloat16),
                        preferred_element_type=jnp.float32,
                    )
                )
            top = pl.multiple_of(where * own + j * rows + g * 2 * ROWS, 2 * ROWS)
            for v in range(MPOB):
                for s in range(PHYS):
                    first = (v * PHYS + s) * ROWS
                    both = jnp.concatenate([one[first : first + ROWS] for one in results], axis=0)
                    mixture[s, pl.ds(top, 2 * ROWS), v * wide : (v + 1) * wide] = both.astype(
                        jnp.bfloat16
                    )
            return carry

        lax.fori_loop(0, rows // (2 * ROWS), spread, 0)
        return carry

    lax.fori_loop(0, chunks * p, mix, 0)

    for d in range(1, q):
        landed = partial_in.at[lax.rem(minor + d, q)]
        copy(
            landed, landed, partial_send.at[d], partial_recv.at[d], device(0, 0, d)
        ).wait_recv()

    def products(d, j, write):
        first, width = spans[j]

        def body(s, carry):
            top = pl.ds(pl.multiple_of(slot(d) * own, own), own)
            lanes = slice(first, first + width)
            value = 2.0 * jnp.dot(
                mixture[s, top, :],
                right[:, :, lanes].reshape(MPOB * wide, width),
                preferred_element_type=jnp.float32,
            )
            for r in range(q):
                prev_rows = pl.ds(pl.multiple_of(major * wide + r * own, own), own)
                value = value - jnp.dot(
                    partial_in[r, s, top, :],
                    prev_right_ref[prev_rows, lanes],
                    preferred_element_type=jnp.float32,
                )
            write(s, lanes, value)
            return carry

        lax.fori_loop(0, PHYS, body, 0)

    def target_flow(d, j, back):
        first, width = spans[j]
        lanes = pl.ds(first, width)
        return copy(
            outgoing.at[d - 1, :, :, lanes], incoming.at[back - 1, :, :, lanes],
            target_send.at[d, j], target_recv.at[back, j], device(0, d, 0),
        )

    for j in range(len(spans)):
        for d in range(1, q):
            right_flow(d, j, lax.rem(minor + d, q), d).wait_recv()
        for d in range(1, p):

            def keep(s, lanes, value):
                outgoing[d - 1, s, :, lanes] = value.astype(jnp.bfloat16)

            products(d, j, keep)
            flow = target_flow(d, j, p - d)
            flow.start()
            sends.append(flow)

        def own_part(s, lanes, value):
            total[s, :, lanes] = value

        products(0, j, own_part)
    for j, (first, width) in enumerate(spans):
        for d in range(1, p):
            target_flow(d, j, d).wait_recv()
        lanes = slice(first, first + width)

        def add(s, carry):
            value = total[s, :, lanes]
            for d in range(1, p):
                value = value + incoming[d - 1, s, :, lanes].astype(jnp.float32)
            target_ref[s, :, lanes] = value.astype(jnp.bfloat16)
            return carry

        lax.fori_loop(0, PHYS, add, 0)
    for flow in sends:
        flow.wait_send()


def front(left, prev_left, current, right, prev_site, prev_right, coupling):
    n, segments = lax.axis_size("bond"), lax.axis_size("seg")
    q = minor_size(n)
    p = n // q
    own, bond = left.shape[1], left.shape[2]
    wide, tall = q * own, p * own
    rows = min(LEFT_ROWS, own)
    edges = len(edge_spans(bond))
    side = MPOB * PHYS * ROWS
    low, full = jnp.bfloat16, jnp.float32
    whole = pl.BlockSpec(memory_space=pltpu.VMEM)
    there = pl.BlockSpec(memory_space=pl.ANY)

    def pairs(*shape):
        return [pltpu.SemaphoreType.DMA(shape)] * 2

    return pl.pallas_call(
        functools.partial(front_kernel, segments, n),
        out_shape=jax.ShapeDtypeStruct((PHYS, own, bond), low),
        in_specs=[there] * 4 + [whole] * 3,
        out_specs=whole,
        scratch_shapes=[
            pltpu.VMEM((p, MPOB, own, bond), low),
            pltpu.VMEM((PHYS, bond, wide), low),
            pltpu.VMEM((MPOB, wide, bond), low),
            pltpu.VMEM((bond, bond), low),
            pltpu.VMEM((max(q - 1, 1), PHYS, tall, own), low),
            pltpu.VMEM((q, PHYS, tall, own), low),
            pltpu.VMEM((PHYS, MPOB * rows, wide), full),
            pltpu.VMEM((PHYS, tall, MPOB * wide), low),
            pltpu.VMEM((max(p - 1, 1), PHYS, own, bond), low),
            pltpu.VMEM((max(p - 1, 1), PHYS, own, bond), low),
            pltpu.VMEM((PHYS, own, bond), full),
            pltpu.VMEM((side, side), low),
        ]
        + pairs(p, own // rows)
        + pairs(1)
        + pairs(p, 2)
        + pairs(q, 2)
        + pairs(p, q, 2)
        + pairs(q, edges)
        + pairs(q)
        + pairs(p, edges)
        + [pltpu.SemaphoreType.DMA((2,))],
        compiler_params=pltpu.CompilerParams(
            collective_id=1, has_side_effects=True, vmem_limit_bytes=49 * 2**20
        ),
        name="front",
    )(left, prev_left, current, right, prev_site, prev_right, coupling)


def shards(left_env, prev_left, cur_site, prev_site, hamiltonian, right_env, prev_right):
    own_rows, bond_width = left_env.shape[1], left_env.shape[3]
    target = front(
        jnp.transpose(left_env[0], (1, 0, 2)),
        prev_left[0],
        jnp.transpose(cur_site[0], (1, 0, 2)),
        jnp.transpose(right_env[0], (1, 0, 2)),
        jnp.transpose(prev_site[0], (1, 0, 2)),
        prev_right[0],
        hamiltonian[0].reshape(MPOB * MPOB, PHYS * PHYS),
    ).reshape(PHYS * own_rows, bond_width)
    site, center = back(target)
    site = jnp.transpose(site.reshape(PHYS, own_rows, bond_width), (1, 0, 2))
    return (site[None], center[None])


def solution(mesh):
    return jax.shard_map(
        shards,
        mesh=mesh,
        in_specs=(
            P("seg", "bond", None, None),
            P("seg", None, None),
            P("seg", "bond", None, None),
            P("seg", None, None, "bond"),
            P("seg", None, None, None, None),
            P("seg", "bond", None, None),
            P("seg", None, None),
        ),
        out_specs=(P("seg", "bond", None, None), P("seg", "bond", None)),
        check_vma=False,
    )
```

```python
import functools
import math

import jax
import jax.numpy as jnp
from jax import lax
from jax.experimental import pallas as pl
from jax.experimental.pallas import tpu as pltpu
from jax.sharding import PartitionSpec as P

PHYS = 4
MPOB = 6
BLOCK = 128
STRIP = 256
GROUP = 8
PIECE = 64
ROWS = 8
AHEAD = 3
EDGES = 8
LEFT_ROWS = 64


def halves(x):
    high = x.astype(jnp.bfloat16)
    return high, (x - high.astype(jnp.float32)).astype(jnp.bfloat16)


def split_dot(a, b, dims):
    def dot(x, y):
        return lax.dot_general(x, y, (dims, ((), ())), preferred_element_type=jnp.float32)

    return dot(a[0], b[0]) + (dot(a[0], b[1]) + dot(a[1], b[0]))


def eliminate(block, base, rows_ref):
    height, size = block.shape
    lane = lax.broadcasted_iota(jnp.int32, (1, size), 1)
    rest = block
    top = 0
    for first in range(0, height, GROUP):
        start = first // 8 * 8
        rest, top = rest[start - top :], start
        at = first - top
        pivot = base + first
        rows = [rest[at + q : at + q + 1, :] for q in range(GROUP)]
        columns = [
            jnp.broadcast_to(rest[:, pivot + q : pivot + q + 1], rest.shape) for q in range(GROUP)
        ]
        small = [[columns[r][at + p : at + p + 1, :] for r in range(GROUP)] for p in range(GROUP)]
        change = None
        for q in range(GROUP):
            rows_ref[pl.ds(pivot + q, 1), :] = rows[q]
            inverse = 1.0 / small[q][q]
            lead = jnp.where(lane == pivot + q, 1.0, rows[q])
            for p in range(q + 1, GROUP):
                factor = small[q][p] * inverse
                for r in range(p, GROUP):
                    small[p][r] = small[p][r] - factor * small[q][r]
                rows[p] = jnp.where(lane == pivot + q, 0.0, rows[p]) - factor * lead
                columns[p] = columns[p] - factor * columns[q]
            if first + GROUP < height:
                lead = jnp.where((lane > pivot + q) & (lane < pivot + GROUP), 0.0, lead)
                term = columns[q] * (inverse * lead)
                change = term if change is None else change + term
        if first + GROUP < height:
            rest = jnp.where((lane >= pivot) & (lane < pivot + GROUP), 0.0, rest) - change


def factor_tile(block, rows_ref):
    size = block.shape[0]
    row = lax.broadcasted_iota(jnp.int32, (PIECE, size), 0)
    column = lax.broadcasted_iota(jnp.int32, (PIECE, size), 1)
    tops, inverses = [], []
    for base in range(0, size, PIECE):
        eliminate(block[:PIECE], base, rows_ref)
        done = rows_ref[base : base + PIECE, :]
        diagonal = column == row + base
        scale = lax.rsqrt(jnp.sum(jnp.where(diagonal, done, 0.0), axis=1, keepdims=True))
        scaled = done * scale
        upper = jnp.where(column >= row + base, scaled, 0.0)
        inverse = jnp.where(column < row + base, scaled, jnp.where(diagonal, scale, 0.0))
        tops.append(upper)
        inverses.append(inverse)
        if base + PIECE < size:
            right = jnp.where(column >= base + PIECE, scaled, inverse)
            change = split_dot(halves(scaled), halves(right), ((0,), (0,)))
            below = block[PIECE:]
            inside = lax.broadcasted_iota(jnp.int32, below.shape, 1)
            inside = (inside >= base) & (inside < base + PIECE)
            block = jnp.where(inside, 0.0, below) - change[base + PIECE :]
    return jnp.concatenate(tops, axis=0), jnp.concatenate(inverses, axis=0)


def back_kernel(
    n, norming, target_ref, site_ref, center_ref,
    turned, mine, theirs, work, whole_high, whole_low,
    upper, left, panel, given_high, given_low, rows_ref,
    out_send, out_recv, back_send, back_recv,
):
    me = lax.axis_index("bond")
    height, size = target_ref.shape
    blocks = size // BLOCK
    share = BLOCK // n
    peers = [lax.rem(me + d, n) for d in range(n)]
    barrier = pltpu.get_barrier_semaphore()
    for peer in peers[1:]:
        pl.semaphore_signal(barrier, inc=1, device_id={"bond": peer})
    pl.semaphore_wait(barrier, n - 1)

    def lanes_of(s):
        return pl.ds(0, (s + 1) * BLOCK)

    def rows_of(s, peer):
        return pl.ds(pl.multiple_of(s * BLOCK + peer * share, share), share)

    def outward(s, d):
        return pltpu.make_async_remote_copy(
            src_ref=mine.at[s, peers[d], :, lanes_of(s)],
            dst_ref=theirs.at[n - d - 1, s, :, lanes_of(s)],
            send_sem=out_send.at[s, d],
            recv_sem=out_recv.at[s, n - d],
            device_id={"bond": peers[d]},
        )

    def arriving(s, d):
        return pltpu.make_async_remote_copy(
            src_ref=mine.at[s, peers[d], :, lanes_of(s)],
            dst_ref=theirs.at[d - 1, s, :, lanes_of(s)],
            send_sem=out_send.at[s, d],
            recv_sem=out_recv.at[s, d],
            device_id={"bond": peers[d]},
        )

    def shared(s, d):
        here = work.at[rows_of(s, me), lanes_of(s)]
        return pltpu.make_async_remote_copy(
            src_ref=here,
            dst_ref=here,
            send_sem=back_send.at[s, d],
            recv_sem=back_recv.at[s, n - d],
            device_id={"bond": peers[d]},
        )

    def returning(s, d):
        there = work.at[rows_of(s, peers[d]), lanes_of(s)]
        return pltpu.make_async_remote_copy(
            src_ref=there,
            dst_ref=there,
            send_sem=back_send.at[s, d],
            recv_sem=back_recv.at[s, d],
            device_id={"bond": peers[d]},
        )

    def send_out(s):
        for d in range(1, n):
            outward(s, d).start()

    def reduce(s):
        last = (s + 1) * BLOCK
        for d in range(1, n):
            arriving(s, d).wait_recv()
        value = mine[s, me, :, :last]
        for d in range(1, n):
            value = value + theirs[d - 1, s, :, :last]
        work[rows_of(s, me), :last] = value
        for d in range(1, n):
            shared(s, d).start()

    def collect(s):
        for d in range(1, n):
            returning(s, d).wait_recv()

    per = STRIP // BLOCK
    for g in range(size // STRIP):
        turned[...] = target_ref[:, g * STRIP : (g + 1) * STRIP].T

        def correlate(c, carry):
            lanes = pl.ds(pl.multiple_of(c * STRIP, STRIP), STRIP)
            value = jnp.dot(turned[...], target_ref[:, lanes], preferred_element_type=jnp.float32)
            for b in range(per):
                part = value[b * BLOCK : (b + 1) * BLOCK, :]
                for i in range(n):
                    mine[g * per + b, i, :, lanes] = part[i * share : (i + 1) * share, :]
            return carry

        lax.fori_loop(0, g + 1, correlate, 0)
        for s in range(g * per, min((g + 1) * per, AHEAD)):
            send_out(s)
    whole_high[...] = jnp.zeros_like(whole_high)
    whole_low[...] = jnp.zeros_like(whole_low)
    left[...] = jnp.zeros_like(left)
    for s in range(min(AHEAD, blocks)):
        reduce(s)
        if s + AHEAD < blocks:
            send_out(s + AHEAD)

    full_column = lax.broadcasted_iota(jnp.int32, (BLOCK, size), 1)

    def solve_block(k):
        own = pl.ds(pl.multiple_of(k * BLOCK, BLOCK), BLOCK)
        dims = (((1,), (1,)), ((), ()))
        target = target_ref[...]
        value = lax.dot_general(
            target, whole_high[own, :], dims, preferred_element_type=jnp.float32
        ) + lax.dot_general(target, whole_low[own, :], dims, preferred_element_type=jnp.float32)
        site_ref[:, own] = (value * norming).astype(jnp.bfloat16)

    def step(k, carry):
        for s in range(blocks):

            @pl.when(k == s)
            def _():
                collect(s)
                if s + AHEAD < blocks:
                    reduce(s + AHEAD)
                if s + 2 * AHEAD < blocks:
                    send_out(s + 2 * AHEAD)

        own = pl.ds(pl.multiple_of(k * BLOCK, BLOCK), BLOCK)
        given_high[...], given_low[...] = halves(
            jnp.where(full_column < k * BLOCK, work[own, :], 0.0)
        )

        for c in range(size // STRIP):

            @pl.when(c * per < k)
            def _():
                span, depth = slice(c * STRIP, (c + 1) * STRIP), (c + 1) * STRIP
                left[:, span] = split_dot(
                    (given_high[:, :depth], given_low[:, :depth]),
                    (whole_high[span, :depth], whole_low[span, :depth]),
                    ((1,), (1,)),
                )

        given_high[...], given_low[...] = halves(left[...])
        given = (given_high[...], given_low[...])
        panel[...] = split_dot(given, (whole_high[...], whole_low[...]), ((1,), (0,)))
        solve_block(jnp.maximum(k - 1, 0))
        upper[:, own] = left[...].T
        top, inverse = factor_tile(
            work[own, own] - split_dot(given, given, ((1,), (1,))), rows_ref
        )
        whole = split_dot(halves(-inverse), halves(panel[...]), ((1,), (0,)))
        whole_high[own, :], whole_low[own, :] = halves(whole)
        whole_high[own, own], whole_low[own, own] = halves(inverse)
        upper[own, own] = top
        return carry

    lax.fori_loop(0, blocks, step, 0)
    solve_block(blocks - 1)
    own_rows = center_ref.shape[0]
    center_ref[...] = upper[pl.ds(pl.multiple_of(me * own_rows, own_rows), own_rows), :] / norming
    for s in range(blocks):
        for d in range(1, n):
            outward(s, d).wait_send()
            shared(s, d).wait_send()


def back(target):
    n = lax.axis_size("bond")
    height, size = target.shape
    blocks, share = size // BLOCK, BLOCK // n
    norming = math.sqrt(size * PHYS)
    half, full = jnp.bfloat16, jnp.float32
    whole = pl.BlockSpec(memory_space=pltpu.VMEM)
    return pl.pallas_call(
        functools.partial(back_kernel, n, norming),
        out_shape=(
            jax.ShapeDtypeStruct((height, size), half),
            jax.ShapeDtypeStruct((size // n, size), full),
        ),
        in_specs=[whole],
        out_specs=[whole] * 2,
        scratch_shapes=[
            pltpu.VMEM((STRIP, height), half),
            pltpu.VMEM((blocks, n, share, size), full),
            pltpu.VMEM((n - 1, blocks, share, size), full),
            pltpu.VMEM((size, size), full),
            pltpu.VMEM((size, size), half),
            pltpu.VMEM((size, size), half),
            pltpu.VMEM((size, size), full),
            pltpu.VMEM((BLOCK, size), full),
            pltpu.VMEM((BLOCK, size), full),
            pltpu.VMEM((BLOCK, size), half),
            pltpu.VMEM((BLOCK, size), half),
            pltpu.VMEM((BLOCK, BLOCK), full),
        ]
        + [pltpu.SemaphoreType.DMA((blocks, n))] * 4,
        compiler_params=pltpu.CompilerParams(
            collective_id=0, has_side_effects=True, vmem_limit_bytes=36 * 2**20
        ),
        name="back",
    )(target)


def minor_size(n):
    return max(d for d in range(1, n + 1) if n % d == 0 and d * d <= n)


def edge_spans(width):
    unit = width // EDGES
    return [(j * unit, unit) for j in range(EDGES)]


def spread_coupling(coupling):
    pair, side, table = PHYS * ROWS, MPOB * PHYS * ROWS, MPOB * PHYS * PHYS

    def grid(height, width):
        shape = (height, width)
        return [lax.broadcasted_iota(jnp.int32, shape, axis) for axis in range(2)]

    def within(offset, size):
        return (offset >= 0) & (offset < size)

    row, column = grid(side, MPOB)
    hot = jnp.where(within(row - pair * column, pair), 1.0, 0.0).astype(jnp.bfloat16)
    picked = lax.dot_general(
        hot, coupling, (((1,), (1,)), ((), ())), preferred_element_type=jnp.float32
    )
    row, column = grid(side, table)
    offset = (row & (pair - 1)) * PHYS - ROWS * (column & (PHYS * PHYS - PHYS))
    kept = jnp.where(within(offset, ROWS * PHYS), picked, 0.0).astype(jnp.bfloat16)
    row, column = grid(table, side)
    first = (row & (PHYS - 1)) * ROWS
    same_u = within(row * pair - column * (PHYS * PHYS) + (column & (pair - 1)) * (PHYS * PHYS)
                    - (row & (PHYS * PHYS - 1)) * pair, 1)
    same_t = within((column & (pair - 1)) - first, ROWS)
    hot = jnp.where(same_u & same_t, 1.0, 0.0).astype(jnp.bfloat16)
    total = jnp.dot(kept, hot, preferred_element_type=jnp.float32)
    row, column = grid(side, side)
    same = (row & (ROWS - 1)) == (column & (ROWS - 1))
    return jnp.where(same, total, 0.0).astype(jnp.bfloat16)


def front_kernel(
    segments, n, left_ref, prev_left_ref, current_ref, right_ref,
    prev_site_ref, prev_right_ref, coupling_ref, target_ref,
    left, current, right, prev_left, partial_out, partial_in, projected, mixture, outgoing, incoming,
    total, spread_ref,
    left_send, left_recv, prev_send, prev_recv, major_send, major_recv, minor_send, minor_recv,
    relay_send, relay_recv, right_send, right_recv, partial_send, partial_recv,
    target_send, target_recv, local_sem,
):
    q = minor_size(n)
    p = n // q
    seg, index = lax.axis_index("seg"), lax.axis_index("bond")
    major, minor = index // q, lax.rem(index, q)
    own, bond = left_ref.shape[1], left_ref.shape[2]
    wide, tall = q * own, p * own
    half = own // 2
    rows = projected.shape[1] // MPOB
    chunks = own // rows
    spans = edge_spans(bond)

    def device(hop, dm, dr):
        m, r = lax.rem(major + dm, p), lax.rem(minor + dr, q)
        return {"seg": lax.rem(seg + hop, segments), "bond": m * q + r}

    def copy(src, dst, send, recv, to):
        return pltpu.make_async_remote_copy(
            src_ref=src, dst_ref=dst, send_sem=send, recv_sem=recv, device_id=to
        )

    def slot(d):
        return lax.rem(major + d, p)

    def place(dm, dr):
        return (lax.rem(major + dm, p) * q + lax.rem(minor + dr, q)) * own

    barrier = pltpu.get_barrier_semaphore()
    peers = [device(0, d, 0) for d in range(1, p)] + [device(0, 0, d) for d in range(1, q)]
    peers += [device(hop, d, 0) for d in range(p) for hop in (1, segments - 1)]
    for peer in peers:
        pl.semaphore_signal(barrier, inc=1, device_id=peer)
    pl.semaphore_wait(barrier, len(peers))

    def left_flow(d, j, slot_index, back):
        span = pl.ds(pl.multiple_of(j * rows, rows), rows)
        return copy(
            left_ref.at[:, span, :],
            left.at[slot_index, :, span, :],
            left_send.at[d, j],
            left_recv.at[back, j],
            device(1, d, 0),
        )

    def left_out(d, j):
        return left_flow(d, j, major, (p - d) % p)

    def left_in(d, j):
        return left_flow(d, j, slot(d), d)

    def current_rows(dm, dr, h):
        return pl.ds(pl.multiple_of(place(dm, dr) + h * half, half), half)

    def source_columns(dm):
        return pl.ds(pl.multiple_of(slot(dm) * wide, wide), wide)

    prev_flow = copy(prev_left_ref, prev_left, prev_send.at[0], prev_recv.at[0], device(1, 0, 0))
    prev_flow.start()
    sends = [prev_flow]
    for h in range(2):
        source = pl.ds(h * half, half)
        for d in range(1, p):
            flow = copy(
                current_ref.at[:, source, source_columns(d)],
                current.at[:, current_rows(0, 0, h), :],
                major_send.at[d, h],
                major_recv.at[p - d, h],
                device(0, d, 0),
            )
            flow.start()
            sends.append(flow)
        for d in range(1, q):
            flow = copy(
                current_ref.at[:, source, source_columns(0)],
                current.at[:, current_rows(0, 0, h), :],
                minor_send.at[d, h],
                minor_recv.at[q - d, h],
                device(0, 0, d),
            )
            flow.start()
            sends.append(flow)
    for j in range(chunks):
        for d in range(p):
            flow = left_out(d, j)
            flow.start()
            sends.append(flow)
    locals_ = [
        pltpu.make_async_copy(
            current_ref.at[:, :, source_columns(0)],
            current.at[:, pl.ds(pl.multiple_of(place(0, 0), own), own), :],
            local_sem.at[0],
        ),
        pltpu.make_async_copy(
            right_ref, right.at[:, pl.ds(pl.multiple_of(minor * own, own), own), :], local_sem.at[1]
        ),
    ]
    for one in locals_:
        one.start()

    spread_ref[...] = spread_coupling(coupling_ref[...])

    for h in range(2):
        for dm in range(1, p):
            landed = current.at[:, current_rows(dm, 0, h), :]
            copy(
                landed, landed, major_send.at[dm, h], major_recv.at[dm, h], device(0, dm, 0)
            ).wait_recv()
            for d in range(1, q):
                flow = copy(
                    landed, landed, relay_send.at[dm, d, h], relay_recv.at[dm, q - d, h],
                    device(0, 0, d),
                )
                flow.start()
                sends.append(flow)

    prev_flow.wait_recv()

    def contract(d, out):
        def body(step, carry):
            m, s = step // PHYS, lax.rem(step, PHYS)
            top = (m * q + lax.rem(minor + d, q)) * own
            value = jnp.dot(
                prev_left[pl.ds(pl.multiple_of(top, own), own), :],
                prev_site_ref[s],
                preferred_element_type=jnp.float32,
            )
            out[s, pl.ds(pl.multiple_of(m * own, own), own), :] = value.astype(jnp.bfloat16)
            return carry

        lax.fori_loop(0, p * PHYS, body, 0)

    for d in range(1, q):
        contract(d, partial_out.at[d - 1])
        flow = copy(
            partial_out.at[d - 1], partial_in.at[minor], partial_send.at[d],
            partial_recv.at[q - d], device(0, 0, d),
        )
        flow.start()
        sends.append(flow)

    def right_flow(d, j, row, back):
        first, width = spans[j]
        lanes = pl.ds(first, width)
        return copy(
            right_ref.at[:, :, lanes],
            right.at[:, pl.ds(pl.multiple_of(row * own, own), own), lanes],
            right_send.at[d, j],
            right_recv.at[back, j],
            device(0, 0, d),
        )

    for j in range(len(spans)):
        for d in range(1, q):
            flow = right_flow(d, j, minor, q - d)
            flow.start()
            sends.append(flow)
    contract(0, partial_in.at[minor])

    for h in range(2):
        for d in range(1, q):
            landed = current.at[:, current_rows(0, d, h), :]
            copy(
                landed, landed, minor_send.at[d, h], minor_recv.at[d, h], device(0, 0, d)
            ).wait_recv()
            for dm in range(1, p):
                landed = current.at[:, current_rows(dm, d, h), :]
                copy(
                    landed, landed, relay_send.at[dm, d, h], relay_recv.at[dm, d, h],
                    device(0, 0, d),
                ).wait_recv()
    for one in locals_:
        one.wait()

    def mix(step, carry):
        j, order = step // p, lax.rem(step, p)
        where = lax.rem(major + order, p)
        left_in(order, j).wait_recv()
        span = pl.ds(pl.multiple_of(j * rows, rows), rows)
        block = left[where, :, span, :].reshape(MPOB * rows, bond)

        def project(t, carry):
            projected[t] = jnp.dot(block, current[t], preferred_element_type=jnp.float32)
            return carry

        lax.fori_loop(0, PHYS, project, 0)

        def spread(g, carry):
            results = []
            for first in range(2):
                at = g * 2 * ROWS + first * ROWS
                stack = jnp.concatenate(
                    [
                        projected[t, pl.ds(pl.multiple_of(u * rows + at, ROWS), ROWS), :]
                        for u in range(MPOB)
                        for t in range(PHYS)
                    ],
                    axis=0,
                )
                results.append(
                    jnp.dot(
                        spread_ref[...],
                        stack.astype(jnp.bfloat16),
                        preferred_element_type=jnp.float32,
                    )
                )
            top = pl.multiple_of(where * own + j * rows + g * 2 * ROWS, 2 * ROWS)
            for v in range(MPOB):
                for s in range(PHYS):
                    first = (v * PHYS + s) * ROWS
                    both = jnp.concatenate([one[first : first + ROWS] for one in results], axis=0)
                    mixture[s, pl.ds(top, 2 * ROWS), v * wide : (v + 1) * wide] = both.astype(
                        jnp.bfloat16
                    )
            return carry

        lax.fori_loop(0, rows // (2 * ROWS), spread, 0)
        return carry

    lax.fori_loop(0, chunks * p, mix, 0)

    for d in range(1, q):
        landed = partial_in.at[lax.rem(minor + d, q)]
        copy(
            landed, landed, partial_send.at[d], partial_recv.at[d], device(0, 0, d)
        ).wait_recv()

    def products(d, j, write):
        first, width = spans[j]

        def body(s, carry):
            top = pl.ds(pl.multiple_of(slot(d) * own, own), own)
            lanes = slice(first, first + width)
            value = 2.0 * jnp.dot(
                mixture[s, top, :],
                right[:, :, lanes].reshape(MPOB * wide, width),
                preferred_element_type=jnp.float32,
            )
            for r in range(q):
                prev_rows = pl.ds(pl.multiple_of(major * wide + r * own, own), own)
                value = value - jnp.dot(
                    partial_in[r, s, top, :],
                    prev_right_ref[prev_rows, lanes],
                    preferred_element_type=jnp.float32,
                )
            write(s, lanes, value)
            return carry

        lax.fori_loop(0, PHYS, body, 0)

    def target_flow(d, j, back):
        first, width = spans[j]
        lanes = pl.ds(first, width)
        return copy(
            outgoing.at[d - 1, :, :, lanes], incoming.at[back - 1, :, :, lanes],
            target_send.at[d, j], target_recv.at[back, j], device(0, d, 0),
        )

    for j in range(len(spans)):
        for d in range(1, q):
            right_flow(d, j, lax.rem(minor + d, q), d).wait_recv()
        for d in range(1, p):

            def keep(s, lanes, value):
                outgoing[d - 1, s, :, lanes] = value.astype(jnp.bfloat16)

            products(d, j, keep)
            flow = target_flow(d, j, p - d)
            flow.start()
            sends.append(flow)

        def own_part(s, lanes, value):
            total[s, :, lanes] = value

        products(0, j, own_part)
    for j, (first, width) in enumerate(spans):
        for d in range(1, p):
            target_flow(d, j, d).wait_recv()
        lanes = slice(first, first + width)

        def add(s, carry):
            value = total[s, :, lanes]
            for d in range(1, p):
                value = value + incoming[d - 1, s, :, lanes].astype(jnp.float32)
            target_ref[s, :, lanes] = value.astype(jnp.bfloat16)
            return carry

        lax.fori_loop(0, PHYS, add, 0)
    for flow in sends:
        flow.wait_send()


def front(left, prev_left, current, right, prev_site, prev_right, coupling):
    n, segments = lax.axis_size("bond"), lax.axis_size("seg")
    q = minor_size(n)
    p = n // q
    own, bond = left.shape[1], left.shape[2]
    wide, tall = q * own, p * own
    rows = min(LEFT_ROWS, own)
    edges = len(edge_spans(bond))
    side = MPOB * PHYS * ROWS
    low, full = jnp.bfloat16, jnp.float32
    whole = pl.BlockSpec(memory_space=pltpu.VMEM)
    there = pl.BlockSpec(memory_space=pl.ANY)

    def pairs(*shape):
        return [pltpu.SemaphoreType.DMA(shape)] * 2

    return pl.pallas_call(
        functools.partial(front_kernel, segments, n),
        out_shape=jax.ShapeDtypeStruct((PHYS, own, bond), low),
        in_specs=[there] * 4 + [whole] * 3,
        out_specs=whole,
        scratch_shapes=[
            pltpu.VMEM((p, MPOB, own, bond), low),
            pltpu.VMEM((PHYS, bond, wide), low),
            pltpu.VMEM((MPOB, wide, bond), low),
            pltpu.VMEM((bond, bond), low),
            pltpu.VMEM((max(q - 1, 1), PHYS, tall, own), low),
            pltpu.VMEM((q, PHYS, tall, own), low),
            pltpu.VMEM((PHYS, MPOB * rows, wide), full),
            pltpu.VMEM((PHYS, tall, MPOB * wide), low),
            pltpu.VMEM((max(p - 1, 1), PHYS, own, bond), low),
            pltpu.VMEM((max(p - 1, 1), PHYS, own, bond), low),
            pltpu.VMEM((PHYS, own, bond), full),
            pltpu.VMEM((side, side), low),
        ]
        + pairs(p, own // rows)
        + pairs(1)
        + pairs(p, 2)
        + pairs(q, 2)
        + pairs(p, q, 2)
        + pairs(q, edges)
        + pairs(q)
        + pairs(p, edges)
        + [pltpu.SemaphoreType.DMA((2,))],
        compiler_params=pltpu.CompilerParams(
            collective_id=1, has_side_effects=True, vmem_limit_bytes=49 * 2**20
        ),
        name="front",
    )(left, prev_left, current, right, prev_site, prev_right, coupling)


def shards(left_env, prev_left, cur_site, prev_site, hamiltonian, right_env, prev_right):
    own_rows, bond_width = left_env.shape[1], left_env.shape[3]
    target = front(
        jnp.transpose(left_env[0], (1, 0, 2)),
        prev_left[0],
        jnp.transpose(cur_site[0], (1, 0, 2)),
        jnp.transpose(right_env[0], (1, 0, 2)),
        jnp.transpose(prev_site[0], (1, 0, 2)),
        prev_right[0],
        jnp.transpose(hamiltonian[0], (0, 2, 3, 1)).reshape(MPOB * PHYS * PHYS, MPOB),
    ).reshape(PHYS * own_rows, bond_width)
    site, center = back(target)
    site = jnp.transpose(site.reshape(PHYS, own_rows, bond_width), (1, 0, 2))
    return (site[None], center[None])


def solution(mesh):
    return jax.shard_map(
        shards,
        mesh=mesh,
        in_specs=(
            P("seg", "bond", None, None),
            P("seg", None, None),
            P("seg", "bond", None, None),
            P("seg", None, None, "bond"),
            P("seg", None, None, None, None),
            P("seg", "bond", None, None),
            P("seg", None, None),
        ),
        out_specs=(P("seg", "bond", None, None), P("seg", "bond", None)),
        check_vma=False,
    )
```
